32 devices in a mesh: tile: 16 (over z, y, x), mode: 2 (over core).
Axes of the slice: x: 2, y: 2, z: 4, core: 2. Of those that a mesh axis runs over, the one named last changes fastest.
Arguments:
- object_tiles: float32 [2, 2048, 2048], P(None, 'tile'), may hold values from -6 to 6
- probe_modes: float32 [4, 2, 256, 256], P('mode'), may hold values from -5 to 5
- amplitudes: float32 [16, 256, 256], P('tile'), may hold values from 0.25 to 4
- scan_offsets: int32 [8192, 2], replicated, may hold values from 0 to 1792, as said below
- slot_scan: int32 [16], P('tile'), may hold values from 0 to 8191, as said below
- slot_count: int32 [16], P('tile'), may hold values from 0 to 1, as said below
Outputs:
- updated_object: float32 [2, 2048, 2048], P(None, 'tile')
- object_gradient: float32 [2, 2048, 2048], P(None, 'tile')
The draws below stay inside these ranges and needn't reach their ends.
Inputs may be any that keep to these rules, and one draw needn't show every extreme that they name: `scan_offsets`: every patch of 256 x 256 pixels at an offset lies inside the object. `slot_scan`: on every index d of tile but the last, the row offset of each slot's scan position lies in [d * 128, (d + 1) * 128). The positions of one device's slots are distinct. `slot_count`: the live slots of a device are its first ones. The last index of tile holds none, every other holds at least one; some index holds 1.
All inputs are finite; a program needn't handle non-finite values.
Results may differ from the reference program's by a relative error of at most 0.0001.
Values sent between devices are 32-bit elements; how exact they have to be, the bound alone decides.
No kernel may reach another device: no remote copies, remote signals or barrier semaphores. Data moves between devices by JAX's collectives and lax.ppermute only.
A program may use at most 64 MiB of HBM per device.

```python
import math
import jax
import jax.numpy as jnp
from jax import lax

FRAME = 256
MODES = 4
SLOTS = 1
OBJ_COLS = 2048
SCAN_COLS = 256
ROWS_DEV = 128
OBJ_ROWS = 2048
TOTAL_SLOTS = 16


def draw_scan_offsets(key, part):
    base = jax.random.fold_in(key, 11)
    key_row, key_col = jax.random.split(base)
    raster = 2 * (OBJ_ROWS // ROWS_DEV)
    halfway = ROWS_DEV // 2
    step_col = (OBJ_COLS - FRAME) // SCAN_COLS
    row_jitter = jax.random.randint(key_row, (raster, SCAN_COLS), 1, halfway)
    col_jitter = jax.random.randint(key_col, (raster, SCAN_COLS), 0, step_col + 1)
    col_jitter = col_jitter.at[:, 0].set(0)
    row_offset = jnp.minimum(jnp.arange(raster, dtype=jnp.int32)[:, None] * halfway + row_jitter, OBJ_ROWS - FRAME)
    column_index = jnp.arange(SCAN_COLS, dtype=jnp.int32)[None, :]
    col_offset = column_index * step_col + col_jitter
    col_offset = jnp.where(column_index == SCAN_COLS - 1, OBJ_COLS - FRAME, col_offset)
    col_offset = jnp.broadcast_to(col_offset, (raster, SCAN_COLS))
    return jnp.stack([row_offset.reshape(-1), col_offset.reshape(-1)], axis=1).astype(jnp.int32)


def draw_slot_scan(key, part):
    devices = OBJ_ROWS // ROWS_DEV
    device_keys = jax.random.split(jax.random.fold_in(key, 13), devices)

    def choose(device_key):
        return jax.random.permutation(device_key, 2 * SCAN_COLS)[:SLOTS]
    chosen = jax.vmap(choose)(device_keys).astype(jnp.int32)
    leading = chosen[0]
    has_zero = jnp.any(leading == 0)
    leading = jnp.where(has_zero, leading, leading.at[0].set(0))
    chosen = chosen.at[0].set(leading)
    topmost = 2 * SCAN_COLS - 1 - jnp.arange(SLOTS, dtype=jnp.int32)
    chosen = chosen.at[devices - 1].set(topmost)
    first = 2 * SCAN_COLS * jnp.arange(devices, dtype=jnp.int32)[:, None]
    return (first + chosen).reshape(-1).astype(jnp.int32)


def draw_slot_count(key, part):
    devices = OBJ_ROWS // ROWS_DEV
    key_first, key_second, key_busy = jax.random.split(jax.random.fold_in(key, 17), 3)
    first = jax.random.randint(key_first, (devices,), 0, SLOTS + 1)
    second = jax.random.randint(key_second, (devices,), 0, SLOTS + 1)
    counts = jnp.maximum(first * second // SLOTS, 1)
    busiest = jax.random.randint(key_busy, (), 0, devices - 1)
    index = jnp.arange(devices, dtype=jnp.int32)
    counts = jnp.where(index == busiest, SLOTS, counts)
    counts = jnp.where(index == devices - 1, 0, counts)
    return counts.astype(jnp.int32)


def steps_of(own_key, dims, pieces, smallest, high):
    loudness, own = 1.0, jax.random.fold_in(own_key, 6)
    for dim, blocks in pieces:
        steps = jnp.exp(jax.random.uniform(jax.random.fold_in(own, dim), (blocks,), jnp.float32, smallest / len(pieces), high / len(pieces)))
        loudness = loudness * jnp.repeat(steps, dims[dim] // blocks).reshape([-1 if axis == dim else 1 for axis in range(len(dims))])
    return loudness


def gaussian(stream_key, shape, deviation, most, pieces=(), kind=jnp.bfloat16):
    level = steps_of(stream_key, shape, pieces, -0.22, 0.18) if pieces else 1.0
    drawn = jax.random.normal(stream_key, shape, jnp.float32) * deviation * level
    return jnp.minimum(jnp.maximum(drawn, -most), most).astype(kind)


def setup_inputs(seed: int = 0) -> dict:
    streams_of = jax.random.split(jax.random.key(seed), 7)
    return {
        "object_tiles": gaussian(streams_of[0], (2, OBJ_ROWS, OBJ_COLS), 0.7, 6.0, ((1, 16),), jnp.float32),
        "probe_modes": gaussian(streams_of[1], (MODES, 2, FRAME, FRAME), 0.35, 5.0, ((0, 2),), jnp.float32),
        "amplitudes": jnp.clip(jnp.exp(math.log(4.0) - 2.7725887 * jax.random.uniform(streams_of[2], (TOTAL_SLOTS, FRAME, FRAME), jnp.float32) ** steps_of(streams_of[2], (TOTAL_SLOTS, FRAME, FRAME), ((0, 16),), -0.2, 0.2)), 0.25, 4.0),
        "scan_offsets": draw_scan_offsets(jax.random.fold_in(streams_of[6], 71), 0),
        "slot_scan": draw_slot_scan(jax.random.fold_in(streams_of[6], 71), 0),
        "slot_count": draw_slot_count(jax.random.fold_in(streams_of[6], 71), 0),
    }


FLOOR = 0.25
ALPHA = 0.5

def reference(object_tiles, probe_modes, amplitudes, scan_offsets, slot_scan, slot_count):
    frame = probe_modes.shape[2]
    capacity = slot_scan.shape[0] // slot_count.shape[0]
    probe_re = probe_modes[:, 0]
    probe_im = probe_modes[:, 1]
    illumination = lax.optimization_barrier(jnp.sum(probe_re * probe_re + probe_im * probe_im, axis=0))
    probe_wave = probe_re + 1j * probe_im

    def add_slot(index, totals):
        owner = index // capacity
        active = (index % capacity < slot_count[owner]).astype(object_tiles.dtype)
        scanned = slot_scan[index]
        row_at = scan_offsets[scanned, 0].astype(jnp.int32)
        col_at = scan_offsets[scanned, 1].astype(jnp.int32)
        anchor = jnp.zeros((), jnp.int32)
        patch = lax.dynamic_slice(object_tiles, (anchor, row_at, col_at), (2, frame, frame))
        wave = probe_wave * (patch[0] + 1j * patch[1])[None]
        far = jnp.fft.fft2(wave, norm='ortho')
        intensity = lax.optimization_barrier(jnp.sum(far.real * far.real + far.imag * far.imag, axis=0))
        factor = amplitudes[index] / jnp.sqrt(jnp.maximum(intensity, FLOOR))
        back = jnp.fft.ifft2(far * factor[None], norm='ortho')
        change = lax.optimization_barrier(jnp.sum(jnp.conj(probe_wave) * (back - wave), axis=0))
        piece = jnp.stack([change.real, change.imag, illumination]) * active
        current = lax.dynamic_slice(totals, (anchor, row_at, col_at), (3, frame, frame))
        return lax.dynamic_update_slice(totals, current + piece, (anchor, row_at, col_at))
    start = jnp.zeros((3,) + object_tiles.shape[1:], object_tiles.dtype)
    totals = lax.fori_loop(0, slot_scan.shape[0], add_slot, start)
    gradient = totals[:2]
    updated = object_tiles + gradient / (totals[2] + ALPHA)
    return (updated, gradient)
```

```python
import math

import jax
import jax.numpy as jnp
import numpy as np
from jax import lax
from jax.experimental import pallas as pl
from jax.experimental.pallas import tpu as pltpu
from jax.sharding import PartitionSpec as P

FLOOR = 0.25
ALPHA = 0.5
LANES = 128
AXES = ("tile", "mode")
VMEM = pltpu.VMEM
SMEM = pltpu.SMEM


def split(value):
    high = value.astype(jnp.bfloat16)
    low = (value - high.astype(jnp.float32)).astype(jnp.bfloat16)
    return high, low


def matrices(frame):
    half = frame // 2
    pixel = np.arange(half)[:, None]
    wave = np.arange(half)[None, :]
    blocks = []
    for parity in (0, 1):
        phase = 2.0 * math.pi * (pixel * (2 * wave + parity) % frame) / frame
        cos, sin = np.cos(phase) / math.sqrt(frame), np.sin(phase) / math.sqrt(frame)
        forward = np.block([[cos, -sin], [sin, cos]])
        for table in (forward, forward.T):
            high = table.astype(jnp.bfloat16)
            blocks.append(high)
            blocks.append((table - high.astype(np.float64)).astype(jnp.bfloat16))
    return np.stack(blocks)


def lookup(table_ref, scan):
    base = pl.multiple_of((scan // LANES) * LANES, LANES)
    chunk = table_ref[:, pl.ds(base, LANES)].astype(jnp.float32)
    lane = lax.broadcasted_iota(jnp.int32, chunk.shape, 1)
    picked = jnp.where(lane == scan - base, chunk, 0.0)
    row = jnp.sum(picked[0:1]).astype(jnp.int32)
    col = jnp.sum(picked[1:2]).astype(jnp.int32)
    return row, col


def strip_window(object_ref, col):
    blocks = object_ref.shape[2] // LANES
    block, shift = col // LANES, col % LANES
    first = object_ref[:, :, pl.ds(pl.multiple_of(block * LANES, LANES), LANES)]
    second = object_ref[:, :, pl.ds(pl.multiple_of((block + 1) * LANES, LANES), LANES)]
    last = jnp.minimum(block + 2, blocks - 1)
    third = object_ref[:, :, pl.ds(pl.multiple_of(last * LANES, LANES), LANES)]
    lane = lax.broadcasted_iota(jnp.int32, first.shape, 2)
    return jnp.where(lane < shift, third, first), second


def select_kernel(scan_ref, table_ref, object_ref, out_ref):
    _, col = lookup(table_ref, scan_ref[0])
    low, high = strip_window(object_ref, col)
    out_ref[:, :, :LANES] = low
    out_ref[:, :, LANES:] = high


def rolled(value, row, col):
    return pltpu.roll(pltpu.roll(value, col, 1), row, 0)


def prepare_kernel(
    own_scan_ref, received_ref, swapped_ref, table_ref, object_ref, own_probe_ref, other_probe_ref,
    amplitude_ref, probe_ref, factor_ref, window_ref, light_ref, nearer_ref, farther_ref, place_ref, rows_ref,
):
    modes = own_probe_ref.shape[0]
    height = object_ref.shape[1]
    frame = own_probe_ref.shape[2]
    tile = lax.axis_index("tile")
    core = lax.axis_index("mode")
    row, col = lookup(table_ref, own_scan_ref[0])
    row = row - tile * height
    shift = col % LANES
    total = jnp.zeros((frame, frame), jnp.float32)
    for index in range(2 * modes):
        source = own_probe_ref if index < modes else other_probe_ref
        for part in range(2):
            value = source[index % modes, part]
            total = total + value * value
            probe_ref[index, part] = rolled(value, row, shift)
    light_ref[...] = rolled(total, row, shift)
    low, high = strip_window(object_ref, col)
    window_ref[:, :, :LANES] = low
    window_ref[:, :, LANES:] = high
    nearer_scan = jnp.where(core == 0, received_ref[0], swapped_ref[0])
    farther_scan = jnp.where(core == 0, swapped_ref[0], received_ref[0])
    row1, col1 = lookup(table_ref, nearer_scan)
    row2, col2 = lookup(table_ref, farther_scan)
    row1 = row1 - (tile - 1) * height
    row2 = row2 - (tile - 2) * height
    row1 = jnp.where(tile < 1, 0, row1)
    row2 = jnp.where(tile < 2, 0, row2)
    nearer_ref[...] = rolled(total, row1, col1 % LANES)[height:]
    farther_ref[...] = rolled(total, row2, col2 % LANES)[:height]
    place_ref[0] = row
    place_ref[1] = col
    place_ref[2] = row1
    place_ref[3] = col1
    place_ref[4] = row2
    place_ref[5] = col2
    place_ref[6] = 0
    place_ref[7] = 0
    source = lax.broadcasted_iota(jnp.int32, (frame, frame), 0)
    target = lax.broadcasted_iota(jnp.int32, (frame, frame), 1)
    half = frame // 2
    order = jnp.where(target < half, 2 * target, 2 * target - frame + 1)
    pick = jnp.where(source == order, 1.0, 0.0).astype(jnp.bfloat16)
    value = amplitude_ref[0]
    high = value.astype(jnp.bfloat16)
    rest = value - high.astype(jnp.float32)
    middle = rest.astype(jnp.bfloat16)
    low = (rest - middle.astype(jnp.float32)).astype(jnp.bfloat16)
    columns = jnp.dot(high, pick, preferred_element_type=jnp.float32)
    columns = columns + jnp.dot(middle, pick, preferred_element_type=jnp.float32)
    columns = columns + jnp.dot(low, pick, preferred_element_type=jnp.float32)
    for index in range(frame // LANES):
        at = slice(index * LANES, (index + 1) * LANES)
        rows_ref[index] = columns[:, at]
        factor_ref[:half, at] = rows_ref[index, pl.ds(0, half, stride=2), :]
        factor_ref[half:, at] = rows_ref[index, pl.ds(1, half, stride=2), :]


def right(value, high, low):
    first, second = split(value)
    return jnp.dot(
        jnp.concatenate([first, second, first], axis=1),
        jnp.concatenate([high, high, low], axis=0),
        preferred_element_type=jnp.float32,
    )


def left(high, low, value):
    first, second = split(value)
    return jnp.dot(
        jnp.concatenate([high, high, low], axis=1),
        jnp.concatenate([first, second, first], axis=0),
        preferred_element_type=jnp.float32,
    )


def wave_kernel(
    count_ref, place_ref, window_ref, received_ref, swapped_ref, probe_ref, amplitude_ref, light_ref,
    matrix_ref, send_ref, keep_ref, patch_ref, far_ref,
):
    modes, _, frame, _ = probe_ref.shape
    height = window_ref.shape[1]
    half = frame // 2
    core = lax.axis_index("mode")
    row = place_ref[0]
    level = lax.broadcasted_iota(jnp.int32, (height, frame), 0)
    for part in range(2):
        got, given = received_ref[part], swapped_ref[part]
        nearer = jnp.where(core == 0, got, given)
        farther = jnp.where(core == 0, given, got)
        patch_ref[part, :height] = jnp.where(level < row, farther, window_ref[part])
        patch_ref[part, height:] = nearer
    intensity = jnp.zeros((frame, frame), jnp.float32)
    for mode in range(modes):
        probe_re, probe_im = probe_ref[mode, 0], probe_ref[mode, 1]
        patch_re, patch_im = patch_ref[0], patch_ref[1]
        wave_re = probe_re * patch_re - probe_im * patch_im
        wave_im = probe_re * patch_im + probe_im * patch_re
        added = jnp.concatenate([wave_re[:, :half] + wave_re[:, half:], wave_im[:, :half] + wave_im[:, half:]], axis=1)
        taken = jnp.concatenate([wave_re[:, :half] - wave_re[:, half:], wave_im[:, :half] - wave_im[:, half:]], axis=1)
        even = right(added, matrix_ref[0], matrix_ref[1])
        odd = right(taken, matrix_ref[4], matrix_ref[5])
        mid_re = jnp.concatenate([even[:, :half], odd[:, :half]], axis=1)
        mid_im = jnp.concatenate([even[:, half:], odd[:, half:]], axis=1)
        added = jnp.concatenate([mid_re[:half] + mid_re[half:], mid_im[:half] + mid_im[half:]], axis=0)
        taken = jnp.concatenate([mid_re[:half] - mid_re[half:], mid_im[:half] - mid_im[half:]], axis=0)
        even = left(matrix_ref[2], matrix_ref[3], added)
        odd = left(matrix_ref[6], matrix_ref[7], taken)
        far_ref[mode, 0] = even
        far_ref[mode, 1] = odd
        squares = jnp.concatenate(
            [even[:half] * even[:half] + even[half:] * even[half:], odd[:half] * odd[:half] + odd[half:] * odd[half:]],
            axis=0,
        )
        intensity = intensity + squares
    factor = amplitude_ref[...] * lax.rsqrt(jnp.maximum(intensity, FLOOR))
    grad_re = jnp.zeros((frame, frame), jnp.float32)
    grad_im = jnp.zeros((frame, frame), jnp.float32)
    even_factor = jnp.concatenate([factor[:half], factor[:half]], axis=0)
    odd_factor = jnp.concatenate([factor[half:], factor[half:]], axis=0)
    for mode in range(modes):
        even = left(matrix_ref[0], matrix_ref[1], far_ref[mode, 0] * even_factor)
        odd = left(matrix_ref[4], matrix_ref[5], far_ref[mode, 1] * odd_factor)
        top, bottom = even + odd, even - odd
        mid_re = jnp.concatenate([top[:half], bottom[:half]], axis=0)
        mid_im = jnp.concatenate([top[half:], bottom[half:]], axis=0)
        even = right(jnp.concatenate([mid_re[:, :half], mid_im[:, :half]], axis=1), matrix_ref[2], matrix_ref[3])
        odd = right(jnp.concatenate([mid_re[:, half:], mid_im[:, half:]], axis=1), matrix_ref[6], matrix_ref[7])
        fore, aft = even + odd, even - odd
        back_re = jnp.concatenate([fore[:, :half], aft[:, :half]], axis=1)
        back_im = jnp.concatenate([fore[:, half:], aft[:, half:]], axis=1)
        probe_re, probe_im = probe_ref[mode, 0], probe_ref[mode, 1]
        grad_re = grad_re + (probe_re * back_re + probe_im * back_im)
        grad_im = grad_im + (probe_re * back_im - probe_im * back_re)
    live = (count_ref[0] > 0).astype(jnp.float32)
    grad_re = (grad_re - light_ref[...] * patch_ref[0]) * live
    grad_im = (grad_im - light_ref[...] * patch_ref[1]) * live
    send_ref[:height] = jnp.where(core == 0, grad_re[height:], grad_re[:height])
    send_ref[height : 2 * height] = jnp.where(core == 0, grad_im[height:], grad_im[:height])
    send_ref[2 * height :] = jnp.full((8, frame), live, jnp.float32)
    keep_ref[0] = grad_re[:height]
    keep_ref[1] = grad_im[:height]


def covers(col, block, low, high, lane):
    start, shift = col // LANES, col % LANES
    distance = block - start
    value = jnp.where(distance == 1, high, low)
    first = jnp.where(distance == 0, shift, jnp.where(distance == 1, 0, LANES))
    last = jnp.where(distance == 2, shift, 0)
    keep = (lane >= first) | (lane < last)
    return jnp.where(keep, value, 0.0)


def base_kernel(
    count_ref, place_ref, object_ref, keep_ref, light_ref, updated_ref, gradient_ref, total_ref, weight_ref,
    new_ref, sems,
):
    height, breadth = object_ref.shape[1:]
    row, col = place_ref[0], place_ref[1]
    live = (count_ref[0] > 0).astype(jnp.float32)
    total_ref[...] = jnp.zeros_like(total_ref)
    weight_ref[...] = jnp.zeros_like(weight_ref)
    new_ref[...] = object_ref[...]
    lane = lax.broadcasted_iota(jnp.int32, (height, LANES), 1)
    level = lax.broadcasted_iota(jnp.int32, (height, LANES), 0)
    kept = level >= row
    for offset in range(3):
        block = jnp.minimum(col // LANES + offset, breadth // LANES - 1)
        at = pl.ds(pl.multiple_of(block * LANES, LANES), LANES)
        light = covers(col, block, light_ref[:height, :LANES], light_ref[:height, LANES:], lane)
        weight = jnp.where(kept, light * live, 0.0)
        weight_ref[:, at] = weight
        for part in range(2):
            change = covers(col, block, keep_ref[part, :, :LANES], keep_ref[part, :, LANES:], lane)
            change = jnp.where(kept, change, 0.0)
            total_ref[part, :, at] = change
            new_ref[part, :, at] = object_ref[part, :, at] + change / (weight + ALPHA)
    first = pltpu.make_async_copy(total_ref, gradient_ref, sems.at[0])
    second = pltpu.make_async_copy(new_ref, updated_ref, sems.at[1])
    first.start()
    second.start()
    first.wait()
    second.wait()


def final_kernel(
    place_ref, object_ref, total_ref, weight_ref, nearer_ref, farther_ref, received_ref, swapped_ref,
    old_updated_ref, old_gradient_ref, updated_ref, gradient_ref, new_ref, sum_ref, sems,
):
    del old_updated_ref, old_gradient_ref
    height, breadth = object_ref.shape[1:]
    blocks = breadth // LANES
    core = lax.axis_index("mode")
    col1, row2, col2 = place_ref[3], place_ref[4], place_ref[5]
    lane = lax.broadcasted_iota(jnp.int32, (height, LANES), 1)
    level = lax.broadcasted_iota(jnp.int32, (height, LANES), 0)
    start1, start2 = col1 // LANES, col2 // LANES
    copies = []
    for slot in range(6):
        start, offset = (start1, slot) if slot < 3 else (start2, slot - 3)
        block = jnp.minimum(start + offset, blocks - 1)
        fresh = start + offset < blocks
        if slot >= 3:
            fresh = fresh & ((block < start1) | (block > start1 + 2))
        at = pl.ds(pl.multiple_of(block * LANES, LANES), LANES)

        def halves(ref, base):
            return ref[base : base + height, :LANES], ref[base : base + height, LANES:]

        def pick(base):
            got, given = halves(received_ref, base), halves(swapped_ref, base)
            near = tuple(jnp.where(core == 0, a, b) for a, b in zip(got, given))
            far = tuple(jnp.where(core == 0, b, a) for a, b in zip(got, given))
            return near, far

        got, given = received_ref[2 * height : 2 * height + 1, :1], swapped_ref[2 * height : 2 * height + 1, :1]
        near_live = jnp.where(core == 0, got, given)
        far_live = jnp.where(core == 0, given, got)
        light = covers(col1, block, *halves(nearer_ref, 0), lane) * near_live
        light = light + jnp.where(level < row2, covers(col2, block, *halves(farther_ref, 0), lane), 0.0) * far_live
        scale = 1.0 / (weight_ref[:, at] + light + ALPHA)
        for part in range(2):
            near, far = pick(part * height)
            change = total_ref[part, :, at] + covers(col1, block, *near, lane)
            change = change + jnp.where(level < row2, covers(col2, block, *far, lane), 0.0)
            sum_ref[slot, part] = change
            new_ref[slot, part] = object_ref[part, :, at] + change * scale
        one = pltpu.make_async_copy(sum_ref.at[slot], gradient_ref.at[:, :, at], sems.at[2 * slot])
        two = pltpu.make_async_copy(new_ref.at[slot], updated_ref.at[:, :, at], sems.at[2 * slot + 1])
        copies.append((fresh, one, two))

        @pl.when(fresh)
        def _(one=one, two=two):
            one.start()
            two.start()

    for fresh, one, two in copies:

        @pl.when(fresh)
        def _(one=one, two=two):
            one.wait()
            two.wait()


def call(kernel, out_shape, in_specs, out_specs, scratch=(), cost=1, aliases=None):
    return pl.pallas_call(
        kernel,
        out_shape=out_shape,
        in_specs=in_specs,
        out_specs=out_specs,
        scratch_shapes=list(scratch),
        input_output_aliases=aliases or {},
        cost_estimate=pl.CostEstimate(flops=cost * 1000000, bytes_accessed=cost * 1000000, transcendentals=0),
        name=kernel.__name__,
    )


def space(where):
    return pl.BlockSpec(memory_space=where)


def shape(*dims, dtype=jnp.float32):
    return jax.ShapeDtypeStruct(dims, dtype)


def solution(mesh):
    tiles, cores = mesh.shape["tile"], mesh.shape["mode"]
    up = [(2 * t, 2 * (t + 1)) for t in range(tiles - 1)] + [(2 * t + 1, 2 * (t + 2) + 1) for t in range(tiles - 2)]
    down = [(target, source) for source, target in up]
    swap = [(2 * t + core, 2 * t + 1 - core) for t in range(tiles) for core in range(2)]
    assert cores == 2

    def move(value, pairs):
        return lax.ppermute(value, AXES, pairs)

    def shards(object_tiles, probe_modes, amplitudes, scan_offsets, slot_scan, slot_count):
        height, breadth = object_tiles.shape[1:]
        modes, _, frame, _ = probe_modes.shape
        assert slot_scan.shape[0] == 1 and frame == 2 * height and height == LANES
        table = scan_offsets.T
        matrix = jnp.asarray(matrices(frame))
        received_scan = move(slot_scan, up)
        other_probe = move(probe_modes, swap)
        window = call(
            select_kernel, shape(2, height, frame), [space(SMEM), space(VMEM), space(VMEM)], space(VMEM)
        )(received_scan, table, object_tiles)
        received = move(window, down)
        swapped_scan = move(received_scan, swap)
        probe, amplitude, own_window, light, nearer, farther, place = call(
            prepare_kernel,
            (
                shape(2 * modes, 2, frame, frame),
                shape(frame, frame),
                shape(2, height, frame),
                shape(frame, frame),
                shape(height, frame),
                shape(height, frame),
                shape(8, dtype=jnp.int32),
            ),
            [space(SMEM)] * 3 + [space(VMEM)] * 5,
            [space(VMEM)] * 6 + [space(SMEM)],
            [pltpu.VMEM((frame // LANES, frame, LANES), jnp.float32)],
            cost=5,
        )(slot_scan, received_scan, swapped_scan, table, object_tiles, probe_modes, other_probe, amplitudes)
        swapped = move(received, swap)
        send, keep = call(
            wave_kernel,
            (shape(2 * height + 8, frame), shape(2, height, frame)),
            [space(SMEM)] * 2 + [space(VMEM)] * 7,
            [space(VMEM)] * 2,
            [
                pltpu.VMEM((2, frame, frame), jnp.float32),
                pltpu.VMEM((2 * modes, 2, frame, frame), jnp.float32),
            ],
            cost=5,
        )(slot_count, place, own_window, received, swapped, probe, amplitude, light, matrix)
        received_change = move(send, up)
        updated, gradient, total, weight = call(
            base_kernel,
            (
                shape(2, height, breadth),
                shape(2, height, breadth),
                shape(2, height, breadth),
                shape(height, breadth),
            ),
            [space(SMEM)] * 2 + [space(VMEM)] * 3,
            [space(pl.ANY)] * 2 + [space(VMEM)] * 2,
            [pltpu.VMEM((2, height, breadth), jnp.float32), pltpu.SemaphoreType.DMA((2,))],
            cost=5,
        )(slot_count, place, object_tiles, keep, light)
        swapped_change = move(received_change, swap)
        updated, gradient = call(
            final_kernel,
            (shape(2, height, breadth), shape(2, height, breadth)),
            [space(SMEM)] + [space(VMEM)] * 7 + [space(pl.ANY)] * 2,
            [space(pl.ANY)] * 2,
            [
                pltpu.VMEM((6, 2, height, LANES), jnp.float32),
                pltpu.VMEM((6, 2, height, LANES), jnp.float32),
                pltpu.SemaphoreType.DMA((12,)),
            ],
            aliases={8: 0, 9: 1},
        )(place, object_tiles, total, weight, nearer, farther, received_change, swapped_change, updated, gradient)
        return (updated, gradient)

    return jax.shard_map(
        shards,
        mesh=mesh,
        in_specs=(
            P(None, "tile", None),
            P("mode", None, None, None),
            P("tile", None, None),
            P(),
            P("tile"),
            P("tile"),
        ),
        out_specs=(P(None, "tile", None), P(None, "tile", None)),
        check_vma=False,
    )
```

```python
import math

import jax
import jax.numpy as jnp
import numpy as np
from jax import lax
from jax.experimental import pallas as pl
from jax.experimental.pallas import tpu as pltpu
from jax.sharding import PartitionSpec as P


FLOOR = 0.25
ALPHA = 0.5
LANES = 128
AXES = ("tile", "mode")
VMEM = pltpu.VMEM
SMEM = pltpu.SMEM


def split(value):
    high = value.astype(jnp.bfloat16)
    low = (value - high.astype(jnp.float32)).astype(jnp.bfloat16)
    return high, low


def matrices(frame):
    half = frame // 2
    pixel = np.arange(half)[:, None]
    wave = np.arange(half)[None, :]
    blocks = []
    for parity in (0, 1):
        phase = 2.0 * math.pi * (pixel * (2 * wave + parity) % frame) / frame
        cos, sin = np.cos(phase) / math.sqrt(frame), np.sin(phase) / math.sqrt(frame)
        forward = np.block([[cos, -sin], [sin, cos]])
        for table in (forward, forward.T):
            high = table.astype(jnp.bfloat16)
            blocks.append(high)
            blocks.append((table - high.astype(np.float64)).astype(jnp.bfloat16))
    return np.stack(blocks)


def lookup(table_ref, scan):
    base = pl.multiple_of((scan // LANES) * LANES, LANES)
    chunk = table_ref[:, pl.ds(base, LANES)].astype(jnp.float32)
    lane = lax.broadcasted_iota(jnp.int32, chunk.shape, 1)
    picked = jnp.where(lane == scan - base, chunk, 0.0)
    row = jnp.sum(picked[0:1]).astype(jnp.int32)
    col = jnp.sum(picked[1:2]).astype(jnp.int32)
    return row, col


def strip_window(object_ref, col):
    blocks = object_ref.shape[2] // LANES
    block, shift = col // LANES, col % LANES
    first = object_ref[:, :, pl.ds(pl.multiple_of(block * LANES, LANES), LANES)]
    second = object_ref[:, :, pl.ds(pl.multiple_of((block + 1) * LANES, LANES), LANES)]
    last = jnp.minimum(block + 2, blocks - 1)
    third = object_ref[:, :, pl.ds(pl.multiple_of(last * LANES, LANES), LANES)]
    lane = lax.broadcasted_iota(jnp.int32, first.shape, 2)
    return jnp.where(lane < shift, third, first), second


def stage_kernel(object_ref, table_ref, staged_ref, held_ref, sems):
    first = pltpu.make_async_copy(object_ref, staged_ref, sems.at[0])
    second = pltpu.make_async_copy(table_ref, held_ref, sems.at[1])
    first.start()
    second.start()
    first.wait()
    second.wait()


def select_kernel(scan_ref, table_ref, object_ref, out_ref):
    _, col = lookup(table_ref, scan_ref[0])
    low, high = strip_window(object_ref, col)
    out_ref[:, :, :LANES] = low
    out_ref[:, :, LANES:] = high


def rolled(value, row, col):
    return pltpu.roll(pltpu.roll(value, col, 1), row, 0)


def prepare_kernel(
    scan_ref, count_ref, table_ref, object_ref, own_probe_ref, other_probe_ref, amplitude_ref,
    probe_ref, factor_ref, window_ref, light_ref, total_ref, place_ref, rows_ref,
):
    modes = own_probe_ref.shape[0]
    height = object_ref.shape[1]
    frame = own_probe_ref.shape[2]
    row, col = lookup(table_ref, scan_ref[0])
    row = row - lax.axis_index("tile") * height
    shift = col % LANES
    total = jnp.zeros((frame, frame), jnp.float32)
    for index in range(2 * modes):
        source = own_probe_ref if index < modes else other_probe_ref
        for part in range(2):
            value = source[index % modes, part]
            total = total + value * value
            probe_ref[index, part] = rolled(value, row, shift)
    total_ref[...] = total
    light_ref[...] = rolled(total, row, shift)
    low, high = strip_window(object_ref, col)
    window_ref[:, :, :LANES] = low
    window_ref[:, :, LANES:] = high
    place_ref[0] = row
    place_ref[1] = col
    place_ref[2] = count_ref[0]
    place_ref[3] = 0
    source = lax.broadcasted_iota(jnp.int32, (frame, frame), 0)
    target = lax.broadcasted_iota(jnp.int32, (frame, frame), 1)
    half = frame // 2
    order = jnp.where(target < half, 2 * target, 2 * target - frame + 1)
    pick = jnp.where(source == order, 1.0, 0.0).astype(jnp.bfloat16)
    value = amplitude_ref[0]
    high = value.astype(jnp.bfloat16)
    rest = value - high.astype(jnp.float32)
    middle = rest.astype(jnp.bfloat16)
    low = (rest - middle.astype(jnp.float32)).astype(jnp.bfloat16)
    columns = jnp.dot(high, pick, preferred_element_type=jnp.float32)
    columns = columns + jnp.dot(middle, pick, preferred_element_type=jnp.float32)
    columns = columns + jnp.dot(low, pick, preferred_element_type=jnp.float32)
    for index in range(frame // LANES):
        at = slice(index * LANES, (index + 1) * LANES)
        rows_ref[index] = columns[:, at]
        factor_ref[:half, at] = rows_ref[index, pl.ds(0, half, stride=2), :]
        factor_ref[half:, at] = rows_ref[index, pl.ds(1, half, stride=2), :]


def right(value, high, low):
    first, second = split(value)
    return jnp.dot(
        jnp.concatenate([first, second, first], axis=1),
        jnp.concatenate([high, high, low], axis=0),
        preferred_element_type=jnp.float32,
    )


def left(high, low, value):
    first, second = split(value)
    return jnp.dot(
        jnp.concatenate([high, high, low], axis=1),
        jnp.concatenate([first, second, first], axis=0),
        preferred_element_type=jnp.float32,
    )


def wave_kernel(
    place_ref, window_ref, received_ref, swapped_ref, probe_ref, amplitude_ref, light_ref,
    matrix_ref, send_ref, keep_ref, patch_ref, far_ref,
):
    modes, _, frame, _ = probe_ref.shape
    height = window_ref.shape[1]
    half = frame // 2
    core = lax.axis_index("mode")
    row = place_ref[0]
    level = lax.broadcasted_iota(jnp.int32, (height, frame), 0)
    for part in range(2):
        got, given = received_ref[part], swapped_ref[part]
        nearer = jnp.where(core == 0, got, given)
        farther = jnp.where(core == 0, given, got)
        patch_ref[part, :height] = jnp.where(level < row, farther, window_ref[part])
        patch_ref[part, height:] = nearer
    intensity = jnp.zeros((frame, frame), jnp.float32)
    for mode in range(modes):
        probe_re, probe_im = probe_ref[mode, 0], probe_ref[mode, 1]
        patch_re, patch_im = patch_ref[0], patch_ref[1]
        wave_re = probe_re * patch_re - probe_im * patch_im
        wave_im = probe_re * patch_im + probe_im * patch_re
        added = jnp.concatenate([wave_re[:, :half] + wave_re[:, half:], wave_im[:, :half] + wave_im[:, half:]], axis=1)
        taken = jnp.concatenate([wave_re[:, :half] - wave_re[:, half:], wave_im[:, :half] - wave_im[:, half:]], axis=1)
        even = right(added, matrix_ref[0], matrix_ref[1])
        odd = right(taken, matrix_ref[4], matrix_ref[5])
        mid_re = jnp.concatenate([even[:, :half], odd[:, :half]], axis=1)
        mid_im = jnp.concatenate([even[:, half:], odd[:, half:]], axis=1)
        added = jnp.concatenate([mid_re[:half] + mid_re[half:], mid_im[:half] + mid_im[half:]], axis=0)
        taken = jnp.concatenate([mid_re[:half] - mid_re[half:], mid_im[:half] - mid_im[half:]], axis=0)
        even = left(matrix_ref[2], matrix_ref[3], added)
        odd = left(matrix_ref[6], matrix_ref[7], taken)
        far_ref[mode, 0] = even
        far_ref[mode, 1] = odd
        squares = jnp.concatenate(
            [even[:half] * even[:half] + even[half:] * even[half:], odd[:half] * odd[:half] + odd[half:] * odd[half:]],
            axis=0,
        )
        intensity = intensity + squares
    factor = amplitude_ref[...] * lax.rsqrt(jnp.maximum(intensity, FLOOR))
    grad_re = jnp.zeros((frame, frame), jnp.float32)
    grad_im = jnp.zeros((frame, frame), jnp.float32)
    even_factor = jnp.concatenate([factor[:half], factor[:half]], axis=0)
    odd_factor = jnp.concatenate([factor[half:], factor[half:]], axis=0)
    for mode in range(modes):
        even = left(matrix_ref[0], matrix_ref[1], far_ref[mode, 0] * even_factor)
        odd = left(matrix_ref[4], matrix_ref[5], far_ref[mode, 1] * odd_factor)
        top, bottom = even + odd, even - odd
        mid_re = jnp.concatenate([top[:half], bottom[:half]], axis=0)
        mid_im = jnp.concatenate([top[half:], bottom[half:]], axis=0)
        even = right(jnp.concatenate([mid_re[:, :half], mid_im[:, :half]], axis=1), matrix_ref[2], matrix_ref[3])
        odd = right(jnp.concatenate([mid_re[:, half:], mid_im[:, half:]], axis=1), matrix_ref[6], matrix_ref[7])
        fore, aft = even + odd, even - odd
        back_re = jnp.concatenate([fore[:, :half], aft[:, :half]], axis=1)
        back_im = jnp.concatenate([fore[:, half:], aft[:, half:]], axis=1)
        probe_re, probe_im = probe_ref[mode, 0], probe_ref[mode, 1]
        grad_re = grad_re + (probe_re * back_re + probe_im * back_im)
        grad_im = grad_im + (probe_re * back_im - probe_im * back_re)
    live = (place_ref[2] > 0).astype(jnp.float32)
    grad_re = (grad_re - light_ref[...] * patch_ref[0]) * live
    grad_im = (grad_im - light_ref[...] * patch_ref[1]) * live
    send_ref[:height] = jnp.where(core == 0, grad_re[height:], grad_re[:height])
    send_ref[height : 2 * height] = jnp.where(core == 0, grad_im[height:], grad_im[:height])
    send_ref[2 * height :] = jnp.full((8, frame), live, jnp.float32)
    keep_ref[0] = grad_re[:height]
    keep_ref[1] = grad_im[:height]


def covers(col, block, low, high, lane):
    start, shift = col // LANES, col % LANES
    distance = block - start
    value = jnp.where(distance == 1, high, low)
    first = jnp.where(distance == 0, shift, jnp.where(distance == 1, 0, LANES))
    last = jnp.where(distance == 2, shift, 0)
    keep = (lane >= first) | (lane < last)
    return jnp.where(keep, value, 0.0)


def base_kernel(
    place_ref, received_ref, swapped_ref, table_ref, object_ref, keep_ref, light_ref, plain_ref,
    updated_ref, gradient_ref, total_ref, weight_ref, nearer_ref, farther_ref, others_ref, new_ref, sems,
):
    height, breadth = object_ref.shape[1:]
    tile = lax.axis_index("tile")
    core = lax.axis_index("mode")
    row, col = place_ref[0], place_ref[1]
    live = (place_ref[2] > 0).astype(jnp.float32)
    total_ref[...] = jnp.zeros_like(total_ref)
    weight_ref[...] = jnp.zeros_like(weight_ref)
    new_ref[...] = object_ref[...]
    lane = lax.broadcasted_iota(jnp.int32, (height, LANES), 1)
    level = lax.broadcasted_iota(jnp.int32, (height, LANES), 0)
    kept = level >= row
    for offset in range(3):
        block = jnp.minimum(col // LANES + offset, breadth // LANES - 1)
        at = pl.ds(pl.multiple_of(block * LANES, LANES), LANES)
        light = covers(col, block, light_ref[:height, :LANES], light_ref[:height, LANES:], lane)
        weight = jnp.where(kept, light * live, 0.0)
        weight_ref[:, at] = weight
        for part in range(2):
            change = covers(col, block, keep_ref[part, :, :LANES], keep_ref[part, :, LANES:], lane)
            change = jnp.where(kept, change, 0.0)
            total_ref[part, :, at] = change
            new_ref[part, :, at] = object_ref[part, :, at] + change / (weight + ALPHA)
    first = pltpu.make_async_copy(total_ref, gradient_ref, sems.at[0])
    second = pltpu.make_async_copy(new_ref, updated_ref, sems.at[1])
    first.start()
    second.start()
    row1, col1 = lookup(table_ref, jnp.where(core == 0, received_ref[0], swapped_ref[0]))
    row2, col2 = lookup(table_ref, jnp.where(core == 0, swapped_ref[0], received_ref[0]))
    row1 = jnp.where(tile < 1, 0, row1 - (tile - 1) * height)
    row2 = jnp.where(tile < 2, 0, row2 - (tile - 2) * height)
    nearer_ref[...] = rolled(plain_ref[...], row1, col1 % LANES)[height:]
    farther_ref[...] = rolled(plain_ref[...], row2, col2 % LANES)[:height]
    others_ref[0] = col1
    others_ref[1] = row2
    others_ref[2] = col2
    others_ref[3] = 0
    first.wait()
    second.wait()


def final_kernel(
    place_ref, object_ref, total_ref, weight_ref, nearer_ref, farther_ref, received_ref, swapped_ref,
    old_updated_ref, old_gradient_ref, updated_ref, gradient_ref, new_ref, sum_ref, sems,
):
    del old_updated_ref, old_gradient_ref
    height, breadth = object_ref.shape[1:]
    blocks = breadth // LANES
    core = lax.axis_index("mode")
    col1, row2, col2 = place_ref[0], place_ref[1], place_ref[2]
    lane = lax.broadcasted_iota(jnp.int32, (height, LANES), 1)
    level = lax.broadcasted_iota(jnp.int32, (height, LANES), 0)
    start1, start2 = col1 // LANES, col2 // LANES
    copies = []
    for slot in range(6):
        start, offset = (start1, slot) if slot < 3 else (start2, slot - 3)
        block = jnp.minimum(start + offset, blocks - 1)
        fresh = start + offset < blocks
        if slot >= 3:
            fresh = fresh & ((block < start1) | (block > start1 + 2))
        at = pl.ds(pl.multiple_of(block * LANES, LANES), LANES)

        def halves(ref, base):
            return ref[base : base + height, :LANES], ref[base : base + height, LANES:]

        def pick(base):
            got, given = halves(received_ref, base), halves(swapped_ref, base)
            near = tuple(jnp.where(core == 0, a, b) for a, b in zip(got, given))
            far = tuple(jnp.where(core == 0, b, a) for a, b in zip(got, given))
            return near, far

        got, given = received_ref[2 * height : 2 * height + 1, :1], swapped_ref[2 * height : 2 * height + 1, :1]
        near_live = jnp.where(core == 0, got, given)
        far_live = jnp.where(core == 0, given, got)
        light = covers(col1, block, *halves(nearer_ref, 0), lane) * near_live
        light = light + jnp.where(level < row2, covers(col2, block, *halves(farther_ref, 0), lane), 0.0) * far_live
        scale = 1.0 / (weight_ref[:, at] + light + ALPHA)
        for part in range(2):
            near, far = pick(part * height)
            change = total_ref[part, :, at] + covers(col1, block, *near, lane)
            change = change + jnp.where(level < row2, covers(col2, block, *far, lane), 0.0)
            sum_ref[slot, part] = change
            new_ref[slot, part] = object_ref[part, :, at] + change * scale
        one = pltpu.make_async_copy(sum_ref.at[slot], gradient_ref.at[:, :, at], sems.at[2 * slot])
        two = pltpu.make_async_copy(new_ref.at[slot], updated_ref.at[:, :, at], sems.at[2 * slot + 1])
        copies.append((fresh, one, two))

        @pl.when(fresh)
        def _(one=one, two=two):
            one.start()
            two.start()

    for fresh, one, two in copies:

        @pl.when(fresh)
        def _(one=one, two=two):
            one.wait()
            two.wait()


def call(kernel, out_shape, in_specs, out_specs, scratch=(), mebibytes=16, aliases=None):
    return pl.pallas_call(
        kernel,
        out_shape=out_shape,
        in_specs=in_specs,
        out_specs=out_specs,
        scratch_shapes=list(scratch),
        input_output_aliases=aliases or {},
        compiler_params=pltpu.CompilerParams(vmem_limit_bytes=mebibytes << 20),
        cost_estimate=pl.CostEstimate(flops=5000000, bytes_accessed=5000000, transcendentals=0),
    )


def space(where):
    return pl.BlockSpec(memory_space=where)


def shape(*dims, dtype=jnp.float32):
    return jax.ShapeDtypeStruct(dims, dtype)


def solution(mesh):
    tiles, cores = mesh.shape["tile"], mesh.shape["mode"]
    up = [(2 * t, 2 * (t + 1)) for t in range(tiles - 1)] + [(2 * t + 1, 2 * (t + 2) + 1) for t in range(tiles - 2)]
    down = [(target, source) for source, target in up]
    swap = [(2 * t + core, 2 * t + 1 - core) for t in range(tiles) for core in range(2)]
    assert cores == 2

    def move(value, pairs):
        return lax.ppermute(value, AXES, pairs)

    def step(object_tiles, probe_modes, amplitudes, scan_offsets, slot_scan, slot_count):
        height, breadth = object_tiles.shape[1:]
        modes, _, frame, _ = probe_modes.shape
        assert slot_scan.shape[0] == 1 and frame == 2 * height and height == LANES
        table = scan_offsets.T
        matrix = jnp.asarray(matrices(frame))
        received_scan = move(slot_scan, up)
        other_probe = move(probe_modes, swap)
        staged, table = call(
            stage_kernel,
            (shape(*object_tiles.shape), shape(*table.shape, dtype=jnp.int32)),
            [space(pl.ANY)] * 2,
            [space(VMEM)] * 2,
            [pltpu.SemaphoreType.DMA((2,))],
            mebibytes=8,
        )(object_tiles, table)
        window = call(
            select_kernel, shape(2, height, frame), [space(SMEM), space(VMEM), space(VMEM)], space(VMEM)
        )(received_scan, table, staged)
        received = move(window, down)
        swapped_scan = move(received_scan, swap)
        probe, amplitude, own_window, light, plain, place = call(
            prepare_kernel,
            (
                shape(2 * modes, 2, frame, frame),
                shape(frame, frame),
                shape(2, height, frame),
                shape(frame, frame),
                shape(frame, frame),
                shape(4, dtype=jnp.int32),
            ),
            [space(SMEM)] * 2 + [space(VMEM)] * 5,
            [space(VMEM)] * 5 + [space(SMEM)],
            [pltpu.VMEM((frame // LANES, frame, LANES), jnp.float32)],
        )(slot_scan, slot_count, table, staged, probe_modes, other_probe, amplitudes)
        swapped = move(received, swap)
        send, keep = call(
            wave_kernel,
            (shape(2 * height + 8, frame), shape(2, height, frame)),
            [space(SMEM)] + [space(VMEM)] * 7,
            [space(VMEM)] * 2,
            [
                pltpu.VMEM((2, frame, frame), jnp.float32),
                pltpu.VMEM((2 * modes, 2, frame, frame), jnp.float32),
            ],
            mebibytes=24,
        )(place, own_window, received, swapped, probe, amplitude, light, matrix)
        received_change = move(send, up)
        updated, gradient, total, weight, nearer, farther, others = call(
            base_kernel,
            (
                shape(2, height, breadth),
                shape(2, height, breadth),
                shape(2, height, breadth),
                shape(height, breadth),
                shape(height, frame),
                shape(height, frame),
                shape(4, dtype=jnp.int32),
            ),
            [space(SMEM)] * 3 + [space(VMEM)] * 5,
            [space(pl.ANY)] * 2 + [space(VMEM)] * 4 + [space(SMEM)],
            [pltpu.VMEM((2, height, breadth), jnp.float32), pltpu.SemaphoreType.DMA((2,))],
        )(place, received_scan, swapped_scan, table, staged, keep, light, plain)
        swapped_change = move(received_change, swap)
        return call(
            final_kernel,
            (shape(2, height, breadth), shape(2, height, breadth)),
            [space(SMEM)] + [space(VMEM)] * 7 + [space(pl.ANY)] * 2,
            [space(pl.ANY)] * 2,
            [
                pltpu.VMEM((6, 2, height, LANES), jnp.float32),
                pltpu.VMEM((6, 2, height, LANES), jnp.float32),
                pltpu.SemaphoreType.DMA((12,)),
            ],
            aliases={8: 0, 9: 1},
        )(others, staged, total, weight, nearer, farther, received_change, swapped_change, updated, gradient)

    return jax.shard_map(
        step,
        mesh=mesh,
        in_specs=(
            P(None, "tile", None),
            P("mode", None, None, None),
            P("tile", None, None),
            P(),
            P("tile"),
            P("tile"),
        ),
        out_specs=(P(None, "tile", None), P(None, "tile", None)),
        check_vma=False,
    )
```

```python
import math

import jax
import jax.numpy as jnp
import numpy as np
from jax import lax
from jax.experimental import pallas as pl
from jax.experimental.pallas import tpu as pltpu
from jax.sharding import PartitionSpec as P


FLOOR = 0.25
ALPHA = 0.5
LANES = 128
AXES = ("tile", "mode")
VMEM = pltpu.VMEM
SMEM = pltpu.SMEM


def split(value):
    high = value.astype(jnp.bfloat16)
    low = (value - high.astype(jnp.float32)).astype(jnp.bfloat16)
    return high, low


def matrices(frame):
    half = frame // 2
    pixel = np.arange(half)[:, None]
    wave = np.arange(half)[None, :]
    blocks = []
    for parity in (0, 1):
        phase = 2.0 * math.pi * (pixel * (2 * wave + parity) % frame) / frame
        cos, sin = np.cos(phase) / math.sqrt(frame), np.sin(phase) / math.sqrt(frame)
        forward = np.block([[cos, -sin], [sin, cos]])
        for table in (forward, forward.T):
            high = table.astype(jnp.bfloat16)
            blocks.append(high)
            blocks.append((table - high.astype(np.float64)).astype(jnp.bfloat16))
    return np.stack(blocks)


def lookup(table_ref, scan):
    base = pl.multiple_of((scan // LANES) * LANES, LANES)
    chunk = table_ref[:, pl.ds(base, LANES)].astype(jnp.float32)
    lane = lax.broadcasted_iota(jnp.int32, chunk.shape, 1)
    picked = jnp.where(lane == scan - base, chunk, 0.0)
    row = jnp.sum(picked[0:1]).astype(jnp.int32)
    col = jnp.sum(picked[1:2]).astype(jnp.int32)
    return row, col


def strip_window(object_ref, col):
    blocks = object_ref.shape[2] // LANES
    block, shift = col // LANES, col % LANES
    first = object_ref[:, :, pl.ds(pl.multiple_of(block * LANES, LANES), LANES)]
    second = object_ref[:, :, pl.ds(pl.multiple_of((block + 1) * LANES, LANES), LANES)]
    last = jnp.minimum(block + 2, blocks - 1)
    third = object_ref[:, :, pl.ds(pl.multiple_of(last * LANES, LANES), LANES)]
    lane = lax.broadcasted_iota(jnp.int32, first.shape, 2)
    return jnp.where(lane < shift, third, first), second


def stage_kernel(table_ref, held_ref, sem):
    copy = pltpu.make_async_copy(table_ref, held_ref, sem)
    copy.start()
    copy.wait()


def load_kernel(probe_ref, matrix_ref, held_probe_ref, held_matrix_ref, sems):
    for copy in fetch([(probe_ref, held_probe_ref), (matrix_ref, held_matrix_ref)], sems):
        copy.wait()


def fetch(pairs, sems, first=0):
    copies = [pltpu.make_async_copy(a, b, sems.at[first + index]) for index, (a, b) in enumerate(pairs)]
    for copy in copies:
        copy.start()
    return copies


def select_kernel(own_scan_ref, scan_ref, table_ref, object_ref, out_ref, own_ref, got_ref, third_ref, sems):
    odd = lax.axis_index("tile") % 2 == 1
    for copy in fetch([(own_scan_ref, own_ref), (scan_ref, got_ref)], sems):
        copy.wait()
    scan = jnp.where(odd & (lax.axis_index("mode") == 1), own_ref[0], got_ref[0])
    _, col = lookup(table_ref, scan)
    blocks = object_ref.shape[2] // LANES
    block, shift = col // LANES, col % LANES
    last = jnp.minimum(block + 2, blocks - 1)
    pairs = [
        (object_ref.at[:, :, pl.ds(pl.multiple_of(block * LANES, LANES), 2 * LANES)], out_ref),
        (object_ref.at[:, :, pl.ds(pl.multiple_of(last * LANES, LANES), LANES)], third_ref),
    ]
    for copy in fetch(pairs, sems, 2):
        copy.wait()
    lane = lax.broadcasted_iota(jnp.int32, third_ref.shape, 2)
    out_ref[:, :, :LANES] = jnp.where(lane < shift, third_ref[...], out_ref[:, :, :LANES])


def slots(own_ref, received_ref, swapped_ref):
    first = lax.axis_index("mode") == 0
    odd = lax.axis_index("tile") % 2 == 1
    own, got, other = own_ref[0], received_ref[0], swapped_ref[0]
    above = jnp.where(first, got, other)
    further = jnp.where(first, other, got)
    return jnp.where(odd, further, own), above, jnp.where(odd, own, further)


def within(table_ref, scan, strip, height):
    row, col = lookup(table_ref, scan)
    return jnp.clip(row - strip * height, 0, height - 1), col


def roll_into(out_ref, value, row, col, tall_ref):
    frame = value.shape[0]
    half = frame // 2
    turned = pltpu.roll(value, col, 1)
    for index in range(frame // LANES):
        at = slice(index * LANES, (index + 1) * LANES)
        tall_ref[index, :half] = turned[half:, at]
        tall_ref[index, half:] = turned[:, at]
        out_ref[:, at] = tall_ref[index, pl.ds(half - row, frame), :]


def reorder_kernel(own_ref, received_ref, swapped_ref, factor_ref, rows_ref):
    frame = own_ref.shape[1]
    odd = lax.axis_index("tile") % 2 == 1
    moved = jnp.where(lax.axis_index("mode") == 0, received_ref[0], swapped_ref[0])
    value = jnp.where(odd, moved, own_ref[0])
    source = lax.broadcasted_iota(jnp.int32, (frame, frame), 0)
    target = lax.broadcasted_iota(jnp.int32, (frame, frame), 1)
    half = frame // 2
    order = jnp.where(target < half, 2 * target, 2 * target - frame + 1)
    pick = jnp.where(source == order, 1.0, 0.0).astype(jnp.bfloat16)
    high = value.astype(jnp.bfloat16)
    rest = value - high.astype(jnp.float32)
    middle = rest.astype(jnp.bfloat16)
    low = (rest - middle.astype(jnp.float32)).astype(jnp.bfloat16)
    columns = jnp.dot(high, pick, preferred_element_type=jnp.float32)
    columns = columns + jnp.dot(middle, pick, preferred_element_type=jnp.float32)
    columns = columns + jnp.dot(low, pick, preferred_element_type=jnp.float32)
    for index in range(frame // LANES):
        at = slice(index * LANES, (index + 1) * LANES)
        rows_ref[index] = columns[:, at]
        factor_ref[:half, at] = rows_ref[index, pl.ds(0, half, stride=2), :]
        factor_ref[half:, at] = rows_ref[index, pl.ds(1, half, stride=2), :]


def prepare_kernel(
    scan_ref, received_ref, swapped_ref, count_ref, table_ref, object_ref, own_probe_ref, other_probe_ref, matrix_ref,
    gradient_ref, probe_ref, window_ref, light_ref, total_ref, strip_ref, place_ref,
    zero_ref, tall_ref, own_ref, got_ref, other_ref, live_ref, sems,
):
    pairs = [(scan_ref, own_ref), (received_ref, got_ref), (swapped_ref, other_ref), (count_ref, live_ref)]
    scalars = fetch(pairs, sems)
    zero_ref[...] = jnp.zeros_like(zero_ref)
    step = zero_ref.shape[0]
    copies = []
    for part in range(2):
        for at in range(0, object_ref.shape[1], step):
            copies += fetch([(zero_ref, gradient_ref.at[part, at : at + step])], sems, len(pairs) + len(copies))
    for copy in scalars:
        copy.wait()
    modes = own_probe_ref.shape[0]
    height = object_ref.shape[1]
    frame = own_probe_ref.shape[2]
    tile = lax.axis_index("tile")
    odd = tile % 2
    scan, _, _ = slots(own_ref, got_ref, other_ref)
    row, col = within(table_ref, scan, tile - 2 * odd, height)
    shift = col % LANES
    total = jnp.zeros((frame, frame), jnp.float32)
    for index in range(2 * modes):
        source = own_probe_ref if index < modes else other_probe_ref
        for part in range(2):
            value = source[index % modes, part]
            total = total + value * value
            roll_into(probe_ref.at[index, part], value, row, shift, tall_ref.at[index, part])
    total_ref[...] = total
    roll_into(light_ref, total, row, shift, tall_ref.at[0, 0])
    low, high = strip_window(object_ref, col)
    window_ref[:, :, :LANES] = low
    window_ref[:, :, LANES:] = high
    place_ref[0] = row
    place_ref[1] = col
    place_ref[2] = jnp.where(odd == 1, (tile >= 2).astype(jnp.int32), live_ref[0])
    place_ref[3] = jnp.where(odd == 1, 0, row)
    place_ref[4] = jnp.where(odd == 1, row, height)
    for index in range(5, 8):
        place_ref[index] = 0
    transform_rows(probe_ref, 0, window_ref, matrix_ref, strip_ref)
    for copy in copies:
        copy.wait()


def right(value, high, low):
    first, second = split(value)
    return jnp.dot(
        jnp.concatenate([first, second, first], axis=1),
        jnp.concatenate([high, high, low], axis=0),
        preferred_element_type=jnp.float32,
    )


def left(high, low, value):
    first, second = split(value)
    return jnp.dot(
        jnp.concatenate([high, high, low], axis=1),
        jnp.concatenate([first, second, first], axis=0),
        preferred_element_type=jnp.float32,
    )


def transform_rows(probe_ref, start, window_ref, matrix_ref, out_ref):
    modes = probe_ref.shape[0]
    height, frame = window_ref.shape[1:]
    half = frame // 2
    sums, differences = [], []
    for mode in range(modes):
        probe_re = probe_ref[mode, 0, pl.ds(start, height), :]
        probe_im = probe_ref[mode, 1, pl.ds(start, height), :]
        wave_re = probe_re * window_ref[0] - probe_im * window_ref[1]
        wave_im = probe_re * window_ref[1] + probe_im * window_ref[0]
        for pieces, sign in ((sums, 1.0), (differences, -1.0)):
            pieces.append(
                jnp.concatenate(
                    [wave_re[:, :half] + sign * wave_re[:, half:], wave_im[:, :half] + sign * wave_im[:, half:]],
                    axis=1,
                )
            )
    even = right(jnp.concatenate(sums, axis=0), matrix_ref[0], matrix_ref[1])
    odd = right(jnp.concatenate(differences, axis=0), matrix_ref[4], matrix_ref[5])
    for mode in range(modes):
        at = slice(mode * height, (mode + 1) * height)
        out_ref[mode, 0] = jnp.concatenate([even[at, :half], odd[at, :half]], axis=1)
        out_ref[mode, 1] = jnp.concatenate([even[at, half:], odd[at, half:]], axis=1)


def strip_kernel(received_ref, probe_ref, matrix_ref, out_ref):
    height = received_ref.shape[1]
    start = pl.multiple_of((1 - lax.axis_index("mode")) * height, height)
    transform_rows(probe_ref, start, received_ref, matrix_ref, out_ref)


def wave_kernel(
    place_ref, window_ref, received_ref, swapped_ref, own_ref, first_ref, probe_ref, amplitude_ref, light_ref,
    matrix_ref, send_ref, keep_ref, patch_ref, far_ref, second_ref,
):
    modes, _, frame, _ = probe_ref.shape
    height = window_ref.shape[1]
    half = frame // 2
    core = lax.axis_index("mode")
    low, high = place_ref[3], place_ref[4]
    transform_rows(probe_ref, pl.multiple_of(core * height, height), swapped_ref, matrix_ref, second_ref)
    level = lax.broadcasted_iota(jnp.int32, (height, frame), 0)

    def assemble(own, got, given):
        nearer = jnp.where(core == 0, got, given)
        farther = jnp.where(core == 0, given, got)
        return jnp.where((level >= low) & (level < high), own, farther), nearer

    for part in range(2):
        top, bottom = assemble(window_ref[part], received_ref[part], swapped_ref[part])
        patch_ref[part, :height] = top
        patch_ref[part, height:] = bottom
    intensity = jnp.zeros((frame, frame), jnp.float32)
    for mode in range(modes):
        top_re, bottom_re = assemble(own_ref[mode, 0], first_ref[mode, 0], second_ref[mode, 0])
        top_im, bottom_im = assemble(own_ref[mode, 1], first_ref[mode, 1], second_ref[mode, 1])
        added = jnp.concatenate([top_re + bottom_re, top_im + bottom_im], axis=0)
        taken = jnp.concatenate([top_re - bottom_re, top_im - bottom_im], axis=0)
        even = left(matrix_ref[2], matrix_ref[3], added)
        odd = left(matrix_ref[6], matrix_ref[7], taken)
        far_ref[mode, 0] = even
        far_ref[mode, 1] = odd
        squares = jnp.concatenate(
            [even[:half] * even[:half] + even[half:] * even[half:], odd[:half] * odd[:half] + odd[half:] * odd[half:]],
            axis=0,
        )
        intensity = intensity + squares
    factor = amplitude_ref[...] * lax.rsqrt(jnp.maximum(intensity, FLOOR))
    grad_re = jnp.zeros((frame, frame), jnp.float32)
    grad_im = jnp.zeros((frame, frame), jnp.float32)
    even_factor = jnp.concatenate([factor[:half], factor[:half]], axis=0)
    odd_factor = jnp.concatenate([factor[half:], factor[half:]], axis=0)
    evens, odds = [], []
    for mode in range(modes):
        even = left(matrix_ref[0], matrix_ref[1], far_ref[mode, 0] * even_factor)
        odd = left(matrix_ref[4], matrix_ref[5], far_ref[mode, 1] * odd_factor)
        top, bottom = even + odd, even - odd
        mid_re = jnp.concatenate([top[:half], bottom[:half]], axis=0)
        mid_im = jnp.concatenate([top[half:], bottom[half:]], axis=0)
        evens.append(jnp.concatenate([mid_re[:, :half], mid_im[:, :half]], axis=1))
        odds.append(jnp.concatenate([mid_re[:, half:], mid_im[:, half:]], axis=1))
    even = right(jnp.concatenate(evens, axis=0), matrix_ref[2], matrix_ref[3])
    odd = right(jnp.concatenate(odds, axis=0), matrix_ref[6], matrix_ref[7])
    fores, afts = even + odd, even - odd
    for mode in range(modes):
        fore = fores[mode * frame : (mode + 1) * frame]
        aft = afts[mode * frame : (mode + 1) * frame]
        back_re = jnp.concatenate([fore[:, :half], aft[:, :half]], axis=1)
        back_im = jnp.concatenate([fore[:, half:], aft[:, half:]], axis=1)
        probe_re, probe_im = probe_ref[mode, 0], probe_ref[mode, 1]
        grad_re = grad_re + (probe_re * back_re + probe_im * back_im)
        grad_im = grad_im + (probe_re * back_im - probe_im * back_re)
    live = (place_ref[2] > 0).astype(jnp.float32)
    grad_re = (grad_re - light_ref[...] * patch_ref[0]) * live
    grad_im = (grad_im - light_ref[...] * patch_ref[1]) * live
    send_ref[:height] = jnp.where(core == 0, grad_re[height:], grad_re[:height])
    send_ref[height : 2 * height] = jnp.where(core == 0, grad_im[height:], grad_im[:height])
    send_ref[2 * height :] = jnp.full((8, frame), live, jnp.float32)
    keep_ref[0] = grad_re[:height]
    keep_ref[1] = grad_im[:height]


def covers(col, block, low, high, lane):
    start, shift = col // LANES, col % LANES
    distance = block - start
    value = jnp.where(distance == 1, high, low)
    first = jnp.where(distance == 0, shift, jnp.where(distance == 1, 0, LANES))
    last = jnp.where(distance == 2, shift, 0)
    keep = (lane >= first) | (lane < last)
    return jnp.where(keep, value, 0.0)


def base_kernel(
    place_ref, scan_ref, received_ref, swapped_ref, table_ref, object_ref, keep_ref, light_ref, plain_ref,
    old_gradient_ref,
    updated_ref, gradient_ref, total_ref, weight_ref, first_ref, second_ref, others_ref, new_ref, tall_ref, turned_ref,
    own_ref, got_ref, other_ref, sems, fills,
):
    del old_gradient_ref
    height, breadth = object_ref.shape[1:]
    tile = lax.axis_index("tile")
    core = lax.axis_index("mode")
    col = place_ref[1]
    fill = pltpu.make_async_copy(object_ref, updated_ref, fills.at[0])
    fill.start()
    scalars = fetch([(scan_ref, own_ref), (received_ref, got_ref), (swapped_ref, other_ref)], fills, 1)
    live = (place_ref[2] > 0).astype(jnp.float32)
    total_ref[...] = jnp.zeros_like(total_ref)
    weight_ref[...] = jnp.zeros_like(weight_ref)
    lane = lax.broadcasted_iota(jnp.int32, (height, LANES), 1)
    level = lax.broadcasted_iota(jnp.int32, (height, LANES), 0)
    kept = (level >= place_ref[3]) & (level < place_ref[4])
    for slot in range(3):
        block = jnp.minimum(col // LANES + slot, breadth // LANES - 1)
        at = pl.ds(pl.multiple_of(block * LANES, LANES), LANES)
        light = covers(col, block, light_ref[:height, :LANES], light_ref[:height, LANES:], lane)
        weight = jnp.where(kept, light * live, 0.0)
        weight_ref[:, at] = weight
        scale = 1.0 / (weight + ALPHA)
        for part in range(2):
            change = covers(col, block, keep_ref[part, :, :LANES], keep_ref[part, :, LANES:], lane)
            change = jnp.where(kept, change, 0.0)
            total_ref[part, :, at] = change
            new_ref[slot, part] = object_ref[part, :, at] + change * scale
    odd = tile % 2
    for copy in scalars:
        copy.wait()
    _, above, third = slots(own_ref, got_ref, other_ref)
    places = []
    for scan, strip, far in ((above, tile - 1, False), (third, tile - 2 + 2 * odd, True)):
        row, start = within(table_ref, scan, strip, height)
        index = int(far)
        roll_into(turned_ref.at[index], plain_ref[...], row, start % LANES, tall_ref.at[index])
        turned = turned_ref[index]
        begin = jnp.where(odd == 1, row, 0) if far else 0
        end = jnp.where(odd == 1, height, row) if far else height
        places.append((start, begin, end, turned[:height] if far else turned[height:]))
    for slot, out_ref in ((0, first_ref), (1, second_ref)):
        direct = core == slot
        near, far = places
        out_ref[...] = jnp.where(direct, near[3], far[3])
        for index in range(3):
            others_ref[4 * slot + index] = jnp.where(direct, near[index], far[index])
        others_ref[4 * slot + 3] = 0
    fill.wait()
    copies = []
    for slot in range(3):
        block = jnp.minimum(col // LANES + slot, breadth // LANES - 1)
        at = pl.ds(pl.multiple_of(block * LANES, LANES), LANES)
        copies.append(write(slot, col, block, at, total_ref.at[:, :, at], new_ref, gradient_ref, updated_ref, sems))
    finish(copies)


def write(slot, col, block, at, source, new_ref, gradient_ref, updated_ref, sems):
    fresh = col // LANES + slot == block
    one = pltpu.make_async_copy(source, gradient_ref.at[:, :, at], sems.at[2 * slot])
    two = pltpu.make_async_copy(new_ref.at[slot], updated_ref.at[:, :, at], sems.at[2 * slot + 1])

    @pl.when(fresh)
    def _():
        one.start()
        two.start()

    return fresh, one, two


def finish(copies):
    for fresh, one, two in copies:

        @pl.when(fresh)
        def _(one=one, two=two):
            one.wait()
            two.wait()


def add_windows(windows, main, object_ref, total_ref, weight_ref, updated_ref, gradient_ref, new_ref, sum_ref, sems):
    height, breadth = object_ref.shape[1:]
    lane = lax.broadcasted_iota(jnp.int32, (height, LANES), 1)
    level = lax.broadcasted_iota(jnp.int32, (height, LANES), 0)
    col = windows[main][0]
    copies = []
    for slot in range(3):
        block = jnp.minimum(col // LANES + slot, breadth // LANES - 1)
        at = pl.ds(pl.multiple_of(block * LANES, LANES), LANES)
        weight = weight_ref[:, at]
        sums = [total_ref[0, :, at], total_ref[1, :, at]]
        for start, begin, end, light_ref, change_ref in windows:
            inside = (level >= begin) & (level < end)
            live = change_ref[2 * height : 2 * height + 1, :1]
            light = covers(start, block, light_ref[:, :LANES], light_ref[:, LANES:], lane)
            weight = weight + jnp.where(inside, light, 0.0) * live
            for part in range(2):
                rows = slice(part * height, (part + 1) * height)
                change = covers(start, block, change_ref[rows, :LANES], change_ref[rows, LANES:], lane)
                sums[part] = sums[part] + jnp.where(inside, change, 0.0)
        scale = 1.0 / (weight + ALPHA)
        for part in range(2):
            sum_ref[slot, part] = sums[part]
            new_ref[slot, part] = object_ref[part, :, at] + sums[part] * scale
        copies.append(write(slot, col, block, at, sum_ref.at[slot], new_ref, gradient_ref, updated_ref, sems))
    finish(copies)


def first_kernel(
    others_ref, object_ref, total_ref, weight_ref, first_ref, received_ref, old_updated_ref, old_gradient_ref,
    updated_ref, gradient_ref, new_ref, sum_ref, sems,
):
    del old_updated_ref, old_gradient_ref
    windows = [(others_ref[0], others_ref[1], others_ref[2], first_ref, received_ref)]
    add_windows(windows, 0, object_ref, total_ref, weight_ref, updated_ref, gradient_ref, new_ref, sum_ref, sems)


def second_kernel(
    others_ref, object_ref, total_ref, weight_ref, first_ref, second_ref, received_ref, swapped_ref,
    old_updated_ref, old_gradient_ref, updated_ref, gradient_ref, new_ref, sum_ref, sems,
):
    del old_updated_ref, old_gradient_ref
    windows = [
        (others_ref[0], others_ref[1], others_ref[2], first_ref, received_ref),
        (others_ref[4], others_ref[5], others_ref[6], second_ref, swapped_ref),
    ]
    add_windows(windows, 1, object_ref, total_ref, weight_ref, updated_ref, gradient_ref, new_ref, sum_ref, sems)


def call(kernel, out_shape, in_specs, out_specs, scratch=(), mebibytes=16, aliases=None):
    return pl.pallas_call(
        kernel,
        out_shape=out_shape,
        in_specs=in_specs,
        out_specs=out_specs,
        scratch_shapes=list(scratch),
        input_output_aliases=aliases or {},
        compiler_params=pltpu.CompilerParams(vmem_limit_bytes=mebibytes << 20),
        cost_estimate=pl.CostEstimate(flops=5000000, bytes_accessed=5000000, transcendentals=0),
    )


def in_hbm(value):
    return pltpu.with_memory_space_constraint(value, pltpu.HBM)


def space(where):
    return pl.BlockSpec(memory_space=where)


def shape(*dims, dtype=jnp.float32):
    return jax.ShapeDtypeStruct(dims, dtype)


def solution(mesh):
    tiles, cores = mesh.shape["tile"], mesh.shape["mode"]
    up = [(2 * t, 2 * (t + 1)) for t in range(tiles - 1)] + [(2 * t + 1, 2 * (t + 2) + 1) for t in range(tiles - 2)]
    gather = [(2 * t, 2 * (t ^ 1)) for t in range(tiles)]
    gather += [(2 * t + 1, 2 * (t - 2) + 1) for t in range(2, tiles, 2)]
    gather += [(2 * t + 1, 2 * (t + 2) + 1) for t in range(1, tiles - 2, 2)]
    spread = [(target, source) for source, target in gather]
    onward = [(2 * t, 2 * (t + 2)) for t in range(1, tiles - 2, 2)]
    swap = [(2 * t + core, 2 * t + 1 - core) for t in range(tiles) for core in range(2)]
    assert cores == 2 and tiles % 2 == 0

    def move(value, pairs):
        return lax.ppermute(value, AXES, pairs)

    def step(object_tiles, probe_modes, amplitudes, scan_offsets, slot_scan, slot_count):
        height, breadth = object_tiles.shape[1:]
        modes, _, frame, _ = probe_modes.shape
        assert slot_scan.shape[0] == 1 and frame == 2 * height and height == LANES
        table = scan_offsets.T
        matrix = jnp.asarray(matrices(frame))
        received_scan = move(slot_scan, up)
        other_probe = move(probe_modes, swap)
        received_amplitude = move(amplitudes, onward)
        scalar = pltpu.SMEM((1,), jnp.int32)
        staged = object_tiles
        table = call(
            stage_kernel,
            shape(*table.shape, dtype=jnp.int32),
            [space(pltpu.HBM)],
            space(VMEM),
            [pltpu.SemaphoreType.DMA],
            mebibytes=8,
        )(in_hbm(table))
        window = call(
            select_kernel,
            shape(2, height, frame),
            [space(pl.ANY)] * 2 + [space(VMEM), space(pl.ANY)],
            space(VMEM),
            [scalar, scalar, pltpu.VMEM((2, height, LANES), jnp.float32), pltpu.SemaphoreType.DMA((4,))],
        )(slot_scan, received_scan, table, in_hbm(object_tiles))
        received = move(window, gather)
        swapped_scan = move(received_scan, swap)
        swapped_amplitude = move(received_amplitude, swap)
        own_probe, matrix = call(
            load_kernel,
            (shape(*probe_modes.shape), shape(*matrix.shape, dtype=matrix.dtype)),
            [space(pltpu.HBM)] * 2,
            [space(VMEM)] * 2,
            [pltpu.SemaphoreType.DMA((2,))],
            mebibytes=8,
        )(in_hbm(probe_modes), in_hbm(matrix))
        strip = shape(2 * modes, 2, height, frame)
        whole = shape(2, height, breadth)
        gradient, probe, own_window, light, plain, own_strip, place = call(
            prepare_kernel,
            (
                whole,
                shape(2 * modes, 2, frame, frame),
                shape(2, height, frame),
                shape(frame, frame),
                shape(frame, frame),
                strip,
                shape(8, dtype=jnp.int32),
            ),
            [space(pl.ANY)] * 4 + [space(VMEM)] * 5,
            [space(pl.ANY)] + [space(VMEM)] * 5 + [space(SMEM)],
            [
                pltpu.VMEM((height // 8, breadth), jnp.float32),
                pltpu.VMEM((2 * modes, 2, frame // LANES, frame + height, LANES), jnp.float32),
                scalar,
                scalar,
                scalar,
                scalar,
                pltpu.SemaphoreType.DMA((20,)),
            ],
        )(slot_scan, received_scan, swapped_scan, slot_count, table, staged, own_probe, other_probe, matrix)
        swapped = move(received, swap)
        amplitude = call(
            reorder_kernel,
            shape(frame, frame),
            [space(VMEM)] * 3,
            space(VMEM),
            [pltpu.VMEM((frame // LANES, frame, LANES), jnp.float32)],
        )(amplitudes, received_amplitude, swapped_amplitude)
        first_strip = call(strip_kernel, strip, [space(VMEM)] * 3, space(VMEM))(received, probe, matrix)
        send, keep = call(
            wave_kernel,
            (shape(2 * height + 8, frame), shape(2, height, frame)),
            [space(SMEM)] + [space(VMEM)] * 9,
            [space(VMEM)] * 2,
            [
                pltpu.VMEM((2, frame, frame), jnp.float32),
                pltpu.VMEM((2 * modes, 2, frame, frame), jnp.float32),
                pltpu.VMEM((2 * modes, 2, height, frame), jnp.float32),
            ],
            mebibytes=24,
        )(place, own_window, received, swapped, own_strip, first_strip, probe, amplitude, light, matrix)
        received_change = move(send, spread)
        blocks = pltpu.VMEM((3, 2, height, LANES), jnp.float32)
        semaphores = pltpu.SemaphoreType.DMA((6,))
        updated, gradient, total, weight, first, second, others = call(
            base_kernel,
            (
                whole,
                whole,
                whole,
                shape(height, breadth),
                shape(height, frame),
                shape(height, frame),
                shape(8, dtype=jnp.int32),
            ),
            [space(SMEM)] + [space(pl.ANY)] * 3 + [space(VMEM)] * 5 + [space(pl.ANY)],
            [space(pl.ANY)] * 2 + [space(VMEM)] * 4 + [space(SMEM)],
            [
                blocks,
                pltpu.VMEM((2, frame // LANES, frame + height, LANES), jnp.float32),
                pltpu.VMEM((2, frame, frame), jnp.float32),
                scalar,
                scalar,
                scalar,
                semaphores,
                pltpu.SemaphoreType.DMA((4,)),
            ],
            aliases={9: 1},
        )(place, slot_scan, received_scan, swapped_scan, table, staged, keep, light, plain, gradient)
        swapped_change = move(received_change, swap)
        updated, gradient = call(
            first_kernel,
            (whole, whole),
            [space(SMEM)] + [space(VMEM)] * 5 + [space(pl.ANY)] * 2,
            [space(pl.ANY)] * 2,
            [blocks, blocks, semaphores],
            aliases={6: 0, 7: 1},
        )(others, staged, total, weight, first, received_change, updated, gradient)
        return call(
            second_kernel,
            (whole, whole),
            [space(SMEM)] + [space(VMEM)] * 7 + [space(pl.ANY)] * 2,
            [space(pl.ANY)] * 2,
            [blocks, blocks, semaphores],
            aliases={8: 0, 9: 1},
        )(others, staged, total, weight, first, second, received_change, swapped_change, updated, gradient)

    return jax.shard_map(
        step,
        mesh=mesh,
        in_specs=(
            P(None, "tile", None),
            P("mode", None, None, None),
            P("tile", None, None),
            P(),
            P("tile"),
            P("tile"),
        ),
        out_specs=(P(None, "tile", None), P(None, "tile", None)),
        check_vma=False,
    )
```

```python
import math

import jax
import jax.numpy as jnp
import numpy as np
from jax import lax
from jax.experimental import pallas as pl
from jax.experimental.pallas import tpu as pltpu
from jax.sharding import PartitionSpec as P


FLOOR = 0.25
ALPHA = 0.5
LANES = 128
AXES = ("tile", "mode")
VMEM = pltpu.VMEM
SMEM = pltpu.SMEM


def split(value):
    high = value.astype(jnp.bfloat16)
    low = (value - high.astype(jnp.float32)).astype(jnp.bfloat16)
    return high, low


def matrices(frame):
    half = frame // 2
    pixel = np.arange(half)[:, None]
    wave = np.arange(half)[None, :]
    blocks = []
    for parity in (0, 1):
        phase = 2.0 * math.pi * (pixel * (2 * wave + parity) % frame) / frame
        cos, sin = np.cos(phase) / math.sqrt(frame), np.sin(phase) / math.sqrt(frame)
        forward = np.block([[cos, -sin], [sin, cos]])
        for table in (forward, forward.T):
            high = table.astype(jnp.bfloat16)
            blocks.append(high)
            blocks.append((table - high.astype(np.float64)).astype(jnp.bfloat16))
    return np.stack(blocks)


def lookup(table_ref, scan):
    base = pl.multiple_of((scan // LANES) * LANES, LANES)
    chunk = table_ref[:, pl.ds(base, LANES)].astype(jnp.float32)
    lane = lax.broadcasted_iota(jnp.int32, chunk.shape, 1)
    picked = jnp.where(lane == scan - base, chunk, 0.0)
    row = jnp.sum(picked[0:1]).astype(jnp.int32)
    col = jnp.sum(picked[1:2]).astype(jnp.int32)
    return row, col


def strip_window(object_ref, col):
    blocks = object_ref.shape[2] // LANES
    block, shift = col // LANES, col % LANES
    first = object_ref[:, :, pl.ds(pl.multiple_of(block * LANES, LANES), LANES)]
    second = object_ref[:, :, pl.ds(pl.multiple_of((block + 1) * LANES, LANES), LANES)]
    last = jnp.minimum(block + 2, blocks - 1)
    third = object_ref[:, :, pl.ds(pl.multiple_of(last * LANES, LANES), LANES)]
    lane = lax.broadcasted_iota(jnp.int32, first.shape, 2)
    return jnp.where(lane < shift, third, first), second


def stage_kernel(object_ref, table_ref, staged_ref, held_ref, sems):
    first = pltpu.make_async_copy(object_ref, staged_ref, sems.at[0])
    second = pltpu.make_async_copy(table_ref, held_ref, sems.at[1])
    first.start()
    second.start()
    first.wait()
    second.wait()


def fetch(pairs, sems, first=0):
    copies = [pltpu.make_async_copy(a, b, sems.at[first + index]) for index, (a, b) in enumerate(pairs)]
    for copy in copies:
        copy.start()
    return copies


def select_kernel(own_scan_ref, scan_ref, table_ref, object_ref, out_ref):
    odd = lax.axis_index("tile") % 2 == 1
    scan = jnp.where(odd & (lax.axis_index("mode") == 1), own_scan_ref[0], scan_ref[0])
    _, col = lookup(table_ref, scan)
    low, high = strip_window(object_ref, col)
    out_ref[:, :, :LANES] = low
    out_ref[:, :, LANES:] = high


def slots(own_ref, received_ref, swapped_ref):
    first = lax.axis_index("mode") == 0
    odd = lax.axis_index("tile") % 2 == 1
    own, got, other = own_ref[0], received_ref[0], swapped_ref[0]
    above = jnp.where(first, got, other)
    further = jnp.where(first, other, got)
    return jnp.where(odd, further, own), above, jnp.where(odd, own, further)


def keep_scalars(out_ref, values):
    for index, value in enumerate(values):
        row = jnp.full((1, out_ref.shape[1]), value, jnp.int32)
        out_ref[index : index + 1] = row.astype(jnp.float32)


def scalar_of(ref, index):
    return jnp.max(ref[index : index + 1]).astype(jnp.int32)


def within(table_ref, scan, strip, height):
    row, col = lookup(table_ref, scan)
    return jnp.clip(row - strip * height, 0, height - 1), col


def roll_into(out_ref, value, row, col, tall_ref):
    frame = value.shape[0]
    half = frame // 2
    turned = pltpu.roll(value, col, 1)
    for index in range(frame // LANES):
        at = slice(index * LANES, (index + 1) * LANES)
        tall_ref[index, :half] = turned[half:, at]
        tall_ref[index, half:] = turned[:, at]
        out_ref[:, at] = tall_ref[index, pl.ds(half - row, frame), :]


def reorder_kernel(own_ref, received_ref, swapped_ref, factor_ref, rows_ref):
    frame = own_ref.shape[1]
    odd = lax.axis_index("tile") % 2 == 1
    moved = jnp.where(lax.axis_index("mode") == 0, received_ref[0], swapped_ref[0])
    value = jnp.where(odd, moved, own_ref[0])
    source = lax.broadcasted_iota(jnp.int32, (frame, frame), 0)
    target = lax.broadcasted_iota(jnp.int32, (frame, frame), 1)
    half = frame // 2
    order = jnp.where(target < half, 2 * target, 2 * target - frame + 1)
    pick = jnp.where(source == order, 1.0, 0.0).astype(jnp.bfloat16)
    high = value.astype(jnp.bfloat16)
    rest = value - high.astype(jnp.float32)
    middle = rest.astype(jnp.bfloat16)
    low = (rest - middle.astype(jnp.float32)).astype(jnp.bfloat16)
    columns = jnp.dot(high, pick, preferred_element_type=jnp.float32)
    columns = columns + jnp.dot(middle, pick, preferred_element_type=jnp.float32)
    columns = columns + jnp.dot(low, pick, preferred_element_type=jnp.float32)
    for index in range(frame // LANES):
        at = slice(index * LANES, (index + 1) * LANES)
        rows_ref[index] = columns[:, at]
        factor_ref[:half, at] = rows_ref[index, pl.ds(0, half, stride=2), :]
        factor_ref[half:, at] = rows_ref[index, pl.ds(1, half, stride=2), :]


def prepare_kernel(
    scan_ref, received_ref, swapped_ref, table_ref, object_ref, own_probe_ref, other_probe_ref, matrix_ref,
    gradient_ref, probe_ref, window_ref, light_ref, total_ref, strip_ref, place_ref,
    zero_ref, tall_ref, own_ref, got_ref, other_ref, sems,
):
    pairs = [(scan_ref, own_ref), (received_ref, got_ref), (swapped_ref, other_ref)]
    scalars = fetch(pairs, sems)
    zero_ref[...] = jnp.zeros_like(zero_ref)
    step = zero_ref.shape[0]
    copies = []
    for part in range(2):
        for at in range(0, object_ref.shape[1], step):
            copies += fetch([(zero_ref, gradient_ref.at[part, at : at + step])], sems, len(pairs) + len(copies))
    modes = own_probe_ref.shape[0]
    sources = [ref.at[mode, part] for ref in (own_probe_ref, other_probe_ref) for mode in range(modes) for part in range(2)]
    total = sources[0][...] * sources[0][...]
    for source in sources[1:]:
        total = total + source[...] * source[...]
    total_ref[...] = total
    for copy in scalars:
        copy.wait()
    height = object_ref.shape[1]
    tile = lax.axis_index("tile")
    odd = tile % 2
    scan, _, _ = slots(own_ref, got_ref, other_ref)
    row, col = within(table_ref, scan, tile - 2 * odd, height)
    shift = col % LANES
    for index, source in enumerate(sources):
        mode, part = divmod(index, 2)
        roll_into(probe_ref.at[mode, part], source[...], row, shift, tall_ref.at[mode, part])
    roll_into(light_ref, total_ref[...], row, shift, tall_ref.at[0, 0])
    low, high = strip_window(object_ref, col)
    window_ref[:, :, :LANES] = low
    window_ref[:, :, LANES:] = high
    live = jnp.where(odd == 1, (tile >= 2).astype(jnp.int32), 1)
    keep_scalars(place_ref, (jnp.where(odd == 1, 0, row), jnp.where(odd == 1, row, height), live))
    transform_rows(probe_ref, 0, window_ref, matrix_ref, strip_ref)
    for copy in copies:
        copy.wait()


def right(value, high, low):
    first, second = split(value)
    return jnp.dot(
        jnp.concatenate([first, second, first], axis=1),
        jnp.concatenate([high, high, low], axis=0),
        preferred_element_type=jnp.float32,
    )


def left(high, low, value):
    first, second = split(value)
    return jnp.dot(
        jnp.concatenate([high, high, low], axis=1),
        jnp.concatenate([first, second, first], axis=0),
        preferred_element_type=jnp.float32,
    )


def transform_rows(probe_ref, start, window_ref, matrix_ref, out_ref):
    modes = probe_ref.shape[0]
    height, frame = window_ref.shape[1:]
    half = frame // 2
    sums, differences = [], []
    for mode in range(modes):
        probe_re = probe_ref[mode, 0, pl.ds(start, height), :]
        probe_im = probe_ref[mode, 1, pl.ds(start, height), :]
        wave_re = probe_re * window_ref[0] - probe_im * window_ref[1]
        wave_im = probe_re * window_ref[1] + probe_im * window_ref[0]
        for pieces, sign in ((sums, 1.0), (differences, -1.0)):
            pieces.append(
                jnp.concatenate(
                    [wave_re[:, :half] + sign * wave_re[:, half:], wave_im[:, :half] + sign * wave_im[:, half:]],
                    axis=1,
                )
            )
    even = right(jnp.concatenate(sums, axis=0), matrix_ref[0], matrix_ref[1])
    odd = right(jnp.concatenate(differences, axis=0), matrix_ref[4], matrix_ref[5])
    for mode in range(modes):
        at = slice(mode * height, (mode + 1) * height)
        out_ref[mode, 0] = jnp.concatenate([even[at, :half], odd[at, :half]], axis=1)
        out_ref[mode, 1] = jnp.concatenate([even[at, half:], odd[at, half:]], axis=1)


def strip_kernel(received_ref, probe_ref, matrix_ref, out_ref):
    height = received_ref.shape[1]
    start = pl.multiple_of((1 - lax.axis_index("mode")) * height, height)
    transform_rows(probe_ref, start, received_ref, matrix_ref, out_ref)


def wave_kernel(
    place_ref, window_ref, received_ref, swapped_ref, own_ref, first_ref, probe_ref, amplitude_ref, light_ref,
    matrix_ref, send_ref, keep_ref, patch_ref, far_ref, second_ref,
):
    modes, _, frame, _ = probe_ref.shape
    height = window_ref.shape[1]
    half = frame // 2
    core = lax.axis_index("mode")
    low, high = place_ref[0:1, :1].astype(jnp.int32), place_ref[1:2, :1].astype(jnp.int32)
    transform_rows(probe_ref, pl.multiple_of(core * height, height), swapped_ref, matrix_ref, second_ref)
    level = lax.broadcasted_iota(jnp.int32, (height, frame), 0)

    def assemble(own, got, given):
        nearer = jnp.where(core == 0, got, given)
        farther = jnp.where(core == 0, given, got)
        return jnp.where((level >= low) & (level < high), own, farther), nearer

    for part in range(2):
        top, bottom = assemble(window_ref[part], received_ref[part], swapped_ref[part])
        patch_ref[part, :height] = top
        patch_ref[part, height:] = bottom
    intensity = jnp.zeros((frame, frame), jnp.float32)
    for mode in range(modes):
        top_re, bottom_re = assemble(own_ref[mode, 0], first_ref[mode, 0], second_ref[mode, 0])
        top_im, bottom_im = assemble(own_ref[mode, 1], first_ref[mode, 1], second_ref[mode, 1])
        added = jnp.concatenate([top_re + bottom_re, top_im + bottom_im], axis=0)
        taken = jnp.concatenate([top_re - bottom_re, top_im - bottom_im], axis=0)
        even = left(matrix_ref[2], matrix_ref[3], added)
        odd = left(matrix_ref[6], matrix_ref[7], taken)
        far_ref[mode, 0] = even
        far_ref[mode, 1] = odd
        squares = jnp.concatenate(
            [even[:half] * even[:half] + even[half:] * even[half:], odd[:half] * odd[:half] + odd[half:] * odd[half:]],
            axis=0,
        )
        intensity = intensity + squares
    factor = amplitude_ref[...] * lax.rsqrt(jnp.maximum(intensity, FLOOR))
    grad_re = jnp.zeros((frame, frame), jnp.float32)
    grad_im = jnp.zeros((frame, frame), jnp.float32)
    even_factor = jnp.concatenate([factor[:half], factor[:half]], axis=0)
    odd_factor = jnp.concatenate([factor[half:], factor[half:]], axis=0)
    evens, odds = [], []
    for mode in range(modes):
        even = left(matrix_ref[0], matrix_ref[1], far_ref[mode, 0] * even_factor)
        odd = left(matrix_ref[4], matrix_ref[5], far_ref[mode, 1] * odd_factor)
        top, bottom = even + odd, even - odd
        mid_re = jnp.concatenate([top[:half], bottom[:half]], axis=0)
        mid_im = jnp.concatenate([top[half:], bottom[half:]], axis=0)
        evens.append(jnp.concatenate([mid_re[:, :half], mid_im[:, :half]], axis=1))
        odds.append(jnp.concatenate([mid_re[:, half:], mid_im[:, half:]], axis=1))
    even = right(jnp.concatenate(evens, axis=0), matrix_ref[2], matrix_ref[3])
    odd = right(jnp.concatenate(odds, axis=0), matrix_ref[6], matrix_ref[7])
    fores, afts = even + odd, even - odd
    for mode in range(modes):
        fore = fores[mode * frame : (mode + 1) * frame]
        aft = afts[mode * frame : (mode + 1) * frame]
        back_re = jnp.concatenate([fore[:, :half], aft[:, :half]], axis=1)
        back_im = jnp.concatenate([fore[:, half:], aft[:, half:]], axis=1)
        probe_re, probe_im = probe_ref[mode, 0], probe_ref[mode, 1]
        grad_re = grad_re + (probe_re * back_re + probe_im * back_im)
        grad_im = grad_im + (probe_re * back_im - probe_im * back_re)
    live = place_ref[2:3, :1]
    grad_re = (grad_re - light_ref[...] * patch_ref[0]) * live
    grad_im = (grad_im - light_ref[...] * patch_ref[1]) * live
    send_ref[:height] = jnp.where(core == 0, grad_re[height:], grad_re[:height])
    send_ref[height : 2 * height] = jnp.where(core == 0, grad_im[height:], grad_im[:height])
    send_ref[2 * height :] = jnp.broadcast_to(live, (8, frame))
    keep_ref[0] = grad_re[:height]
    keep_ref[1] = grad_im[:height]


def covers(col, block, low, high, lane):
    start, shift = col // LANES, col % LANES
    distance = block - start
    value = jnp.where(distance == 1, high, low)
    first = jnp.where(distance == 0, shift, jnp.where(distance == 1, 0, LANES))
    last = jnp.where(distance == 2, shift, 0)
    keep = (lane >= first) | (lane < last)
    return jnp.where(keep, value, 0.0)


def base_kernel(
    place_ref, scan_ref, received_ref, swapped_ref, table_ref, object_ref, keep_ref, light_ref, plain_ref,
    old_gradient_ref,
    updated_ref, gradient_ref, total_ref, weight_ref, first_ref, second_ref, others_ref, new_ref, tall_ref, turned_ref,
    own_ref, got_ref, other_ref, sems, fills,
):
    del old_gradient_ref
    height, breadth = object_ref.shape[1:]
    tile = lax.axis_index("tile")
    core = lax.axis_index("mode")
    fill = pltpu.make_async_copy(object_ref, updated_ref, fills.at[0])
    fill.start()
    scalars = fetch([(scan_ref, own_ref), (received_ref, got_ref), (swapped_ref, other_ref)], fills, 1)
    total_ref[...] = jnp.zeros_like(total_ref)
    weight_ref[...] = jnp.zeros_like(weight_ref)
    for copy in scalars:
        copy.wait()
    odd = tile % 2
    main, above, third = slots(own_ref, got_ref, other_ref)
    _, col = within(table_ref, main, tile, height)
    live = place_ref[2:3, :1]
    start, stop = place_ref[0:1, :1].astype(jnp.int32), place_ref[1:2, :1].astype(jnp.int32)
    lane = lax.broadcasted_iota(jnp.int32, (height, LANES), 1)
    level = lax.broadcasted_iota(jnp.int32, (height, LANES), 0)
    kept = (level >= start) & (level < stop)
    for slot in range(3):
        block = jnp.minimum(col // LANES + slot, breadth // LANES - 1)
        at = pl.ds(pl.multiple_of(block * LANES, LANES), LANES)
        light = covers(col, block, light_ref[:height, :LANES], light_ref[:height, LANES:], lane)
        weight = jnp.where(kept, light * live, 0.0)
        weight_ref[:, at] = weight
        scale = 1.0 / (weight + ALPHA)
        for part in range(2):
            change = covers(col, block, keep_ref[part, :, :LANES], keep_ref[part, :, LANES:], lane)
            change = jnp.where(kept, change, 0.0)
            total_ref[part, :, at] = change
            new_ref[slot, part] = object_ref[part, :, at] + change * scale
    places = []
    for scan, strip, far in ((above, tile - 1, False), (third, tile - 2 + 2 * odd, True)):
        row, start = within(table_ref, scan, strip, height)
        index = int(far)
        roll_into(turned_ref.at[index], plain_ref[...], row, start % LANES, tall_ref.at[index])
        turned = turned_ref[index]
        begin = jnp.where(odd == 1, row, 0) if far else 0
        end = jnp.where(odd == 1, height, row) if far else height
        places.append((start, begin, end, turned[:height] if far else turned[height:]))
    chosen = []
    for slot, out_ref in ((0, first_ref), (1, second_ref)):
        direct = core == slot
        near, far = places
        out_ref[...] = jnp.where(direct, near[3], far[3])
        chosen += [jnp.where(direct, near[index], far[index]) for index in range(3)]
    keep_scalars(others_ref, chosen)
    fill.wait()
    copies = []
    for slot in range(3):
        block = jnp.minimum(col // LANES + slot, breadth // LANES - 1)
        at = pl.ds(pl.multiple_of(block * LANES, LANES), LANES)
        copies.append(write(slot, col, block, at, total_ref.at[:, :, at], new_ref, gradient_ref, updated_ref, sems))
    finish(copies)


def write(slot, col, block, at, source, new_ref, gradient_ref, updated_ref, sems):
    fresh = col // LANES + slot == block
    one = pltpu.make_async_copy(source, gradient_ref.at[:, :, at], sems.at[2 * slot])
    two = pltpu.make_async_copy(new_ref.at[slot], updated_ref.at[:, :, at], sems.at[2 * slot + 1])

    @pl.when(fresh)
    def _():
        one.start()
        two.start()

    return fresh, one, two


def finish(copies):
    for fresh, one, two in copies:

        @pl.when(fresh)
        def _(one=one, two=two):
            one.wait()
            two.wait()


def add_windows(windows, main, object_ref, total_ref, weight_ref, updated_ref, gradient_ref, new_ref, sum_ref, sems):
    height, breadth = object_ref.shape[1:]
    lane = lax.broadcasted_iota(jnp.int32, (height, LANES), 1)
    level = lax.broadcasted_iota(jnp.int32, (height, LANES), 0)
    col = windows[main][0]
    copies = []
    for slot in range(3):
        block = jnp.minimum(col // LANES + slot, breadth // LANES - 1)
        at = pl.ds(pl.multiple_of(block * LANES, LANES), LANES)
        weight = weight_ref[:, at]
        sums = [total_ref[0, :, at], total_ref[1, :, at]]
        for start, begin, end, light_ref, change_ref in windows:
            inside = (level >= begin) & (level < end)
            live = change_ref[2 * height : 2 * height + 1, :1]
            light = covers(start, block, light_ref[:, :LANES], light_ref[:, LANES:], lane)
            weight = weight + jnp.where(inside, light, 0.0) * live
            for part in range(2):
                rows = slice(part * height, (part + 1) * height)
                change = covers(start, block, change_ref[rows, :LANES], change_ref[rows, LANES:], lane)
                sums[part] = sums[part] + jnp.where(inside, change, 0.0)
        scale = 1.0 / (weight + ALPHA)
        for part in range(2):
            sum_ref[slot, part] = sums[part]
            new_ref[slot, part] = object_ref[part, :, at] + sums[part] * scale
        copies.append(write(slot, col, block, at, sum_ref.at[slot], new_ref, gradient_ref, updated_ref, sems))
    finish(copies)


def first_kernel(
    others_ref, object_ref, total_ref, weight_ref, first_ref, received_ref, old_updated_ref, old_gradient_ref,
    updated_ref, gradient_ref, new_ref, sum_ref, sems,
):
    del old_updated_ref, old_gradient_ref
    windows = [(*(scalar_of(others_ref, index) for index in range(3)), first_ref, received_ref)]
    add_windows(windows, 0, object_ref, total_ref, weight_ref, updated_ref, gradient_ref, new_ref, sum_ref, sems)


def second_kernel(
    others_ref, object_ref, total_ref, weight_ref, first_ref, second_ref, received_ref, swapped_ref,
    old_updated_ref, old_gradient_ref, updated_ref, gradient_ref, new_ref, sum_ref, sems,
):
    del old_updated_ref, old_gradient_ref
    windows = [
        (*(scalar_of(others_ref, index) for index in range(3)), first_ref, received_ref),
        (*(scalar_of(others_ref, index) for index in range(3, 6)), second_ref, swapped_ref),
    ]
    add_windows(windows, 1, object_ref, total_ref, weight_ref, updated_ref, gradient_ref, new_ref, sum_ref, sems)


def call(kernel, out_shape, in_specs, out_specs, scratch=(), mebibytes=16, aliases=None):
    return pl.pallas_call(
        kernel,
        out_shape=out_shape,
        in_specs=in_specs,
        out_specs=out_specs,
        scratch_shapes=list(scratch),
        input_output_aliases=aliases or {},
        compiler_params=pltpu.CompilerParams(vmem_limit_bytes=mebibytes << 20),
        cost_estimate=pl.CostEstimate(flops=5000000, bytes_accessed=5000000, transcendentals=0),
    )


def space(where):
    return pl.BlockSpec(memory_space=where)


def shape(*dims, dtype=jnp.float32):
    return jax.ShapeDtypeStruct(dims, dtype)


def solution(mesh):
    tiles, cores = mesh.shape["tile"], mesh.shape["mode"]
    up = [(2 * t, 2 * (t + 1)) for t in range(tiles - 1)] + [(2 * t + 1, 2 * (t + 2) + 1) for t in range(tiles - 2)]
    gather = [(2 * t, 2 * (t ^ 1)) for t in range(tiles)]
    gather += [(2 * t + 1, 2 * (t - 2) + 1) for t in range(2, tiles, 2)]
    gather += [(2 * t + 1, 2 * (t + 2) + 1) for t in range(1, tiles - 2, 2)]
    spread = [(target, source) for source, target in gather]
    onward = [(2 * t, 2 * (t + 2)) for t in range(1, tiles - 2, 2)]
    swap = [(2 * t + core, 2 * t + 1 - core) for t in range(tiles) for core in range(2)]
    assert cores == 2 and tiles % 2 == 0

    def move(value, pairs):
        return lax.ppermute(value, AXES, pairs)

    def step(object_tiles, probe_modes, amplitudes, scan_offsets, slot_scan, slot_count):
        height, breadth = object_tiles.shape[1:]
        modes, _, frame, _ = probe_modes.shape
        assert slot_scan.shape[0] == 1 and frame == 2 * height and height == LANES
        table = scan_offsets.T
        matrix = jnp.asarray(matrices(frame))
        received_scan = move(slot_scan, up)
        other_probe = move(probe_modes, swap)
        received_amplitude = move(amplitudes, onward)
        scalar = pltpu.SMEM((1,), jnp.int32)
        staged, table = call(
            stage_kernel,
            (shape(*object_tiles.shape), shape(*table.shape, dtype=jnp.int32)),
            [space(pltpu.HBM)] * 2,
            [space(VMEM)] * 2,
            [pltpu.SemaphoreType.DMA((2,))],
            mebibytes=8,
        )(pltpu.with_memory_space_constraint(object_tiles, pltpu.HBM), pltpu.with_memory_space_constraint(table, pltpu.HBM))
        window = call(
            select_kernel, shape(2, height, frame), [space(SMEM)] * 2 + [space(VMEM)] * 2, space(VMEM)
        )(slot_scan, received_scan, table, staged)
        received = move(window, gather)
        swapped_scan = move(received_scan, swap)
        swapped_amplitude = move(received_amplitude, swap)
        scalar = pltpu.SMEM((1,), jnp.int32)
        strip = shape(2 * modes, 2, height, frame)
        whole = shape(2, height, breadth)
        gradient, probe, own_window, light, plain, own_strip, place = call(
            prepare_kernel,
            (
                whole,
                shape(2 * modes, 2, frame, frame),
                shape(2, height, frame),
                shape(frame, frame),
                shape(frame, frame),
                strip,
                shape(8, LANES),
            ),
            [space(pl.ANY)] * 3 + [space(VMEM)] * 5,
            [space(pl.ANY)] + [space(VMEM)] * 6,
            [
                pltpu.VMEM((height // 8, breadth), jnp.float32),
                pltpu.VMEM((2 * modes, 2, frame // LANES, frame + height, LANES), jnp.float32),
                scalar,
                scalar,
                scalar,
                pltpu.SemaphoreType.DMA((19,)),
            ],
        )(slot_scan, received_scan, swapped_scan, table, staged, probe_modes, other_probe, matrix)
        swapped = move(received, swap)
        amplitude = call(
            reorder_kernel,
            shape(frame, frame),
            [space(VMEM)] * 3,
            space(VMEM),
            [pltpu.VMEM((frame // LANES, frame, LANES), jnp.float32)],
        )(amplitudes, received_amplitude, swapped_amplitude)
        first_strip = call(strip_kernel, strip, [space(VMEM)] * 3, space(VMEM))(received, probe, matrix)
        send, keep = call(
            wave_kernel,
            (shape(2 * height + 8, frame), shape(2, height, frame)),
            [space(VMEM)] * 10,
            [space(VMEM)] * 2,
            [
                pltpu.VMEM((2, frame, frame), jnp.float32),
                pltpu.VMEM((2 * modes, 2, frame, frame), jnp.float32),
                pltpu.VMEM((2 * modes, 2, height, frame), jnp.float32),
            ],
            mebibytes=24,
        )(place, own_window, received, swapped, own_strip, first_strip, probe, amplitude, light, matrix)
        received_change = move(send, spread)
        blocks = pltpu.VMEM((3, 2, height, LANES), jnp.float32)
        semaphores = pltpu.SemaphoreType.DMA((6,))
        updated, gradient, total, weight, first, second, others = call(
            base_kernel,
            (
                whole,
                whole,
                whole,
                shape(height, breadth),
                shape(height, frame),
                shape(height, frame),
                shape(8, LANES),
            ),
            [space(VMEM)] + [space(pl.ANY)] * 3 + [space(VMEM)] * 5 + [space(pl.ANY)],
            [space(pl.ANY)] * 2 + [space(VMEM)] * 5,
            [
                blocks,
                pltpu.VMEM((2, frame // LANES, frame + height, LANES), jnp.float32),
                pltpu.VMEM((2, frame, frame), jnp.float32),
                scalar,
                scalar,
                scalar,
                semaphores,
                pltpu.SemaphoreType.DMA((4,)),
            ],
            aliases={9: 1},
        )(place, slot_scan, received_scan, swapped_scan, table, staged, keep, light, plain, gradient)
        swapped_change = move(received_change, swap)
        updated, gradient = call(
            first_kernel,
            (whole, whole),
            [space(VMEM)] * 6 + [space(pl.ANY)] * 2,
            [space(pl.ANY)] * 2,
            [blocks, blocks, semaphores],
            aliases={6: 0, 7: 1},
        )(others, staged, total, weight, first, received_change, updated, gradient)
        return call(
            second_kernel,
            (whole, whole),
            [space(VMEM)] * 8 + [space(pl.ANY)] * 2,
            [space(pl.ANY)] * 2,
            [blocks, blocks, semaphores],
            aliases={8: 0, 9: 1},
        )(others, staged, total, weight, first, second, received_change, swapped_change, updated, gradient)

    return jax.shard_map(
        step,
        mesh=mesh,
        in_specs=(
            P(None, "tile", None),
            P("mode", None, None, None),
            P("tile", None, None),
            P(),
            P("tile"),
            P("tile"),
        ),
        out_specs=(P(None, "tile", None), P(None, "tile", None)),
        check_vma=False,
    )
```

```python
import math

import jax
import jax.numpy as jnp
import numpy as np
from jax import lax
from jax.experimental import pallas as pl
from jax.experimental.pallas import tpu as pltpu
from jax.sharding import PartitionSpec as P


FLOOR = 0.25
ALPHA = 0.5
LANES = 128
AXES = ("tile", "mode")
VMEM = pltpu.VMEM


def split(value):
    high = value.astype(jnp.bfloat16)
    low = (value - high.astype(jnp.float32)).astype(jnp.bfloat16)
    return high, low


def matrices(frame):
    half = frame // 2
    pixel = np.arange(half)[:, None]
    wave = np.arange(half)[None, :]
    blocks = []
    for parity in (0, 1):
        phase = 2.0 * math.pi * (pixel * (2 * wave + parity) % frame) / frame
        cos, sin = np.cos(phase) / math.sqrt(frame), np.sin(phase) / math.sqrt(frame)
        forward = np.block([[cos, -sin], [sin, cos]])
        for table in (forward, forward.T):
            high = table.astype(jnp.bfloat16)
            blocks.append(high)
            blocks.append((table - high.astype(np.float64)).astype(jnp.bfloat16))
    return np.stack(blocks)


def lookup(table_ref, scan):
    base = pl.multiple_of((scan // LANES) * LANES, LANES)
    chunk = table_ref[:, pl.ds(base, LANES)].astype(jnp.float32)
    lane = lax.broadcasted_iota(jnp.int32, chunk.shape, 1)
    picked = jnp.where(lane == scan - base, chunk, 0.0)
    row = jnp.sum(picked[0:1]).astype(jnp.int32)
    col = jnp.sum(picked[1:2]).astype(jnp.int32)
    return row, col


def strip_window(object_ref, col):
    blocks = object_ref.shape[2] // LANES
    block, shift = col // LANES, col % LANES
    first = object_ref[:, :, pl.ds(pl.multiple_of(block * LANES, LANES), LANES)]
    second = object_ref[:, :, pl.ds(pl.multiple_of((block + 1) * LANES, LANES), LANES)]
    last = jnp.minimum(block + 2, blocks - 1)
    third = object_ref[:, :, pl.ds(pl.multiple_of(last * LANES, LANES), LANES)]
    lane = lax.broadcasted_iota(jnp.int32, first.shape, 2)
    return jnp.where(lane < shift, third, first), second


def stage_kernel(object_ref, table_ref, staged_ref, held_ref, sems):
    first = pltpu.make_async_copy(object_ref, staged_ref, sems.at[0])
    second = pltpu.make_async_copy(table_ref, held_ref, sems.at[1])
    first.start()
    second.start()
    first.wait()
    second.wait()


def fetch(pairs, sems, first=0):
    copies = [pltpu.make_async_copy(a, b, sems.at[first + index]) for index, (a, b) in enumerate(pairs)]
    for copy in copies:
        copy.start()
    return copies


def scan_of(ref):
    return jnp.max(ref[...].astype(jnp.float32)).astype(jnp.int32)


def select_kernel(own_scan_ref, scan_ref, table_ref, object_ref, out_ref):
    odd = lax.axis_index("tile") % 2 == 1
    scan = jnp.where(odd & (lax.axis_index("mode") == 1), scan_of(own_scan_ref), scan_of(scan_ref))
    _, col = lookup(table_ref, scan)
    low, high = strip_window(object_ref, col)
    out_ref[:, :, :LANES] = low
    out_ref[:, :, LANES:] = high


def slots(own_ref, received_ref, swapped_ref):
    first = lax.axis_index("mode") == 0
    odd = lax.axis_index("tile") % 2 == 1
    own, got, other = scan_of(own_ref), scan_of(received_ref), scan_of(swapped_ref)
    above = jnp.where(first, got, other)
    further = jnp.where(first, other, got)
    return jnp.where(odd, further, own), above, jnp.where(odd, own, further)


def keep_scalars(out_ref, values):
    for index, value in enumerate(values):
        row = jnp.full((1, out_ref.shape[1]), value, jnp.int32)
        out_ref[index : index + 1] = row.astype(jnp.float32)


def scalar_of(ref, index):
    return jnp.max(ref[index : index + 1]).astype(jnp.int32)


def within(table_ref, scan, strip, height):
    row, col = lookup(table_ref, scan)
    return jnp.clip(row - strip * height, 0, height - 1), col


def roll_into(out_ref, value, row, col, tall_ref):
    frame = value.shape[0]
    half = frame // 2
    turned = pltpu.roll(value, col, 1)
    for index in range(frame // LANES):
        at = slice(index * LANES, (index + 1) * LANES)
        tall_ref[index, :half] = turned[half:, at]
        tall_ref[index, half:] = turned[:, at]
        out_ref[:, at] = tall_ref[index, pl.ds(half - row, frame), :]


def reorder_kernel(own_ref, received_ref, swapped_ref, factor_ref, rows_ref):
    frame = own_ref.shape[1]
    odd = lax.axis_index("tile") % 2 == 1
    moved = jnp.where(lax.axis_index("mode") == 0, received_ref[0], swapped_ref[0])
    value = jnp.where(odd, moved, own_ref[0])
    source = lax.broadcasted_iota(jnp.int32, (frame, frame), 0)
    target = lax.broadcasted_iota(jnp.int32, (frame, frame), 1)
    half = frame // 2
    order = jnp.where(target < half, 2 * target, 2 * target - frame + 1)
    pick = jnp.where(source == order, 1.0, 0.0).astype(jnp.bfloat16)
    high = value.astype(jnp.bfloat16)
    rest = value - high.astype(jnp.float32)
    middle = rest.astype(jnp.bfloat16)
    low = (rest - middle.astype(jnp.float32)).astype(jnp.bfloat16)
    columns = jnp.dot(high, pick, preferred_element_type=jnp.float32)
    columns = columns + jnp.dot(middle, pick, preferred_element_type=jnp.float32)
    columns = columns + jnp.dot(low, pick, preferred_element_type=jnp.float32)
    for index in range(frame // LANES):
        at = slice(index * LANES, (index + 1) * LANES)
        rows_ref[index] = columns[:, at]
        factor_ref[:half, at] = rows_ref[index, pl.ds(0, half, stride=2), :]
        factor_ref[half:, at] = rows_ref[index, pl.ds(1, half, stride=2), :]


def prepare_kernel(
    scan_ref, received_ref, swapped_ref, table_ref, object_ref, own_probe_ref, other_probe_ref, matrix_ref,
    gradient_ref, probe_ref, window_ref, light_ref, total_ref, strip_ref, place_ref,
    zero_ref, tall_ref, sems,
):
    zero_ref[...] = jnp.zeros_like(zero_ref)
    step = zero_ref.shape[0]
    copies = []
    for part in range(2):
        for at in range(0, object_ref.shape[1], step):
            copies += fetch([(zero_ref, gradient_ref.at[part, at : at + step])], sems, len(copies))
    modes = own_probe_ref.shape[0]
    sources = [ref.at[mode, part] for ref in (own_probe_ref, other_probe_ref) for mode in range(modes) for part in range(2)]
    total = sources[0][...] * sources[0][...]
    for source in sources[1:]:
        total = total + source[...] * source[...]
    total_ref[...] = total
    height = object_ref.shape[1]
    tile = lax.axis_index("tile")
    odd = tile % 2
    scan, _, _ = slots(scan_ref, received_ref, swapped_ref)
    row, col = within(table_ref, scan, tile - 2 * odd, height)
    shift = col % LANES
    for index, source in enumerate(sources):
        mode, part = divmod(index, 2)
        roll_into(probe_ref.at[mode, part], source[...], row, shift, tall_ref.at[mode, part])
    roll_into(light_ref, total_ref[...], row, shift, tall_ref.at[0, 0])
    low, high = strip_window(object_ref, col)
    window_ref[:, :, :LANES] = low
    window_ref[:, :, LANES:] = high
    live = jnp.where(odd == 1, (tile >= 2).astype(jnp.int32), 1)
    keep_scalars(place_ref, (jnp.where(odd == 1, 0, row), jnp.where(odd == 1, row, height), live))
    transform_rows(probe_ref, 0, window_ref, matrix_ref, strip_ref)
    for copy in copies:
        copy.wait()


def right(value, high, low):
    first, second = split(value)
    return jnp.dot(
        jnp.concatenate([first, second, first], axis=1),
        jnp.concatenate([high, high, low], axis=0),
        preferred_element_type=jnp.float32,
    )


def left(high, low, value):
    first, second = split(value)
    return jnp.dot(
        jnp.concatenate([high, high, low], axis=1),
        jnp.concatenate([first, second, first], axis=0),
        preferred_element_type=jnp.float32,
    )


def transform_rows(probe_ref, start, window_ref, matrix_ref, out_ref):
    modes = probe_ref.shape[0]
    height, frame = window_ref.shape[1:]
    half = frame // 2
    sums, differences = [], []
    for mode in range(modes):
        probe_re = probe_ref[mode, 0, pl.ds(start, height), :]
        probe_im = probe_ref[mode, 1, pl.ds(start, height), :]
        wave_re = probe_re * window_ref[0] - probe_im * window_ref[1]
        wave_im = probe_re * window_ref[1] + probe_im * window_ref[0]
        for pieces, sign in ((sums, 1.0), (differences, -1.0)):
            pieces.append(
                jnp.concatenate(
                    [wave_re[:, :half] + sign * wave_re[:, half:], wave_im[:, :half] + sign * wave_im[:, half:]],
                    axis=1,
                )
            )
    even = right(jnp.concatenate(sums, axis=0), matrix_ref[0], matrix_ref[1])
    odd = right(jnp.concatenate(differences, axis=0), matrix_ref[4], matrix_ref[5])
    for mode in range(modes):
        at = slice(mode * height, (mode + 1) * height)
        out_ref[mode, 0] = jnp.concatenate([even[at, :half], odd[at, :half]], axis=1)
        out_ref[mode, 1] = jnp.concatenate([even[at, half:], odd[at, half:]], axis=1)


def strip_kernel(received_ref, probe_ref, matrix_ref, out_ref):
    height = received_ref.shape[1]
    start = pl.multiple_of((1 - lax.axis_index("mode")) * height, height)
    transform_rows(probe_ref, start, received_ref, matrix_ref, out_ref)


def wave_kernel(
    place_ref, window_ref, received_ref, swapped_ref, own_ref, first_ref, probe_ref, amplitude_ref, light_ref,
    matrix_ref, send_ref, keep_ref, patch_ref, far_ref, second_ref,
):
    modes, _, frame, _ = probe_ref.shape
    height = window_ref.shape[1]
    half = frame // 2
    core = lax.axis_index("mode")
    low, high = place_ref[0:1, :1].astype(jnp.int32), place_ref[1:2, :1].astype(jnp.int32)
    transform_rows(probe_ref, pl.multiple_of(core * height, height), swapped_ref, matrix_ref, second_ref)
    level = lax.broadcasted_iota(jnp.int32, (height, frame), 0)

    def assemble(own, got, given):
        nearer = jnp.where(core == 0, got, given)
        farther = jnp.where(core == 0, given, got)
        return jnp.where((level >= low) & (level < high), own, farther), nearer

    for part in range(2):
        top, bottom = assemble(window_ref[part], received_ref[part], swapped_ref[part])
        patch_ref[part, :height] = top
        patch_ref[part, height:] = bottom
    intensity = jnp.zeros((frame, frame), jnp.float32)
    for mode in range(modes):
        top_re, bottom_re = assemble(own_ref[mode, 0], first_ref[mode, 0], second_ref[mode, 0])
        top_im, bottom_im = assemble(own_ref[mode, 1], first_ref[mode, 1], second_ref[mode, 1])
        added = jnp.concatenate([top_re + bottom_re, top_im + bottom_im], axis=0)
        taken = jnp.concatenate([top_re - bottom_re, top_im - bottom_im], axis=0)
        even = left(matrix_ref[2], matrix_ref[3], added)
        odd = left(matrix_ref[6], matrix_ref[7], taken)
        far_ref[mode, 0] = even
        far_ref[mode, 1] = odd
        squares = jnp.concatenate(
            [even[:half] * even[:half] + even[half:] * even[half:], odd[:half] * odd[:half] + odd[half:] * odd[half:]],
            axis=0,
        )
        intensity = intensity + squares
    factor = amplitude_ref[...] * lax.rsqrt(jnp.maximum(intensity, FLOOR))
    grad_re = jnp.zeros((frame, frame), jnp.float32)
    grad_im = jnp.zeros((frame, frame), jnp.float32)
    even_factor = jnp.concatenate([factor[:half], factor[:half]], axis=0)
    odd_factor = jnp.concatenate([factor[half:], factor[half:]], axis=0)
    evens, odds = [], []
    for mode in range(modes):
        even = left(matrix_ref[0], matrix_ref[1], far_ref[mode, 0] * even_factor)
        odd = left(matrix_ref[4], matrix_ref[5], far_ref[mode, 1] * odd_factor)
        top, bottom = even + odd, even - odd
        mid_re = jnp.concatenate([top[:half], bottom[:half]], axis=0)
        mid_im = jnp.concatenate([top[half:], bottom[half:]], axis=0)
        evens.append(jnp.concatenate([mid_re[:, :half], mid_im[:, :half]], axis=1))
        odds.append(jnp.concatenate([mid_re[:, half:], mid_im[:, half:]], axis=1))
    even = right(jnp.concatenate(evens, axis=0), matrix_ref[2], matrix_ref[3])
    odd = right(jnp.concatenate(odds, axis=0), matrix_ref[6], matrix_ref[7])
    fores, afts = even + odd, even - odd
    for mode in range(modes):
        fore = fores[mode * frame : (mode + 1) * frame]
        aft = afts[mode * frame : (mode + 1) * frame]
        back_re = jnp.concatenate([fore[:, :half], aft[:, :half]], axis=1)
        back_im = jnp.concatenate([fore[:, half:], aft[:, half:]], axis=1)
        probe_re, probe_im = probe_ref[mode, 0], probe_ref[mode, 1]
        grad_re = grad_re + (probe_re * back_re + probe_im * back_im)
        grad_im = grad_im + (probe_re * back_im - probe_im * back_re)
    live = place_ref[2:3, :1]
    grad_re = (grad_re - light_ref[...] * patch_ref[0]) * live
    grad_im = (grad_im - light_ref[...] * patch_ref[1]) * live
    send_ref[:height] = jnp.where(core == 0, grad_re[height:], grad_re[:height])
    send_ref[height : 2 * height] = jnp.where(core == 0, grad_im[height:], grad_im[:height])
    send_ref[2 * height :] = jnp.broadcast_to(live, (8, frame))
    keep_ref[0] = grad_re[:height]
    keep_ref[1] = grad_im[:height]


def covers(col, block, low, high, lane):
    start, shift = col // LANES, col % LANES
    distance = block - start
    value = jnp.where(distance == 1, high, low)
    first = jnp.where(distance == 0, shift, jnp.where(distance == 1, 0, LANES))
    last = jnp.where(distance == 2, shift, 0)
    keep = (lane >= first) | (lane < last)
    return jnp.where(keep, value, 0.0)


def base_kernel(
    place_ref, scan_ref, received_ref, swapped_ref, table_ref, object_ref, keep_ref, light_ref, plain_ref,
    old_gradient_ref,
    updated_ref, gradient_ref, total_ref, weight_ref, first_ref, second_ref, others_ref, new_ref, tall_ref, turned_ref, sems, fills,
):
    del old_gradient_ref
    height, breadth = object_ref.shape[1:]
    tile = lax.axis_index("tile")
    core = lax.axis_index("mode")
    fill = pltpu.make_async_copy(object_ref, updated_ref, fills.at[0])
    fill.start()
    total_ref[...] = jnp.zeros_like(total_ref)
    weight_ref[...] = jnp.zeros_like(weight_ref)
    odd = tile % 2
    main, above, third = slots(scan_ref, received_ref, swapped_ref)
    _, col = within(table_ref, main, tile, height)
    live = place_ref[2:3, :1]
    start, stop = place_ref[0:1, :1].astype(jnp.int32), place_ref[1:2, :1].astype(jnp.int32)
    lane = lax.broadcasted_iota(jnp.int32, (height, LANES), 1)
    level = lax.broadcasted_iota(jnp.int32, (height, LANES), 0)
    kept = (level >= start) & (level < stop)
    for slot in range(3):
        block = jnp.minimum(col // LANES + slot, breadth // LANES - 1)
        at = pl.ds(pl.multiple_of(block * LANES, LANES), LANES)
        light = covers(col, block, light_ref[:height, :LANES], light_ref[:height, LANES:], lane)
        weight = jnp.where(kept, light * live, 0.0)
        weight_ref[:, at] = weight
        scale = 1.0 / (weight + ALPHA)
        for part in range(2):
            change = covers(col, block, keep_ref[part, :, :LANES], keep_ref[part, :, LANES:], lane)
            change = jnp.where(kept, change, 0.0)
            total_ref[part, :, at] = change
            new_ref[slot, part] = object_ref[part, :, at] + change * scale
    places = []
    for scan, strip, far in ((above, tile - 1, False), (third, tile - 2 + 2 * odd, True)):
        row, start = within(table_ref, scan, strip, height)
        index = int(far)
        roll_into(turned_ref.at[index], plain_ref[...], row, start % LANES, tall_ref.at[index])
        turned = turned_ref[index]
        begin = jnp.where(odd == 1, row, 0) if far else 0
        end = jnp.where(odd == 1, height, row) if far else height
        places.append((start, begin, end, turned[:height] if far else turned[height:]))
    chosen = []
    for slot, out_ref in ((0, first_ref), (1, second_ref)):
        direct = core == slot
        near, far = places
        out_ref[...] = jnp.where(direct, near[3], far[3])
        chosen += [jnp.where(direct, near[index], far[index]) for index in range(3)]
    keep_scalars(others_ref, chosen)
    fill.wait()
    copies = []
    for slot in range(3):
        block = jnp.minimum(col // LANES + slot, breadth // LANES - 1)
        at = pl.ds(pl.multiple_of(block * LANES, LANES), LANES)
        copies.append(write(slot, col, block, at, total_ref.at[:, :, at], new_ref, gradient_ref, updated_ref, sems))
    finish(copies)


def write(slot, col, block, at, source, new_ref, gradient_ref, updated_ref, sems):
    fresh = col // LANES + slot == block
    one = pltpu.make_async_copy(source, gradient_ref.at[:, :, at], sems.at[2 * slot])
    two = pltpu.make_async_copy(new_ref.at[slot], updated_ref.at[:, :, at], sems.at[2 * slot + 1])

    @pl.when(fresh)
    def _():
        one.start()
        two.start()

    return fresh, one, two


def finish(copies):
    for fresh, one, two in copies:

        @pl.when(fresh)
        def _(one=one, two=two):
            one.wait()
            two.wait()


def add_windows(windows, main, object_ref, total_ref, weight_ref, updated_ref, gradient_ref, new_ref, sum_ref, sems):
    height, breadth = object_ref.shape[1:]
    lane = lax.broadcasted_iota(jnp.int32, (height, LANES), 1)
    level = lax.broadcasted_iota(jnp.int32, (height, LANES), 0)
    col = windows[main][0]
    copies = []
    for slot in range(3):
        block = jnp.minimum(col // LANES + slot, breadth // LANES - 1)
        at = pl.ds(pl.multiple_of(block * LANES, LANES), LANES)
        weight = weight_ref[:, at]
        sums = [total_ref[0, :, at], total_ref[1, :, at]]
        for start, begin, end, light_ref, change_ref in windows:
            inside = (level >= begin) & (level < end)
            live = change_ref[2 * height : 2 * height + 1, :1]
            light = covers(start, block, light_ref[:, :LANES], light_ref[:, LANES:], lane)
            weight = weight + jnp.where(inside, light, 0.0) * live
            for part in range(2):
                rows = slice(part * height, (part + 1) * height)
                change = covers(start, block, change_ref[rows, :LANES], change_ref[rows, LANES:], lane)
                sums[part] = sums[part] + jnp.where(inside, change, 0.0)
        scale = 1.0 / (weight + ALPHA)
        for part in range(2):
            sum_ref[slot, part] = sums[part]
            new_ref[slot, part] = object_ref[part, :, at] + sums[part] * scale
        copies.append(write(slot, col, block, at, sum_ref.at[slot], new_ref, gradient_ref, updated_ref, sems))
    finish(copies)


def first_kernel(
    others_ref, object_ref, total_ref, weight_ref, first_ref, received_ref, old_updated_ref, old_gradient_ref,
    updated_ref, gradient_ref, new_ref, sum_ref, sems,
):
    del old_updated_ref, old_gradient_ref
    windows = [(*(scalar_of(others_ref, index) for index in range(3)), first_ref, received_ref)]
    add_windows(windows, 0, object_ref, total_ref, weight_ref, updated_ref, gradient_ref, new_ref, sum_ref, sems)


def second_kernel(
    others_ref, object_ref, total_ref, weight_ref, first_ref, second_ref, received_ref, swapped_ref,
    old_updated_ref, old_gradient_ref, updated_ref, gradient_ref, new_ref, sum_ref, sems,
):
    del old_updated_ref, old_gradient_ref
    windows = [
        (*(scalar_of(others_ref, index) for index in range(3)), first_ref, received_ref),
        (*(scalar_of(others_ref, index) for index in range(3, 6)), second_ref, swapped_ref),
    ]
    add_windows(windows, 1, object_ref, total_ref, weight_ref, updated_ref, gradient_ref, new_ref, sum_ref, sems)


def call(kernel, out_shape, in_specs, out_specs, scratch=(), mebibytes=16, aliases=None):
    return pl.pallas_call(
        kernel,
        out_shape=out_shape,
        in_specs=in_specs,
        out_specs=out_specs,
        scratch_shapes=list(scratch),
        input_output_aliases=aliases or {},
        compiler_params=pltpu.CompilerParams(vmem_limit_bytes=mebibytes << 20),
        cost_estimate=pl.CostEstimate(flops=5000000, bytes_accessed=5000000, transcendentals=0),
    )


def space(where):
    return pl.BlockSpec(memory_space=where)


def shape(*dims, dtype=jnp.float32):
    return jax.ShapeDtypeStruct(dims, dtype)


def solution(mesh):
    tiles, cores = mesh.shape["tile"], mesh.shape["mode"]
    up = [(2 * t, 2 * (t + 1)) for t in range(tiles - 1)] + [(2 * t + 1, 2 * (t + 2) + 1) for t in range(tiles - 2)]
    gather = [(2 * t, 2 * (t ^ 1)) for t in range(tiles)]
    gather += [(2 * t + 1, 2 * (t - 2) + 1) for t in range(2, tiles, 2)]
    gather += [(2 * t + 1, 2 * (t + 2) + 1) for t in range(1, tiles - 2, 2)]
    spread = [(target, source) for source, target in gather]
    onward = [(2 * t, 2 * (t + 2)) for t in range(1, tiles - 2, 2)]
    swap = [(2 * t + core, 2 * t + 1 - core) for t in range(tiles) for core in range(2)]
    assert cores == 2 and tiles % 2 == 0

    def move(value, pairs):
        return lax.ppermute(value, AXES, pairs)

    def step(object_tiles, probe_modes, amplitudes, scan_offsets, slot_scan, slot_count):
        height, breadth = object_tiles.shape[1:]
        modes, _, frame, _ = probe_modes.shape
        assert slot_scan.shape == (1,) and frame == 2 * height and height == LANES
        table = scan_offsets.T
        matrix = jnp.asarray(matrices(frame))
        slot_scan = slot_scan.reshape(1, 1)
        received_scan = move(slot_scan, up)
        other_probe = move(probe_modes, swap)
        received_amplitude = move(amplitudes, onward)
        staged, table = call(
            stage_kernel,
            (shape(*object_tiles.shape), shape(*table.shape, dtype=jnp.int32)),
            [space(pltpu.HBM)] * 2,
            [space(VMEM)] * 2,
            [pltpu.SemaphoreType.DMA((2,))],
            mebibytes=8,
        )(pltpu.with_memory_space_constraint(object_tiles, pltpu.HBM), pltpu.with_memory_space_constraint(table, pltpu.HBM))
        window = call(
            select_kernel, shape(2, height, frame), [space(VMEM)] * 4, space(VMEM)
        )(slot_scan, received_scan, table, staged)
        received = move(window, gather)
        swapped_scan = move(received_scan, swap)
        swapped_amplitude = move(received_amplitude, swap)
        strip = shape(2 * modes, 2, height, frame)
        whole = shape(2, height, breadth)
        gradient, probe, own_window, light, plain, own_strip, place = call(
            prepare_kernel,
            (
                whole,
                shape(2 * modes, 2, frame, frame),
                shape(2, height, frame),
                shape(frame, frame),
                shape(frame, frame),
                strip,
                shape(8, LANES),
            ),
            [space(VMEM)] * 8,
            [space(pl.ANY)] + [space(VMEM)] * 6,
            [
                pltpu.VMEM((height // 8, breadth), jnp.float32),
                pltpu.VMEM((2 * modes, 2, frame // LANES, frame + height, LANES), jnp.float32),
                pltpu.SemaphoreType.DMA((16,)),
            ],
        )(slot_scan, received_scan, swapped_scan, table, staged, probe_modes, other_probe, matrix)
        swapped = move(received, swap)
        amplitude = call(
            reorder_kernel,
            shape(frame, frame),
            [space(VMEM)] * 3,
            space(VMEM),
            [pltpu.VMEM((frame // LANES, frame, LANES), jnp.float32)],
        )(amplitudes, received_amplitude, swapped_amplitude)
        first_strip = call(strip_kernel, strip, [space(VMEM)] * 3, space(VMEM))(received, probe, matrix)
        send, keep = call(
            wave_kernel,
            (shape(2 * height + 8, frame), shape(2, height, frame)),
            [space(VMEM)] * 10,
            [space(VMEM)] * 2,
            [
                pltpu.VMEM((2, frame, frame), jnp.float32),
                pltpu.VMEM((2 * modes, 2, frame, frame), jnp.float32),
                pltpu.VMEM((2 * modes, 2, height, frame), jnp.float32),
            ],
            mebibytes=24,
        )(place, own_window, received, swapped, own_strip, first_strip, probe, amplitude, light, matrix)
        received_change = move(send, spread)
        blocks = pltpu.VMEM((3, 2, height, LANES), jnp.float32)
        semaphores = pltpu.SemaphoreType.DMA((6,))
        updated, gradient, total, weight, first, second, others = call(
            base_kernel,
            (
                whole,
                whole,
                whole,
                shape(height, breadth),
                shape(height, frame),
                shape(height, frame),
                shape(8, LANES),
            ),
            [space(VMEM)] * 9 + [space(pl.ANY)],
            [space(pl.ANY)] * 2 + [space(VMEM)] * 5,
            [
                blocks,
                pltpu.VMEM((2, frame // LANES, frame + height, LANES), jnp.float32),
                pltpu.VMEM((2, frame, frame), jnp.float32),
                semaphores,
                pltpu.SemaphoreType.DMA((1,)),
            ],
            aliases={9: 1},
        )(place, slot_scan, received_scan, swapped_scan, table, staged, keep, light, plain, gradient)
        swapped_change = move(received_change, swap)
        updated, gradient = call(
            first_kernel,
            (whole, whole),
            [space(VMEM)] * 6 + [space(pl.ANY)] * 2,
            [space(pl.ANY)] * 2,
            [blocks, blocks, semaphores],
            aliases={6: 0, 7: 1},
        )(others, staged, total, weight, first, received_change, updated, gradient)
        return call(
            second_kernel,
            (whole, whole),
            [space(VMEM)] * 8 + [space(pl.ANY)] * 2,
            [space(pl.ANY)] * 2,
            [blocks, blocks, semaphores],
            aliases={8: 0, 9: 1},
        )(others, staged, total, weight, first, second, received_change, swapped_change, updated, gradient)

    return jax.shard_map(
        step,
        mesh=mesh,
        in_specs=(
            P(None, "tile", None),
            P("mode", None, None, None),
            P("tile", None, None),
            P(),
            P("tile"),
            P("tile"),
        ),
        out_specs=(P(None, "tile", None), P(None, "tile", None)),
        check_vma=False,
    )
```

```python
import math

import jax
import jax.numpy as jnp
import numpy as np
from jax import lax
from jax.experimental import pallas as pl
from jax.experimental.pallas import tpu as pltpu
from jax.sharding import PartitionSpec as P


FLOOR = 0.25
ALPHA = 0.5
LANES = 128
AXES = ("tile", "mode")
VMEM = pltpu.VMEM
SMEM = pltpu.SMEM


def split(value):
    high = value.astype(jnp.bfloat16)
    low = (value - high.astype(jnp.float32)).astype(jnp.bfloat16)
    return high, low


def matrices(frame):
    half = frame // 2
    pixel = np.arange(half)[:, None]
    wave = np.arange(half)[None, :]
    blocks = []
    for parity in (0, 1):
        phase = 2.0 * math.pi * (pixel * (2 * wave + parity) % frame) / frame
        cos, sin = np.cos(phase) / math.sqrt(frame), np.sin(phase) / math.sqrt(frame)
        forward = np.block([[cos, -sin], [sin, cos]])
        for table in (forward, forward.T):
            high = table.astype(jnp.bfloat16)
            blocks.append(high)
            blocks.append((table - high.astype(np.float64)).astype(jnp.bfloat16))
    return np.stack(blocks)


def lookup(table_ref, scan):
    base = pl.multiple_of((scan // LANES) * LANES, LANES)
    chunk = table_ref[:, pl.ds(base, LANES)].astype(jnp.float32)
    lane = lax.broadcasted_iota(jnp.int32, chunk.shape, 1)
    picked = jnp.where(lane == scan - base, chunk, 0.0)
    row = jnp.sum(picked[0:1]).astype(jnp.int32)
    col = jnp.sum(picked[1:2]).astype(jnp.int32)
    return row, col


def strip_window(object_ref, col):
    blocks = object_ref.shape[2] // LANES
    block, shift = col // LANES, col % LANES
    first = object_ref[:, :, pl.ds(pl.multiple_of(block * LANES, LANES), LANES)]
    second = object_ref[:, :, pl.ds(pl.multiple_of((block + 1) * LANES, LANES), LANES)]
    last = jnp.minimum(block + 2, blocks - 1)
    third = object_ref[:, :, pl.ds(pl.multiple_of(last * LANES, LANES), LANES)]
    lane = lax.broadcasted_iota(jnp.int32, first.shape, 2)
    return jnp.where(lane < shift, third, first), second


def stage_kernel(object_ref, table_ref, staged_ref, held_ref, sems):
    first = pltpu.make_async_copy(object_ref, staged_ref, sems.at[0])
    second = pltpu.make_async_copy(table_ref, held_ref, sems.at[1])
    first.start()
    second.start()
    first.wait()
    second.wait()


def fetch(pairs, sems, first=0):
    copies = [pltpu.make_async_copy(a, b, sems.at[first + index]) for index, (a, b) in enumerate(pairs)]
    for copy in copies:
        copy.start()
    return copies


def select_kernel(own_scan_ref, scan_ref, table_ref, object_ref, out_ref):
    odd = lax.axis_index("tile") % 2 == 1
    scan = jnp.where(odd & (lax.axis_index("mode") == 1), own_scan_ref[0], scan_ref[0])
    _, col = lookup(table_ref, scan)
    low, high = strip_window(object_ref, col)
    out_ref[:, :, :LANES] = low
    out_ref[:, :, LANES:] = high


def slots(own_ref, received_ref, swapped_ref):
    first = lax.axis_index("mode") == 0
    odd = lax.axis_index("tile") % 2 == 1
    own, got, other = own_ref[0], received_ref[0], swapped_ref[0]
    above = jnp.where(first, got, other)
    further = jnp.where(first, other, got)
    return jnp.where(odd, further, own), above, jnp.where(odd, own, further)


def keep_scalars(out_ref, values):
    for index, value in enumerate(values):
        row = jnp.full((1, out_ref.shape[1]), value, jnp.int32)
        out_ref[index : index + 1] = row.astype(jnp.float32)


def scalar_of(ref, index):
    return jnp.max(ref[index : index + 1]).astype(jnp.int32)


def within(table_ref, scan, strip, height):
    row, col = lookup(table_ref, scan)
    return jnp.clip(row - strip * height, 0, height - 1), col


def roll_into(out_ref, value, row, col, tall_ref):
    frame = value.shape[0]
    half = frame // 2
    turned = pltpu.roll(value, col, 1)
    for index in range(frame // LANES):
        at = slice(index * LANES, (index + 1) * LANES)
        tall_ref[index, :half] = turned[half:, at]
        tall_ref[index, half:] = turned[:, at]
        out_ref[:, at] = tall_ref[index, pl.ds(half - row, frame), :]


def reorder_kernel(own_ref, received_ref, swapped_ref, factor_ref, rows_ref):
    frame = own_ref.shape[1]
    odd = lax.axis_index("tile") % 2 == 1
    moved = jnp.where(lax.axis_index("mode") == 0, received_ref[0], swapped_ref[0])
    value = jnp.where(odd, moved, own_ref[0])
    source = lax.broadcasted_iota(jnp.int32, (frame, frame), 0)
    target = lax.broadcasted_iota(jnp.int32, (frame, frame), 1)
    half = frame // 2
    order = jnp.where(target < half, 2 * target, 2 * target - frame + 1)
    pick = jnp.where(source == order, 1.0, 0.0).astype(jnp.bfloat16)
    high = value.astype(jnp.bfloat16)
    rest = value - high.astype(jnp.float32)
    middle = rest.astype(jnp.bfloat16)
    low = (rest - middle.astype(jnp.float32)).astype(jnp.bfloat16)
    columns = jnp.dot(high, pick, preferred_element_type=jnp.float32)
    columns = columns + jnp.dot(middle, pick, preferred_element_type=jnp.float32)
    columns = columns + jnp.dot(low, pick, preferred_element_type=jnp.float32)
    for index in range(frame // LANES):
        at = slice(index * LANES, (index + 1) * LANES)
        rows_ref[index] = columns[:, at]
        factor_ref[:half, at] = rows_ref[index, pl.ds(0, half, stride=2), :]
        factor_ref[half:, at] = rows_ref[index, pl.ds(1, half, stride=2), :]


def prepare_kernel(
    scan_ref, received_ref, swapped_ref, table_ref, object_ref, own_probe_ref, other_probe_ref,
    gradient_ref, probe_ref, window_ref, light_ref, total_ref, place_ref,
    zero_ref, tall_ref, own_ref, got_ref, other_ref, sems,
):
    pairs = [(scan_ref, own_ref), (received_ref, got_ref), (swapped_ref, other_ref)]
    scalars = fetch(pairs, sems)
    zero_ref[...] = jnp.zeros_like(zero_ref)
    step = zero_ref.shape[0]
    copies = []
    for part in range(2):
        for at in range(0, object_ref.shape[1], step):
            copies += fetch([(zero_ref, gradient_ref.at[part, at : at + step])], sems, len(pairs) + len(copies))
    modes = own_probe_ref.shape[0]
    sources = [ref.at[mode, part] for ref in (own_probe_ref, other_probe_ref) for mode in range(modes) for part in range(2)]
    total = sources[0][...] * sources[0][...]
    for source in sources[1:]:
        total = total + source[...] * source[...]
    total_ref[...] = total
    for copy in scalars:
        copy.wait()
    height = object_ref.shape[1]
    tile = lax.axis_index("tile")
    odd = tile % 2
    scan, _, _ = slots(own_ref, got_ref, other_ref)
    row, col = within(table_ref, scan, tile - 2 * odd, height)
    shift = col % LANES
    for index, source in enumerate(sources):
        mode, part = divmod(index, 2)
        roll_into(probe_ref.at[mode, part], source[...], row, shift, tall_ref.at[mode, part])
    roll_into(light_ref, total_ref[...], row, shift, tall_ref.at[0, 0])
    low, high = strip_window(object_ref, col)
    window_ref[:, :, :LANES] = low
    window_ref[:, :, LANES:] = high
    live = jnp.where(odd == 1, (tile >= 2).astype(jnp.int32), 1)
    keep_scalars(place_ref, (jnp.where(odd == 1, 0, row), jnp.where(odd == 1, row, height), live))
    for copy in copies:
        copy.wait()


def right(value, high, low):
    first, second = split(value)
    return jnp.dot(
        jnp.concatenate([first, second, first], axis=1),
        jnp.concatenate([high, high, low], axis=0),
        preferred_element_type=jnp.float32,
    )


def left(high, low, value):
    first, second = split(value)
    return jnp.dot(
        jnp.concatenate([high, high, low], axis=1),
        jnp.concatenate([first, second, first], axis=0),
        preferred_element_type=jnp.float32,
    )


def transform_rows(probe_ref, start, window_ref, matrix_ref, out_ref):
    modes = probe_ref.shape[0]
    height, frame = window_ref.shape[1:]
    half = frame // 2
    sums, differences = [], []
    for mode in range(modes):
        probe_re = probe_ref[mode, 0, pl.ds(start, height), :]
        probe_im = probe_ref[mode, 1, pl.ds(start, height), :]
        wave_re = probe_re * window_ref[0] - probe_im * window_ref[1]
        wave_im = probe_re * window_ref[1] + probe_im * window_ref[0]
        for pieces, sign in ((sums, 1.0), (differences, -1.0)):
            pieces.append(
                jnp.concatenate(
                    [wave_re[:, :half] + sign * wave_re[:, half:], wave_im[:, :half] + sign * wave_im[:, half:]],
                    axis=1,
                )
            )
    even = right(jnp.concatenate(sums, axis=0), matrix_ref[0], matrix_ref[1])
    odd = right(jnp.concatenate(differences, axis=0), matrix_ref[4], matrix_ref[5])
    for mode in range(modes):
        at = slice(mode * height, (mode + 1) * height)
        out_ref[mode, 0] = jnp.concatenate([even[at, :half], odd[at, :half]], axis=1)
        out_ref[mode, 1] = jnp.concatenate([even[at, half:], odd[at, half:]], axis=1)


def strip_kernel(own_ref, received_ref, probe_ref, matrix_ref, own_out_ref, out_ref):
    height = received_ref.shape[1]
    start = pl.multiple_of((1 - lax.axis_index("mode")) * height, height)
    transform_rows(probe_ref, 0, own_ref, matrix_ref, own_out_ref)
    transform_rows(probe_ref, start, received_ref, matrix_ref, out_ref)


def wave_kernel(
    place_ref, window_ref, received_ref, swapped_ref, own_ref, first_ref, probe_ref, amplitude_ref, light_ref,
    matrix_ref, send_ref, keep_ref, patch_ref, far_ref, second_ref,
):
    modes, _, frame, _ = probe_ref.shape
    height = window_ref.shape[1]
    half = frame // 2
    core = lax.axis_index("mode")
    low, high = place_ref[0:1, :1].astype(jnp.int32), place_ref[1:2, :1].astype(jnp.int32)
    transform_rows(probe_ref, pl.multiple_of(core * height, height), swapped_ref, matrix_ref, second_ref)
    level = lax.broadcasted_iota(jnp.int32, (height, frame), 0)

    def assemble(own, got, given):
        nearer = jnp.where(core == 0, got, given)
        farther = jnp.where(core == 0, given, got)
        return jnp.where((level >= low) & (level < high), own, farther), nearer

    for part in range(2):
        top, bottom = assemble(window_ref[part], received_ref[part], swapped_ref[part])
        patch_ref[part, :height] = top
        patch_ref[part, height:] = bottom
    intensity = jnp.zeros((frame, frame), jnp.float32)
    for mode in range(modes):
        top_re, bottom_re = assemble(own_ref[mode, 0], first_ref[mode, 0], second_ref[mode, 0])
        top_im, bottom_im = assemble(own_ref[mode, 1], first_ref[mode, 1], second_ref[mode, 1])
        added = jnp.concatenate([top_re + bottom_re, top_im + bottom_im], axis=0)
        taken = jnp.concatenate([top_re - bottom_re, top_im - bottom_im], axis=0)
        even = left(matrix_ref[2], matrix_ref[3], added)
        odd = left(matrix_ref[6], matrix_ref[7], taken)
        far_ref[mode, 0] = even
        far_ref[mode, 1] = odd
        squares = jnp.concatenate(
            [even[:half] * even[:half] + even[half:] * even[half:], odd[:half] * odd[:half] + odd[half:] * odd[half:]],
            axis=0,
        )
        intensity = intensity + squares
    factor = amplitude_ref[...] * lax.rsqrt(jnp.maximum(intensity, FLOOR))
    grad_re = jnp.zeros((frame, frame), jnp.float32)
    grad_im = jnp.zeros((frame, frame), jnp.float32)
    even_factor = jnp.concatenate([factor[:half], factor[:half]], axis=0)
    odd_factor = jnp.concatenate([factor[half:], factor[half:]], axis=0)
    evens, odds = [], []
    for mode in range(modes):
        even = left(matrix_ref[0], matrix_ref[1], far_ref[mode, 0] * even_factor)
        odd = left(matrix_ref[4], matrix_ref[5], far_ref[mode, 1] * odd_factor)
        top, bottom = even + odd, even - odd
        mid_re = jnp.concatenate([top[:half], bottom[:half]], axis=0)
        mid_im = jnp.concatenate([top[half:], bottom[half:]], axis=0)
        evens.append(jnp.concatenate([mid_re[:, :half], mid_im[:, :half]], axis=1))
        odds.append(jnp.concatenate([mid_re[:, half:], mid_im[:, half:]], axis=1))
    even = right(jnp.concatenate(evens, axis=0), matrix_ref[2], matrix_ref[3])
    odd = right(jnp.concatenate(odds, axis=0), matrix_ref[6], matrix_ref[7])
    fores, afts = even + odd, even - odd
    for mode in range(modes):
        fore = fores[mode * frame : (mode + 1) * frame]
        aft = afts[mode * frame : (mode + 1) * frame]
        back_re = jnp.concatenate([fore[:, :half], aft[:, :half]], axis=1)
        back_im = jnp.concatenate([fore[:, half:], aft[:, half:]], axis=1)
        probe_re, probe_im = probe_ref[mode, 0], probe_ref[mode, 1]
        grad_re = grad_re + (probe_re * back_re + probe_im * back_im)
        grad_im = grad_im + (probe_re * back_im - probe_im * back_re)
    live = place_ref[2:3, :1]
    grad_re = (grad_re - light_ref[...] * patch_ref[0]) * live
    grad_im = (grad_im - light_ref[...] * patch_ref[1]) * live
    send_ref[:height] = jnp.where(core == 0, grad_re[height:], grad_re[:height])
    send_ref[height : 2 * height] = jnp.where(core == 0, grad_im[height:], grad_im[:height])
    send_ref[2 * height :] = jnp.broadcast_to(live, (8, frame))
    keep_ref[0] = grad_re[:height]
    keep_ref[1] = grad_im[:height]


def covers(col, block, low, high, lane):
    start, shift = col // LANES, col % LANES
    distance = block - start
    value = jnp.where(distance == 1, high, low)
    first = jnp.where(distance == 0, shift, jnp.where(distance == 1, 0, LANES))
    last = jnp.where(distance == 2, shift, 0)
    keep = (lane >= first) | (lane < last)
    return jnp.where(keep, value, 0.0)


def base_kernel(
    place_ref, scan_ref, received_ref, swapped_ref, table_ref, object_ref, keep_ref, light_ref, plain_ref,
    old_gradient_ref,
    updated_ref, gradient_ref, total_ref, weight_ref, first_ref, second_ref, others_ref, new_ref, tall_ref, turned_ref,
    own_ref, got_ref, other_ref, sems, fills,
):
    del old_gradient_ref
    height, breadth = object_ref.shape[1:]
    tile = lax.axis_index("tile")
    core = lax.axis_index("mode")
    fill = pltpu.make_async_copy(object_ref, updated_ref, fills.at[0])
    fill.start()
    scalars = fetch([(scan_ref, own_ref), (received_ref, got_ref), (swapped_ref, other_ref)], fills, 1)
    total_ref[...] = jnp.zeros_like(total_ref)
    weight_ref[...] = jnp.zeros_like(weight_ref)
    for copy in scalars:
        copy.wait()
    odd = tile % 2
    main, above, third = slots(own_ref, got_ref, other_ref)
    _, col = within(table_ref, main, tile, height)
    live = place_ref[2:3, :1]
    start, stop = place_ref[0:1, :1].astype(jnp.int32), place_ref[1:2, :1].astype(jnp.int32)
    lane = lax.broadcasted_iota(jnp.int32, (height, LANES), 1)
    level = lax.broadcasted_iota(jnp.int32, (height, LANES), 0)
    kept = (level >= start) & (level < stop)
    for slot in range(3):
        block = jnp.minimum(col // LANES + slot, breadth // LANES - 1)
        at = pl.ds(pl.multiple_of(block * LANES, LANES), LANES)
        light = covers(col, block, light_ref[:height, :LANES], light_ref[:height, LANES:], lane)
        weight = jnp.where(kept, light * live, 0.0)
        weight_ref[:, at] = weight
        scale = 1.0 / (weight + ALPHA)
        for part in range(2):
            change = covers(col, block, keep_ref[part, :, :LANES], keep_ref[part, :, LANES:], lane)
            change = jnp.where(kept, change, 0.0)
            total_ref[part, :, at] = change
            new_ref[slot, part] = object_ref[part, :, at] + change * scale
    places = []
    for scan, strip, far in ((above, tile - 1, False), (third, tile - 2 + 2 * odd, True)):
        row, start = within(table_ref, scan, strip, height)
        index = int(far)
        roll_into(turned_ref.at[index], plain_ref[...], row, start % LANES, tall_ref.at[index])
        turned = turned_ref[index]
        begin = jnp.where(odd == 1, row, 0) if far else 0
        end = jnp.where(odd == 1, height, row) if far else height
        places.append((start, begin, end, turned[:height] if far else turned[height:]))
    chosen = []
    for slot, out_ref in ((0, first_ref), (1, second_ref)):
        direct = core == slot
        near, far = places
        out_ref[...] = jnp.where(direct, near[3], far[3])
        chosen += [jnp.where(direct, near[index], far[index]) for index in range(3)]
    keep_scalars(others_ref, chosen)
    fill.wait()
    copies = []
    for slot in range(3):
        block = jnp.minimum(col // LANES + slot, breadth // LANES - 1)
        at = pl.ds(pl.multiple_of(block * LANES, LANES), LANES)
        copies.append(write(slot, col, block, at, total_ref.at[:, :, at], new_ref, gradient_ref, updated_ref, sems))
    finish(copies)


def write(slot, col, block, at, source, new_ref, gradient_ref, updated_ref, sems):
    fresh = col // LANES + slot == block
    one = pltpu.make_async_copy(source, gradient_ref.at[:, :, at], sems.at[2 * slot])
    two = pltpu.make_async_copy(new_ref.at[slot], updated_ref.at[:, :, at], sems.at[2 * slot + 1])

    @pl.when(fresh)
    def _():
        one.start()
        two.start()

    return fresh, one, two


def finish(copies):
    for fresh, one, two in copies:

        @pl.when(fresh)
        def _(one=one, two=two):
            one.wait()
            two.wait()


def add_windows(windows, main, object_ref, total_ref, weight_ref, updated_ref, gradient_ref, new_ref, sum_ref, sems):
    height, breadth = object_ref.shape[1:]
    lane = lax.broadcasted_iota(jnp.int32, (height, LANES), 1)
    level = lax.broadcasted_iota(jnp.int32, (height, LANES), 0)
    col = windows[main][0]
    copies = []
    for slot in range(3):
        block = jnp.minimum(col // LANES + slot, breadth // LANES - 1)
        at = pl.ds(pl.multiple_of(block * LANES, LANES), LANES)
        weight = weight_ref[:, at]
        sums = [total_ref[0, :, at], total_ref[1, :, at]]
        for start, begin, end, light_ref, change_ref in windows:
            inside = (level >= begin) & (level < end)
            live = change_ref[2 * height : 2 * height + 1, :1]
            light = covers(start, block, light_ref[:, :LANES], light_ref[:, LANES:], lane)
            weight = weight + jnp.where(inside, light, 0.0) * live
            for part in range(2):
                rows = slice(part * height, (part + 1) * height)
                change = covers(start, block, change_ref[rows, :LANES], change_ref[rows, LANES:], lane)
                sums[part] = sums[part] + jnp.where(inside, change, 0.0)
        scale = 1.0 / (weight + ALPHA)
        for part in range(2):
            sum_ref[slot, part] = sums[part]
            new_ref[slot, part] = object_ref[part, :, at] + sums[part] * scale
        copies.append(write(slot, col, block, at, sum_ref.at[slot], new_ref, gradient_ref, updated_ref, sems))
    finish(copies)


def first_kernel(
    others_ref, object_ref, total_ref, weight_ref, first_ref, received_ref, old_updated_ref, old_gradient_ref,
    updated_ref, gradient_ref, new_ref, sum_ref, sems,
):
    del old_updated_ref, old_gradient_ref
    windows = [(*(scalar_of(others_ref, index) for index in range(3)), first_ref, received_ref)]
    add_windows(windows, 0, object_ref, total_ref, weight_ref, updated_ref, gradient_ref, new_ref, sum_ref, sems)


def second_kernel(
    others_ref, object_ref, total_ref, weight_ref, first_ref, second_ref, received_ref, swapped_ref,
    old_updated_ref, old_gradient_ref, updated_ref, gradient_ref, new_ref, sum_ref, sems,
):
    del old_updated_ref, old_gradient_ref
    windows = [
        (*(scalar_of(others_ref, index) for index in range(3)), first_ref, received_ref),
        (*(scalar_of(others_ref, index) for index in range(3, 6)), second_ref, swapped_ref),
    ]
    add_windows(windows, 1, object_ref, total_ref, weight_ref, updated_ref, gradient_ref, new_ref, sum_ref, sems)


def call(kernel, out_shape, in_specs, out_specs, scratch=(), mebibytes=16, aliases=None):
    return pl.pallas_call(
        kernel,
        out_shape=out_shape,
        in_specs=in_specs,
        out_specs=out_specs,
        scratch_shapes=list(scratch),
        input_output_aliases=aliases or {},
        compiler_params=pltpu.CompilerParams(vmem_limit_bytes=mebibytes << 20),
        cost_estimate=pl.CostEstimate(flops=5000000, bytes_accessed=5000000, transcendentals=0),
    )


def space(where):
    return pl.BlockSpec(memory_space=where)


def shape(*dims, dtype=jnp.float32):
    return jax.ShapeDtypeStruct(dims, dtype)


def solution(mesh):
    tiles, cores = mesh.shape["tile"], mesh.shape["mode"]
    up = [(2 * t, 2 * (t + 1)) for t in range(tiles - 1)] + [(2 * t + 1, 2 * (t + 2) + 1) for t in range(tiles - 2)]
    gather = [(2 * t, 2 * (t ^ 1)) for t in range(tiles)]
    gather += [(2 * t + 1, 2 * (t - 2) + 1) for t in range(2, tiles, 2)]
    gather += [(2 * t + 1, 2 * (t + 2) + 1) for t in range(1, tiles - 2, 2)]
    spread = [(target, source) for source, target in gather]
    onward = [(2 * t, 2 * (t + 2)) for t in range(1, tiles - 2, 2)]
    swap = [(2 * t + core, 2 * t + 1 - core) for t in range(tiles) for core in range(2)]
    assert cores == 2 and tiles % 2 == 0

    def move(value, pairs):
        return lax.ppermute(value, AXES, pairs)

    def step(object_tiles, probe_modes, amplitudes, scan_offsets, slot_scan, slot_count):
        height, breadth = object_tiles.shape[1:]
        modes, _, frame, _ = probe_modes.shape
        assert slot_scan.shape[0] == 1 and frame == 2 * height and height == LANES
        table = scan_offsets.T
        matrix = jnp.asarray(matrices(frame))
        received_scan = move(slot_scan, up)
        other_probe = move(probe_modes, swap)
        received_amplitude = move(amplitudes, onward)
        scalar = pltpu.SMEM((1,), jnp.int32)
        staged, table = call(
            stage_kernel,
            (shape(*object_tiles.shape), shape(*table.shape, dtype=jnp.int32)),
            [space(pltpu.HBM)] * 2,
            [space(VMEM)] * 2,
            [pltpu.SemaphoreType.DMA((2,))],
            mebibytes=8,
        )(pltpu.with_memory_space_constraint(object_tiles, pltpu.HBM), pltpu.with_memory_space_constraint(table, pltpu.HBM))
        window = call(
            select_kernel, shape(2, height, frame), [space(SMEM)] * 2 + [space(VMEM)] * 2, space(VMEM)
        )(slot_scan, received_scan, table, staged)
        received = move(window, gather)
        swapped_scan = move(received_scan, swap)
        swapped_amplitude = move(received_amplitude, swap)
        scalar = pltpu.SMEM((1,), jnp.int32)
        strip = shape(2 * modes, 2, height, frame)
        whole = shape(2, height, breadth)
        gradient, probe, own_window, light, plain, place = call(
            prepare_kernel,
            (
                whole,
                shape(2 * modes, 2, frame, frame),
                shape(2, height, frame),
                shape(frame, frame),
                shape(frame, frame),
                shape(8, LANES),
            ),
            [space(pl.ANY)] * 3 + [space(VMEM)] * 4,
            [space(pl.ANY)] + [space(VMEM)] * 5,
            [
                pltpu.VMEM((height // 8, breadth), jnp.float32),
                pltpu.VMEM((2 * modes, 2, frame // LANES, frame + height, LANES), jnp.float32),
                scalar,
                scalar,
                scalar,
                pltpu.SemaphoreType.DMA((19,)),
            ],
        )(slot_scan, received_scan, swapped_scan, table, staged, probe_modes, other_probe)
        swapped = move(received, swap)
        amplitude = call(
            reorder_kernel,
            shape(frame, frame),
            [space(VMEM)] * 3,
            space(VMEM),
            [pltpu.VMEM((frame // LANES, frame, LANES), jnp.float32)],
        )(amplitudes, received_amplitude, swapped_amplitude)
        own_strip, first_strip = call(strip_kernel, (strip, strip), [space(VMEM)] * 4, [space(VMEM)] * 2)(
            own_window, received, probe, matrix
        )
        send, keep = call(
            wave_kernel,
            (shape(2 * height + 8, frame), shape(2, height, frame)),
            [space(VMEM)] * 10,
            [space(VMEM)] * 2,
            [
                pltpu.VMEM((2, frame, frame), jnp.float32),
                pltpu.VMEM((2 * modes, 2, frame, frame), jnp.float32),
                pltpu.VMEM((2 * modes, 2, height, frame), jnp.float32),
            ],
            mebibytes=24,
        )(place, own_window, received, swapped, own_strip, first_strip, probe, amplitude, light, matrix)
        received_change = move(send, spread)
        blocks = pltpu.VMEM((3, 2, height, LANES), jnp.float32)
        semaphores = pltpu.SemaphoreType.DMA((6,))
        updated, gradient, total, weight, first, second, others = call(
            base_kernel,
            (
                whole,
                whole,
                whole,
                shape(height, breadth),
                shape(height, frame),
                shape(height, frame),
                shape(8, LANES),
            ),
            [space(VMEM)] + [space(pl.ANY)] * 3 + [space(VMEM)] * 5 + [space(pl.ANY)],
            [space(pl.ANY)] * 2 + [space(VMEM)] * 5,
            [
                blocks,
                pltpu.VMEM((2, frame // LANES, frame + height, LANES), jnp.float32),
                pltpu.VMEM((2, frame, frame), jnp.float32),
                scalar,
                scalar,
                scalar,
                semaphores,
                pltpu.SemaphoreType.DMA((4,)),
            ],
            aliases={9: 1},
        )(place, slot_scan, received_scan, swapped_scan, table, staged, keep, light, plain, gradient)
        swapped_change = move(received_change, swap)
        updated, gradient = call(
            first_kernel,
            (whole, whole),
            [space(VMEM)] * 6 + [space(pl.ANY)] * 2,
            [space(pl.ANY)] * 2,
            [blocks, blocks, semaphores],
            aliases={6: 0, 7: 1},
        )(others, staged, total, weight, first, received_change, updated, gradient)
        return call(
            second_kernel,
            (whole, whole),
            [space(VMEM)] * 8 + [space(pl.ANY)] * 2,
            [space(pl.ANY)] * 2,
            [blocks, blocks, semaphores],
            aliases={8: 0, 9: 1},
        )(others, staged, total, weight, first, second, received_change, swapped_change, updated, gradient)

    return jax.shard_map(
        step,
        mesh=mesh,
        in_specs=(
            P(None, "tile", None),
            P("mode", None, None, None),
            P("tile", None, None),
            P(),
            P("tile"),
            P("tile"),
        ),
        out_specs=(P(None, "tile", None), P(None, "tile", None)),
        check_vma=False,
    )
```

```python
import math

import jax
import jax.numpy as jnp
import numpy as np
from jax import lax
from jax.experimental import pallas as pl
from jax.experimental.pallas import tpu as pltpu
from jax.sharding import PartitionSpec as P


FLOOR = 0.25
ALPHA = 0.5
LANES = 128
AXES = ("tile", "mode")
VMEM = pltpu.VMEM
SMEM = pltpu.SMEM


def split(value):
    high = value.astype(jnp.bfloat16)
    low = (value - high.astype(jnp.float32)).astype(jnp.bfloat16)
    return high, low


def matrices(frame):
    half = frame // 2
    pixel = np.arange(half)[:, None]
    wave = np.arange(half)[None, :]
    blocks = []
    for parity in (0, 1):
        phase = 2.0 * math.pi * (pixel * (2 * wave + parity) % frame) / frame
        cos, sin = np.cos(phase) / math.sqrt(frame), np.sin(phase) / math.sqrt(frame)
        forward = np.block([[cos, -sin], [sin, cos]])
        for table in (forward, forward.T):
            high = table.astype(jnp.bfloat16)
            blocks.append(high)
            blocks.append((table - high.astype(np.float64)).astype(jnp.bfloat16))
    return np.stack(blocks)


def lookup(table_ref, scan):
    base = pl.multiple_of((scan // LANES) * LANES, LANES)
    chunk = table_ref[:, pl.ds(base, LANES)].astype(jnp.float32)
    lane = lax.broadcasted_iota(jnp.int32, chunk.shape, 1)
    picked = jnp.where(lane == scan - base, chunk, 0.0)
    row = jnp.sum(picked[0:1]).astype(jnp.int32)
    col = jnp.sum(picked[1:2]).astype(jnp.int32)
    return row, col


def strip_window(object_ref, col):
    blocks = object_ref.shape[2] // LANES
    block, shift = col // LANES, col % LANES
    first = object_ref[:, :, pl.ds(pl.multiple_of(block * LANES, LANES), LANES)]
    second = object_ref[:, :, pl.ds(pl.multiple_of((block + 1) * LANES, LANES), LANES)]
    last = jnp.minimum(block + 2, blocks - 1)
    third = object_ref[:, :, pl.ds(pl.multiple_of(last * LANES, LANES), LANES)]
    lane = lax.broadcasted_iota(jnp.int32, first.shape, 2)
    return jnp.where(lane < shift, third, first), second


def fetch(pairs, sems, first=0):
    copies = [pltpu.make_async_copy(a, b, sems.at[first + index]) for index, (a, b) in enumerate(pairs)]
    for copy in copies:
        copy.start()
    return copies


def select_kernel(own_scan_ref, scan_ref, table_ref, object_ref, out_ref):
    odd = lax.axis_index("tile") % 2 == 1
    scan = jnp.where(odd & (lax.axis_index("mode") == 1), own_scan_ref[0], scan_ref[0])
    _, col = lookup(table_ref, scan)
    low, high = strip_window(object_ref, col)
    out_ref[:, :, :LANES] = low
    out_ref[:, :, LANES:] = high


def slots(own_ref, received_ref, swapped_ref):
    first = lax.axis_index("mode") == 0
    odd = lax.axis_index("tile") % 2 == 1
    own, got, other = own_ref[0], received_ref[0], swapped_ref[0]
    above = jnp.where(first, got, other)
    further = jnp.where(first, other, got)
    return jnp.where(odd, further, own), above, jnp.where(odd, own, further)


def keep_scalars(out_ref, values):
    for index, value in enumerate(values):
        row = jnp.full((1, out_ref.shape[1]), value, jnp.int32)
        out_ref[index : index + 1] = row.astype(jnp.float32)


def scalar_of(ref, index):
    return jnp.max(ref[index : index + 1]).astype(jnp.int32)


def within(table_ref, scan, strip, height):
    row, col = lookup(table_ref, scan)
    return jnp.clip(row - strip * height, 0, height - 1), col


def roll_into(out_ref, value, row, col, tall_ref):
    frame = value.shape[0]
    half = frame // 2
    turned = pltpu.roll(value, col, 1)
    for index in range(frame // LANES):
        at = slice(index * LANES, (index + 1) * LANES)
        tall_ref[index, :half] = turned[half:, at]
        tall_ref[index, half:] = turned[:, at]
        out_ref[:, at] = tall_ref[index, pl.ds(half - row, frame), :]


def reorder_kernel(own_ref, received_ref, swapped_ref, factor_ref, rows_ref):
    frame = own_ref.shape[1]
    odd = lax.axis_index("tile") % 2 == 1
    moved = jnp.where(lax.axis_index("mode") == 0, received_ref[0], swapped_ref[0])
    value = jnp.where(odd, moved, own_ref[0])
    source = lax.broadcasted_iota(jnp.int32, (frame, frame), 0)
    target = lax.broadcasted_iota(jnp.int32, (frame, frame), 1)
    half = frame // 2
    order = jnp.where(target < half, 2 * target, 2 * target - frame + 1)
    pick = jnp.where(source == order, 1.0, 0.0).astype(jnp.bfloat16)
    high = value.astype(jnp.bfloat16)
    rest = value - high.astype(jnp.float32)
    middle = rest.astype(jnp.bfloat16)
    low = (rest - middle.astype(jnp.float32)).astype(jnp.bfloat16)
    columns = jnp.dot(high, pick, preferred_element_type=jnp.float32)
    columns = columns + jnp.dot(middle, pick, preferred_element_type=jnp.float32)
    columns = columns + jnp.dot(low, pick, preferred_element_type=jnp.float32)
    for index in range(frame // LANES):
        at = slice(index * LANES, (index + 1) * LANES)
        rows_ref[index] = columns[:, at]
        factor_ref[:half, at] = rows_ref[index, pl.ds(0, half, stride=2), :]
        factor_ref[half:, at] = rows_ref[index, pl.ds(1, half, stride=2), :]


def prepare_kernel(
    scan_ref, received_ref, swapped_ref, table_ref, object_ref, own_probe_ref, other_probe_ref,
    gradient_ref, probe_ref, window_ref, light_ref, total_ref, place_ref,
    zero_ref, tall_ref, own_ref, got_ref, other_ref, sems,
):
    pairs = [(scan_ref, own_ref), (received_ref, got_ref), (swapped_ref, other_ref)]
    scalars = fetch(pairs, sems)
    zero_ref[...] = jnp.zeros_like(zero_ref)
    step = zero_ref.shape[0]
    copies = []
    for part in range(2):
        for at in range(0, object_ref.shape[1], step):
            copies += fetch([(zero_ref, gradient_ref.at[part, at : at + step])], sems, len(pairs) + len(copies))
    modes = own_probe_ref.shape[0]
    sources = [ref.at[mode, part] for ref in (own_probe_ref, other_probe_ref) for mode in range(modes) for part in range(2)]
    total = sources[0][...] * sources[0][...]
    for source in sources[1:]:
        total = total + source[...] * source[...]
    total_ref[...] = total
    for copy in scalars:
        copy.wait()
    height = object_ref.shape[1]
    tile = lax.axis_index("tile")
    odd = tile % 2
    scan, _, _ = slots(own_ref, got_ref, other_ref)
    row, col = within(table_ref, scan, tile - 2 * odd, height)
    shift = col % LANES
    for index, source in enumerate(sources):
        mode, part = divmod(index, 2)
        roll_into(probe_ref.at[mode, part], source[...], row, shift, tall_ref.at[mode, part])
    roll_into(light_ref, total_ref[...], row, shift, tall_ref.at[0, 0])
    low, high = strip_window(object_ref, col)
    window_ref[:, :, :LANES] = low
    window_ref[:, :, LANES:] = high
    live = jnp.where(odd == 1, (tile >= 2).astype(jnp.int32), 1)
    keep_scalars(place_ref, (jnp.where(odd == 1, 0, row), jnp.where(odd == 1, row, height), live))
    for copy in copies:
        copy.wait()


def right(value, high, low):
    first, second = split(value)
    return jnp.dot(
        jnp.concatenate([first, second, first], axis=1),
        jnp.concatenate([high, high, low], axis=0),
        preferred_element_type=jnp.float32,
    )


def left(high, low, value):
    first, second = split(value)
    return jnp.dot(
        jnp.concatenate([high, high, low], axis=1),
        jnp.concatenate([first, second, first], axis=0),
        preferred_element_type=jnp.float32,
    )


def transform_rows(probe_ref, start, window_ref, matrix_ref, out_ref):
    modes = probe_ref.shape[0]
    height, frame = window_ref.shape[1:]
    half = frame // 2
    sums, differences = [], []
    for mode in range(modes):
        probe_re = probe_ref[mode, 0, pl.ds(start, height), :]
        probe_im = probe_ref[mode, 1, pl.ds(start, height), :]
        wave_re = probe_re * window_ref[0] - probe_im * window_ref[1]
        wave_im = probe_re * window_ref[1] + probe_im * window_ref[0]
        for pieces, sign in ((sums, 1.0), (differences, -1.0)):
            pieces.append(
                jnp.concatenate(
                    [wave_re[:, :half] + sign * wave_re[:, half:], wave_im[:, :half] + sign * wave_im[:, half:]],
                    axis=1,
                )
            )
    even = right(jnp.concatenate(sums, axis=0), matrix_ref[0], matrix_ref[1])
    odd = right(jnp.concatenate(differences, axis=0), matrix_ref[4], matrix_ref[5])
    for mode in range(modes):
        at = slice(mode * height, (mode + 1) * height)
        out_ref[mode, 0] = jnp.concatenate([even[at, :half], odd[at, :half]], axis=1)
        out_ref[mode, 1] = jnp.concatenate([even[at, half:], odd[at, half:]], axis=1)


def strip_kernel(own_ref, received_ref, probe_ref, matrix_ref, own_out_ref, out_ref):
    height = received_ref.shape[1]
    start = pl.multiple_of((1 - lax.axis_index("mode")) * height, height)
    transform_rows(probe_ref, 0, own_ref, matrix_ref, own_out_ref)
    transform_rows(probe_ref, start, received_ref, matrix_ref, out_ref)


def wave_kernel(
    place_ref, window_ref, received_ref, swapped_ref, own_ref, first_ref, probe_ref, amplitude_ref, light_ref,
    matrix_ref, send_ref, keep_ref, patch_ref, far_ref, second_ref,
):
    modes, _, frame, _ = probe_ref.shape
    height = window_ref.shape[1]
    half = frame // 2
    core = lax.axis_index("mode")
    low, high = place_ref[0:1, :1].astype(jnp.int32), place_ref[1:2, :1].astype(jnp.int32)
    transform_rows(probe_ref, pl.multiple_of(core * height, height), swapped_ref, matrix_ref, second_ref)
    level = lax.broadcasted_iota(jnp.int32, (height, frame), 0)

    def assemble(own, got, given):
        nearer = jnp.where(core == 0, got, given)
        farther = jnp.where(core == 0, given, got)
        return jnp.where((level >= low) & (level < high), own, farther), nearer

    for part in range(2):
        top, bottom = assemble(window_ref[part], received_ref[part], swapped_ref[part])
        patch_ref[part, :height] = top
        patch_ref[part, height:] = bottom
    intensity = jnp.zeros((frame, frame), jnp.float32)
    for mode in range(modes):
        top_re, bottom_re = assemble(own_ref[mode, 0], first_ref[mode, 0], second_ref[mode, 0])
        top_im, bottom_im = assemble(own_ref[mode, 1], first_ref[mode, 1], second_ref[mode, 1])
        added = jnp.concatenate([top_re + bottom_re, top_im + bottom_im], axis=0)
        taken = jnp.concatenate([top_re - bottom_re, top_im - bottom_im], axis=0)
        even = left(matrix_ref[2], matrix_ref[3], added)
        odd = left(matrix_ref[6], matrix_ref[7], taken)
        far_ref[mode, 0] = even
        far_ref[mode, 1] = odd
        squares = jnp.concatenate(
            [even[:half] * even[:half] + even[half:] * even[half:], odd[:half] * odd[:half] + odd[half:] * odd[half:]],
            axis=0,
        )
        intensity = intensity + squares
    factor = amplitude_ref[...] * lax.rsqrt(jnp.maximum(intensity, FLOOR))
    grad_re = jnp.zeros((frame, frame), jnp.float32)
    grad_im = jnp.zeros((frame, frame), jnp.float32)
    even_factor = jnp.concatenate([factor[:half], factor[:half]], axis=0)
    odd_factor = jnp.concatenate([factor[half:], factor[half:]], axis=0)
    evens, odds = [], []
    for mode in range(modes):
        even = left(matrix_ref[0], matrix_ref[1], far_ref[mode, 0] * even_factor)
        odd = left(matrix_ref[4], matrix_ref[5], far_ref[mode, 1] * odd_factor)
        top, bottom = even + odd, even - odd
        mid_re = jnp.concatenate([top[:half], bottom[:half]], axis=0)
        mid_im = jnp.concatenate([top[half:], bottom[half:]], axis=0)
        evens.append(jnp.concatenate([mid_re[:, :half], mid_im[:, :half]], axis=1))
        odds.append(jnp.concatenate([mid_re[:, half:], mid_im[:, half:]], axis=1))
    even = right(jnp.concatenate(evens, axis=0), matrix_ref[2], matrix_ref[3])
    odd = right(jnp.concatenate(odds, axis=0), matrix_ref[6], matrix_ref[7])
    fores, afts = even + odd, even - odd
    for mode in range(modes):
        fore = fores[mode * frame : (mode + 1) * frame]
        aft = afts[mode * frame : (mode + 1) * frame]
        back_re = jnp.concatenate([fore[:, :half], aft[:, :half]], axis=1)
        back_im = jnp.concatenate([fore[:, half:], aft[:, half:]], axis=1)
        probe_re, probe_im = probe_ref[mode, 0], probe_ref[mode, 1]
        grad_re = grad_re + (probe_re * back_re + probe_im * back_im)
        grad_im = grad_im + (probe_re * back_im - probe_im * back_re)
    live = place_ref[2:3, :1]
    grad_re = (grad_re - light_ref[...] * patch_ref[0]) * live
    grad_im = (grad_im - light_ref[...] * patch_ref[1]) * live
    send_ref[:height] = jnp.where(core == 0, grad_re[height:], grad_re[:height])
    send_ref[height : 2 * height] = jnp.where(core == 0, grad_im[height:], grad_im[:height])
    send_ref[2 * height :] = jnp.broadcast_to(live, (8, frame))
    keep_ref[0] = grad_re[:height]
    keep_ref[1] = grad_im[:height]


def covers(col, block, low, high, lane):
    start, shift = col // LANES, col % LANES
    distance = block - start
    value = jnp.where(distance == 1, high, low)
    first = jnp.where(distance == 0, shift, jnp.where(distance == 1, 0, LANES))
    last = jnp.where(distance == 2, shift, 0)
    keep = (lane >= first) | (lane < last)
    return jnp.where(keep, value, 0.0)


def base_kernel(
    place_ref, scan_ref, received_ref, swapped_ref, table_ref, object_ref, keep_ref, light_ref, plain_ref,
    old_gradient_ref,
    updated_ref, gradient_ref, total_ref, weight_ref, first_ref, second_ref, others_ref, new_ref, tall_ref, turned_ref,
    own_ref, got_ref, other_ref, sems, fills,
):
    del old_gradient_ref
    height, breadth = object_ref.shape[1:]
    tile = lax.axis_index("tile")
    core = lax.axis_index("mode")
    fill = pltpu.make_async_copy(object_ref, updated_ref, fills.at[0])
    fill.start()
    scalars = fetch([(scan_ref, own_ref), (received_ref, got_ref), (swapped_ref, other_ref)], fills, 1)
    total_ref[...] = jnp.zeros_like(total_ref)
    weight_ref[...] = jnp.zeros_like(weight_ref)
    for copy in scalars:
        copy.wait()
    odd = tile % 2
    main, above, third = slots(own_ref, got_ref, other_ref)
    _, col = within(table_ref, main, tile, height)
    live = place_ref[2:3, :1]
    start, stop = place_ref[0:1, :1].astype(jnp.int32), place_ref[1:2, :1].astype(jnp.int32)
    lane = lax.broadcasted_iota(jnp.int32, (height, LANES), 1)
    level = lax.broadcasted_iota(jnp.int32, (height, LANES), 0)
    kept = (level >= start) & (level < stop)
    for slot in range(3):
        block = jnp.minimum(col // LANES + slot, breadth // LANES - 1)
        at = pl.ds(pl.multiple_of(block * LANES, LANES), LANES)
        light = covers(col, block, light_ref[:height, :LANES], light_ref[:height, LANES:], lane)
        weight = jnp.where(kept, light * live, 0.0)
        weight_ref[:, at] = weight
        scale = 1.0 / (weight + ALPHA)
        for part in range(2):
            change = covers(col, block, keep_ref[part, :, :LANES], keep_ref[part, :, LANES:], lane)
            change = jnp.where(kept, change, 0.0)
            total_ref[part, :, at] = change
            new_ref[slot, part] = object_ref[part, :, at] + change * scale
    places = []
    for scan, strip, far in ((above, tile - 1, False), (third, tile - 2 + 2 * odd, True)):
        row, start = within(table_ref, scan, strip, height)
        index = int(far)
        roll_into(turned_ref.at[index], plain_ref[...], row, start % LANES, tall_ref.at[index])
        turned = turned_ref[index]
        begin = jnp.where(odd == 1, row, 0) if far else 0
        end = jnp.where(odd == 1, height, row) if far else height
        places.append((start, begin, end, turned[:height] if far else turned[height:]))
    chosen = []
    for slot, out_ref in ((0, first_ref), (1, second_ref)):
        direct = core == slot
        near, far = places
        out_ref[...] = jnp.where(direct, near[3], far[3])
        chosen += [jnp.where(direct, near[index], far[index]) for index in range(3)]
    keep_scalars(others_ref, chosen)
    fill.wait()
    copies = []
    for slot in range(3):
        block = jnp.minimum(col // LANES + slot, breadth // LANES - 1)
        at = pl.ds(pl.multiple_of(block * LANES, LANES), LANES)
        copies.append(write(slot, col, block, at, total_ref.at[:, :, at], new_ref, gradient_ref, updated_ref, sems))
    finish(copies)


def write(slot, col, block, at, source, new_ref, gradient_ref, updated_ref, sems):
    fresh = col // LANES + slot == block
    one = pltpu.make_async_copy(source, gradient_ref.at[:, :, at], sems.at[2 * slot])
    two = pltpu.make_async_copy(new_ref.at[slot], updated_ref.at[:, :, at], sems.at[2 * slot + 1])

    @pl.when(fresh)
    def _():
        one.start()
        two.start()

    return fresh, one, two


def finish(copies):
    for fresh, one, two in copies:

        @pl.when(fresh)
        def _(one=one, two=two):
            one.wait()
            two.wait()


def add_windows(windows, main, object_ref, total_ref, weight_ref, updated_ref, gradient_ref, new_ref, sum_ref, sems):
    height, breadth = object_ref.shape[1:]
    lane = lax.broadcasted_iota(jnp.int32, (height, LANES), 1)
    level = lax.broadcasted_iota(jnp.int32, (height, LANES), 0)
    col = windows[main][0]
    copies = []
    for slot in range(3):
        block = jnp.minimum(col // LANES + slot, breadth // LANES - 1)
        at = pl.ds(pl.multiple_of(block * LANES, LANES), LANES)
        weight = weight_ref[:, at]
        sums = [total_ref[0, :, at], total_ref[1, :, at]]
        for start, begin, end, light_ref, change_ref in windows:
            inside = (level >= begin) & (level < end)
            live = change_ref[2 * height : 2 * height + 1, :1]
            light = covers(start, block, light_ref[:, :LANES], light_ref[:, LANES:], lane)
            weight = weight + jnp.where(inside, light, 0.0) * live
            for part in range(2):
                rows = slice(part * height, (part + 1) * height)
                change = covers(start, block, change_ref[rows, :LANES], change_ref[rows, LANES:], lane)
                sums[part] = sums[part] + jnp.where(inside, change, 0.0)
        scale = 1.0 / (weight + ALPHA)
        for part in range(2):
            sum_ref[slot, part] = sums[part]
            new_ref[slot, part] = object_ref[part, :, at] + sums[part] * scale
        copies.append(write(slot, col, block, at, sum_ref.at[slot], new_ref, gradient_ref, updated_ref, sems))
    finish(copies)


def first_kernel(
    others_ref, object_ref, total_ref, weight_ref, first_ref, received_ref, old_updated_ref, old_gradient_ref,
    updated_ref, gradient_ref, new_ref, sum_ref, sems,
):
    del old_updated_ref, old_gradient_ref
    windows = [(*(scalar_of(others_ref, index) for index in range(3)), first_ref, received_ref)]
    add_windows(windows, 0, object_ref, total_ref, weight_ref, updated_ref, gradient_ref, new_ref, sum_ref, sems)


def second_kernel(
    others_ref, object_ref, total_ref, weight_ref, first_ref, second_ref, received_ref, swapped_ref,
    old_updated_ref, old_gradient_ref, updated_ref, gradient_ref, new_ref, sum_ref, sems,
):
    del old_updated_ref, old_gradient_ref
    windows = [
        (*(scalar_of(others_ref, index) for index in range(3)), first_ref, received_ref),
        (*(scalar_of(others_ref, index) for index in range(3, 6)), second_ref, swapped_ref),
    ]
    add_windows(windows, 1, object_ref, total_ref, weight_ref, updated_ref, gradient_ref, new_ref, sum_ref, sems)


def call(kernel, out_shape, in_specs, out_specs, scratch=(), mebibytes=16, aliases=None):
    return pl.pallas_call(
        kernel,
        out_shape=out_shape,
        in_specs=in_specs,
        out_specs=out_specs,
        scratch_shapes=list(scratch),
        input_output_aliases=aliases or {},
        compiler_params=pltpu.CompilerParams(vmem_limit_bytes=mebibytes << 20),
        cost_estimate=pl.CostEstimate(flops=5000000, bytes_accessed=5000000, transcendentals=0),
    )


def space(where):
    return pl.BlockSpec(memory_space=where)


def shape(*dims, dtype=jnp.float32):
    return jax.ShapeDtypeStruct(dims, dtype)


def solution(mesh):
    tiles, cores = mesh.shape["tile"], mesh.shape["mode"]
    up = [(2 * t, 2 * (t + 1)) for t in range(tiles - 1)] + [(2 * t + 1, 2 * (t + 2) + 1) for t in range(tiles - 2)]
    gather = [(2 * t, 2 * (t ^ 1)) for t in range(tiles)]
    gather += [(2 * t + 1, 2 * (t - 2) + 1) for t in range(2, tiles, 2)]
    gather += [(2 * t + 1, 2 * (t + 2) + 1) for t in range(1, tiles - 2, 2)]
    spread = [(target, source) for source, target in gather]
    onward = [(2 * t, 2 * (t + 2)) for t in range(1, tiles - 2, 2)]
    swap = [(2 * t + core, 2 * t + 1 - core) for t in range(tiles) for core in range(2)]
    assert cores == 2 and tiles % 2 == 0

    def move(value, pairs):
        return lax.ppermute(value, AXES, pairs)

    def step(object_tiles, probe_modes, amplitudes, scan_offsets, slot_scan, slot_count):
        height, breadth = object_tiles.shape[1:]
        modes, _, frame, _ = probe_modes.shape
        assert slot_scan.shape[0] == 1 and frame == 2 * height and height == LANES
        table = scan_offsets.T
        matrix = jnp.asarray(matrices(frame))
        received_scan = move(slot_scan, up)
        staged = move(object_tiles, swap)
        table = move(table, swap)
        other_probe = move(probe_modes, swap)
        received_amplitude = move(amplitudes, onward)
        scalar = pltpu.SMEM((1,), jnp.int32)
        window = call(
            select_kernel, shape(2, height, frame), [space(SMEM)] * 2 + [space(VMEM)] * 2, space(VMEM)
        )(slot_scan, received_scan, table, staged)
        received = move(window, gather)
        swapped_scan = move(received_scan, swap)
        swapped_amplitude = move(received_amplitude, swap)
        scalar = pltpu.SMEM((1,), jnp.int32)
        strip = shape(2 * modes, 2, height, frame)
        whole = shape(2, height, breadth)
        gradient, probe, own_window, light, plain, place = call(
            prepare_kernel,
            (
                whole,
                shape(2 * modes, 2, frame, frame),
                shape(2, height, frame),
                shape(frame, frame),
                shape(frame, frame),
                shape(8, LANES),
            ),
            [space(pl.ANY)] * 3 + [space(VMEM)] * 4,
            [space(pl.ANY)] + [space(VMEM)] * 5,
            [
                pltpu.VMEM((height // 8, breadth), jnp.float32),
                pltpu.VMEM((2 * modes, 2, frame // LANES, frame + height, LANES), jnp.float32),
                scalar,
                scalar,
                scalar,
                pltpu.SemaphoreType.DMA((19,)),
            ],
        )(slot_scan, received_scan, swapped_scan, table, staged, probe_modes, other_probe)
        swapped = move(received, swap)
        amplitude = call(
            reorder_kernel,
            shape(frame, frame),
            [space(VMEM)] * 3,
            space(VMEM),
            [pltpu.VMEM((frame // LANES, frame, LANES), jnp.float32)],
        )(amplitudes, received_amplitude, swapped_amplitude)
        own_strip, first_strip = call(strip_kernel, (strip, strip), [space(VMEM)] * 4, [space(VMEM)] * 2)(
            own_window, received, probe, matrix
        )
        send, keep = call(
            wave_kernel,
            (shape(2 * height + 8, frame), shape(2, height, frame)),
            [space(VMEM)] * 10,
            [space(VMEM)] * 2,
            [
                pltpu.VMEM((2, frame, frame), jnp.float32),
                pltpu.VMEM((2 * modes, 2, frame, frame), jnp.float32),
                pltpu.VMEM((2 * modes, 2, height, frame), jnp.float32),
            ],
            mebibytes=24,
        )(place, own_window, received, swapped, own_strip, first_strip, probe, amplitude, light, matrix)
        received_change = move(send, spread)
        blocks = pltpu.VMEM((3, 2, height, LANES), jnp.float32)
        semaphores = pltpu.SemaphoreType.DMA((6,))
        updated, gradient, total, weight, first, second, others = call(
            base_kernel,
            (
                whole,
                whole,
                whole,
                shape(height, breadth),
                shape(height, frame),
                shape(height, frame),
                shape(8, LANES),
            ),
            [space(VMEM)] + [space(pl.ANY)] * 3 + [space(VMEM)] * 5 + [space(pl.ANY)],
            [space(pl.ANY)] * 2 + [space(VMEM)] * 5,
            [
                blocks,
                pltpu.VMEM((2, frame // LANES, frame + height, LANES), jnp.float32),
                pltpu.VMEM((2, frame, frame), jnp.float32),
                scalar,
                scalar,
                scalar,
                semaphores,
                pltpu.SemaphoreType.DMA((4,)),
            ],
            aliases={9: 1},
        )(place, slot_scan, received_scan, swapped_scan, table, staged, keep, light, plain, gradient)
        swapped_change = move(received_change, swap)
        updated, gradient = call(
            first_kernel,
            (whole, whole),
            [space(VMEM)] * 6 + [space(pl.ANY)] * 2,
            [space(pl.ANY)] * 2,
            [blocks, blocks, semaphores],
            aliases={6: 0, 7: 1},
        )(others, staged, total, weight, first, received_change, updated, gradient)
        return call(
            second_kernel,
            (whole, whole),
            [space(VMEM)] * 8 + [space(pl.ANY)] * 2,
            [space(pl.ANY)] * 2,
            [blocks, blocks, semaphores],
            aliases={8: 0, 9: 1},
        )(others, staged, total, weight, first, second, received_change, swapped_change, updated, gradient)

    return jax.shard_map(
        step,
        mesh=mesh,
        in_specs=(
            P(None, "tile", None),
            P("mode", None, None, None),
            P("tile", None, None),
            P(),
            P("tile"),
            P("tile"),
        ),
        out_specs=(P(None, "tile", None), P(None, "tile", None)),
        check_vma=False,
    )
```

```python
import math

import jax
import jax.numpy as jnp
import numpy as np
from jax import lax
from jax.experimental import pallas as pl
from jax.experimental.pallas import tpu as pltpu
from jax.sharding import PartitionSpec as P


FLOOR = 0.25
ALPHA = 0.5
LANES = 128
AXES = ("tile", "mode")
VMEM = pltpu.VMEM
SMEM = pltpu.SMEM


def split(value):
    high = value.astype(jnp.bfloat16)
    low = (value - high.astype(jnp.float32)).astype(jnp.bfloat16)
    return high, low


def matrices(frame):
    half = frame // 2
    pixel = np.arange(half)[:, None]
    wave = np.arange(half)[None, :]
    blocks = []
    for parity in (0, 1):
        phase = 2.0 * math.pi * (pixel * (2 * wave + parity) % frame) / frame
        cos, sin = np.cos(phase) / math.sqrt(frame), np.sin(phase) / math.sqrt(frame)
        forward = np.block([[cos, -sin], [sin, cos]])
        for table in (forward, forward.T):
            high = table.astype(jnp.bfloat16)
            blocks.append(high)
            blocks.append((table - high.astype(np.float64)).astype(jnp.bfloat16))
    return np.stack(blocks)


def lookup(table_ref, scan):
    base = pl.multiple_of((scan // LANES) * LANES, LANES)
    chunk = table_ref[:, pl.ds(base, LANES)].astype(jnp.float32)
    lane = lax.broadcasted_iota(jnp.int32, chunk.shape, 1)
    picked = jnp.where(lane == scan - base, chunk, 0.0)
    row = jnp.sum(picked[0:1]).astype(jnp.int32)
    col = jnp.sum(picked[1:2]).astype(jnp.int32)
    return row, col


def strip_window(object_ref, col):
    blocks = object_ref.shape[2] // LANES
    block, shift = col // LANES, col % LANES
    first = object_ref[:, :, pl.ds(pl.multiple_of(block * LANES, LANES), LANES)]
    second = object_ref[:, :, pl.ds(pl.multiple_of((block + 1) * LANES, LANES), LANES)]
    last = jnp.minimum(block + 2, blocks - 1)
    third = object_ref[:, :, pl.ds(pl.multiple_of(last * LANES, LANES), LANES)]
    lane = lax.broadcasted_iota(jnp.int32, first.shape, 2)
    return jnp.where(lane < shift, third, first), second


def fetch(pairs, sems, first=0):
    copies = [pltpu.make_async_copy(a, b, sems.at[first + index]) for index, (a, b) in enumerate(pairs)]
    for copy in copies:
        copy.start()
    return copies


def select_kernel(own_scan_ref, scan_ref, table_ref, object_ref, out_ref):
    odd = lax.axis_index("tile") % 2 == 1
    scan = jnp.where(odd & (lax.axis_index("mode") == 1), own_scan_ref[0], scan_ref[0])
    _, col = lookup(table_ref, scan)
    low, high = strip_window(object_ref, col)
    out_ref[:, :, :LANES] = low
    out_ref[:, :, LANES:] = high


def slots(own_ref, received_ref, swapped_ref):
    first = lax.axis_index("mode") == 0
    odd = lax.axis_index("tile") % 2 == 1
    own, got, other = own_ref[0], received_ref[0], swapped_ref[0]
    above = jnp.where(first, got, other)
    further = jnp.where(first, other, got)
    return jnp.where(odd, further, own), above, jnp.where(odd, own, further)


def keep_scalars(out_ref, values):
    for index, value in enumerate(values):
        row = jnp.full((1, out_ref.shape[1]), value, jnp.int32)
        out_ref[index : index + 1] = row.astype(jnp.float32)


def scalar_of(ref, index):
    return jnp.max(ref[index : index + 1]).astype(jnp.int32)


def within(table_ref, scan, strip, height):
    row, col = lookup(table_ref, scan)
    return jnp.clip(row - strip * height, 0, height - 1), col


def roll_into(out_ref, value, row, col, tall_ref):
    frame = value.shape[0]
    half = frame // 2
    turned = pltpu.roll(value, col, 1)
    for index in range(frame // LANES):
        at = slice(index * LANES, (index + 1) * LANES)
        tall_ref[index, :half] = turned[half:, at]
        tall_ref[index, half:] = turned[:, at]
        out_ref[:, at] = tall_ref[index, pl.ds(half - row, frame), :]


def reorder_kernel(own_ref, received_ref, swapped_ref, factor_ref, rows_ref):
    frame = own_ref.shape[1]
    odd = lax.axis_index("tile") % 2 == 1
    moved = jnp.where(lax.axis_index("mode") == 0, received_ref[0], swapped_ref[0])
    value = jnp.where(odd, moved, own_ref[0])
    source = lax.broadcasted_iota(jnp.int32, (frame, frame), 0)
    target = lax.broadcasted_iota(jnp.int32, (frame, frame), 1)
    half = frame // 2
    order = jnp.where(target < half, 2 * target, 2 * target - frame + 1)
    pick = jnp.where(source == order, 1.0, 0.0).astype(jnp.bfloat16)
    high = value.astype(jnp.bfloat16)
    rest = value - high.astype(jnp.float32)
    middle = rest.astype(jnp.bfloat16)
    low = (rest - middle.astype(jnp.float32)).astype(jnp.bfloat16)
    columns = jnp.dot(high, pick, preferred_element_type=jnp.float32)
    columns = columns + jnp.dot(middle, pick, preferred_element_type=jnp.float32)
    columns = columns + jnp.dot(low, pick, preferred_element_type=jnp.float32)
    for index in range(frame // LANES):
        at = slice(index * LANES, (index + 1) * LANES)
        rows_ref[index] = columns[:, at]
        factor_ref[:half, at] = rows_ref[index, pl.ds(0, half, stride=2), :]
        factor_ref[half:, at] = rows_ref[index, pl.ds(1, half, stride=2), :]


def probe_parts(own_probe_ref, other_probe_ref):
    modes = own_probe_ref.shape[0]
    return [ref.at[mode, part] for ref in (own_probe_ref, other_probe_ref) for mode in range(modes) for part in range(2)]


def fill_kernel(own_probe_ref, other_probe_ref, gradient_ref, total_ref, zero_ref, sems):
    zero_ref[...] = jnp.zeros_like(zero_ref)
    step = zero_ref.shape[0]
    copies = []
    for part in range(2):
        for at in range(0, gradient_ref.shape[1], step):
            copies += fetch([(zero_ref, gradient_ref.at[part, at : at + step])], sems, len(copies))
    total = jnp.zeros(total_ref.shape, jnp.float32)
    for source in probe_parts(own_probe_ref, other_probe_ref):
        total = total + source[...] * source[...]
    total_ref[...] = total
    for copy in copies:
        copy.wait()


def prepare_kernel(
    scan_ref, received_ref, swapped_ref, table_ref, object_ref, own_probe_ref, other_probe_ref, total_ref,
    probe_ref, window_ref, light_ref, place_ref, tall_ref, own_ref, got_ref, other_ref, sems,
):
    for copy in fetch([(scan_ref, own_ref), (received_ref, got_ref), (swapped_ref, other_ref)], sems):
        copy.wait()
    sources = probe_parts(own_probe_ref, other_probe_ref)
    height = object_ref.shape[1]
    tile = lax.axis_index("tile")
    odd = tile % 2
    scan, _, _ = slots(own_ref, got_ref, other_ref)
    row, col = within(table_ref, scan, tile - 2 * odd, height)
    shift = col % LANES
    for index, source in enumerate(sources):
        roll_into(probe_ref.at[index // 2, index % 2], source[...], row, shift, tall_ref.at[index])
    roll_into(light_ref, total_ref[...], row, shift, tall_ref.at[len(sources)])
    low, high = strip_window(object_ref, col)
    window_ref[:, :, :LANES] = low
    window_ref[:, :, LANES:] = high
    live = jnp.where(odd == 1, (tile >= 2).astype(jnp.int32), 1)
    keep_scalars(place_ref, (jnp.where(odd == 1, 0, row), jnp.where(odd == 1, row, height), live))


def right(value, high, low):
    first, second = split(value)
    return jnp.dot(
        jnp.concatenate([first, second, first], axis=1),
        jnp.concatenate([high, high, low], axis=0),
        preferred_element_type=jnp.float32,
    )


def left(high, low, value):
    first, second = split(value)
    return jnp.dot(
        jnp.concatenate([high, high, low], axis=1),
        jnp.concatenate([first, second, first], axis=0),
        preferred_element_type=jnp.float32,
    )


def transform_rows(probe_ref, start, window_ref, matrix_ref, out_ref):
    modes = probe_ref.shape[0]
    height, frame = window_ref.shape[1:]
    half = frame // 2
    sums, differences = [], []
    for mode in range(modes):
        probe_re = probe_ref[mode, 0, pl.ds(start, height), :]
        probe_im = probe_ref[mode, 1, pl.ds(start, height), :]
        wave_re = probe_re * window_ref[0] - probe_im * window_ref[1]
        wave_im = probe_re * window_ref[1] + probe_im * window_ref[0]
        for pieces, sign in ((sums, 1.0), (differences, -1.0)):
            pieces.append(
                jnp.concatenate(
                    [wave_re[:, :half] + sign * wave_re[:, half:], wave_im[:, :half] + sign * wave_im[:, half:]],
                    axis=1,
                )
            )
    even = right(jnp.concatenate(sums, axis=0), matrix_ref[0], matrix_ref[1])
    odd = right(jnp.concatenate(differences, axis=0), matrix_ref[4], matrix_ref[5])
    for mode in range(modes):
        at = slice(mode * height, (mode + 1) * height)
        out_ref[mode, 0] = jnp.concatenate([even[at, :half], odd[at, :half]], axis=1)
        out_ref[mode, 1] = jnp.concatenate([even[at, half:], odd[at, half:]], axis=1)


def strip_kernel(own_ref, received_ref, probe_ref, matrix_ref, own_out_ref, out_ref):
    height = received_ref.shape[1]
    start = pl.multiple_of((1 - lax.axis_index("mode")) * height, height)
    transform_rows(probe_ref, 0, own_ref, matrix_ref, own_out_ref)
    transform_rows(probe_ref, start, received_ref, matrix_ref, out_ref)


def wave_kernel(
    place_ref, window_ref, received_ref, swapped_ref, own_ref, first_ref, probe_ref, amplitude_ref, light_ref,
    matrix_ref, send_ref, keep_ref, patch_ref, far_ref, second_ref,
):
    modes, _, frame, _ = probe_ref.shape
    height = window_ref.shape[1]
    half = frame // 2
    core = lax.axis_index("mode")
    low, high = place_ref[0:1, :1].astype(jnp.int32), place_ref[1:2, :1].astype(jnp.int32)
    transform_rows(probe_ref, pl.multiple_of(core * height, height), swapped_ref, matrix_ref, second_ref)
    level = lax.broadcasted_iota(jnp.int32, (height, frame), 0)

    def assemble(own, got, given):
        nearer = jnp.where(core == 0, got, given)
        farther = jnp.where(core == 0, given, got)
        return jnp.where((level >= low) & (level < high), own, farther), nearer

    for part in range(2):
        top, bottom = assemble(window_ref[part], received_ref[part], swapped_ref[part])
        patch_ref[part, :height] = top
        patch_ref[part, height:] = bottom
    intensity = jnp.zeros((frame, frame), jnp.float32)
    for mode in range(modes):
        top_re, bottom_re = assemble(own_ref[mode, 0], first_ref[mode, 0], second_ref[mode, 0])
        top_im, bottom_im = assemble(own_ref[mode, 1], first_ref[mode, 1], second_ref[mode, 1])
        added = jnp.concatenate([top_re + bottom_re, top_im + bottom_im], axis=0)
        taken = jnp.concatenate([top_re - bottom_re, top_im - bottom_im], axis=0)
        even = left(matrix_ref[2], matrix_ref[3], added)
        odd = left(matrix_ref[6], matrix_ref[7], taken)
        far_ref[mode, 0] = even
        far_ref[mode, 1] = odd
        squares = jnp.concatenate(
            [even[:half] * even[:half] + even[half:] * even[half:], odd[:half] * odd[:half] + odd[half:] * odd[half:]],
            axis=0,
        )
        intensity = intensity + squares
    factor = amplitude_ref[...] * lax.rsqrt(jnp.maximum(intensity, FLOOR))
    grad_re = jnp.zeros((frame, frame), jnp.float32)
    grad_im = jnp.zeros((frame, frame), jnp.float32)
    even_factor = jnp.concatenate([factor[:half], factor[:half]], axis=0)
    odd_factor = jnp.concatenate([factor[half:], factor[half:]], axis=0)
    evens, odds = [], []
    for mode in range(modes):
        even = left(matrix_ref[0], matrix_ref[1], far_ref[mode, 0] * even_factor)
        odd = left(matrix_ref[4], matrix_ref[5], far_ref[mode, 1] * odd_factor)
        top, bottom = even + odd, even - odd
        mid_re = jnp.concatenate([top[:half], bottom[:half]], axis=0)
        mid_im = jnp.concatenate([top[half:], bottom[half:]], axis=0)
        evens.append(jnp.concatenate([mid_re[:, :half], mid_im[:, :half]], axis=1))
        odds.append(jnp.concatenate([mid_re[:, half:], mid_im[:, half:]], axis=1))
    even = right(jnp.concatenate(evens, axis=0), matrix_ref[2], matrix_ref[3])
    odd = right(jnp.concatenate(odds, axis=0), matrix_ref[6], matrix_ref[7])
    fores, afts = even + odd, even - odd
    for mode in range(modes):
        fore = fores[mode * frame : (mode + 1) * frame]
        aft = afts[mode * frame : (mode + 1) * frame]
        back_re = jnp.concatenate([fore[:, :half], aft[:, :half]], axis=1)
        back_im = jnp.concatenate([fore[:, half:], aft[:, half:]], axis=1)
        probe_re, probe_im = probe_ref[mode, 0], probe_ref[mode, 1]
        grad_re = grad_re + (probe_re * back_re + probe_im * back_im)
        grad_im = grad_im + (probe_re * back_im - probe_im * back_re)
    live = place_ref[2:3, :1]
    grad_re = (grad_re - light_ref[...] * patch_ref[0]) * live
    grad_im = (grad_im - light_ref[...] * patch_ref[1]) * live
    send_ref[:height] = jnp.where(core == 0, grad_re[height:], grad_re[:height])
    send_ref[height : 2 * height] = jnp.where(core == 0, grad_im[height:], grad_im[:height])
    send_ref[2 * height :] = jnp.broadcast_to(live, (8, frame))
    keep_ref[0] = grad_re[:height]
    keep_ref[1] = grad_im[:height]


def covers(col, block, low, high, lane):
    start, shift = col // LANES, col % LANES
    distance = block - start
    value = jnp.where(distance == 1, high, low)
    first = jnp.where(distance == 0, shift, jnp.where(distance == 1, 0, LANES))
    last = jnp.where(distance == 2, shift, 0)
    keep = (lane >= first) | (lane < last)
    return jnp.where(keep, value, 0.0)


def base_kernel(
    place_ref, scan_ref, received_ref, swapped_ref, table_ref, object_ref, keep_ref, light_ref, plain_ref,
    old_gradient_ref,
    updated_ref, gradient_ref, total_ref, weight_ref, first_ref, second_ref, others_ref, new_ref, tall_ref, turned_ref,
    own_ref, got_ref, other_ref, sems, fills,
):
    del old_gradient_ref
    height, breadth = object_ref.shape[1:]
    tile = lax.axis_index("tile")
    core = lax.axis_index("mode")
    fill = pltpu.make_async_copy(object_ref, updated_ref, fills.at[0])
    fill.start()
    scalars = fetch([(scan_ref, own_ref), (received_ref, got_ref), (swapped_ref, other_ref)], fills, 1)
    total_ref[...] = jnp.zeros_like(total_ref)
    weight_ref[...] = jnp.zeros_like(weight_ref)
    for copy in scalars:
        copy.wait()
    odd = tile % 2
    main, above, third = slots(own_ref, got_ref, other_ref)
    _, col = within(table_ref, main, tile, height)
    live = place_ref[2:3, :1]
    start, stop = place_ref[0:1, :1].astype(jnp.int32), place_ref[1:2, :1].astype(jnp.int32)
    lane = lax.broadcasted_iota(jnp.int32, (height, LANES), 1)
    level = lax.broadcasted_iota(jnp.int32, (height, LANES), 0)
    kept = (level >= start) & (level < stop)
    for slot in range(3):
        block = jnp.minimum(col // LANES + slot, breadth // LANES - 1)
        at = pl.ds(pl.multiple_of(block * LANES, LANES), LANES)
        light = covers(col, block, light_ref[:height, :LANES], light_ref[:height, LANES:], lane)
        weight = jnp.where(kept, light * live, 0.0)
        weight_ref[:, at] = weight
        scale = 1.0 / (weight + ALPHA)
        for part in range(2):
            change = covers(col, block, keep_ref[part, :, :LANES], keep_ref[part, :, LANES:], lane)
            change = jnp.where(kept, change, 0.0)
            total_ref[part, :, at] = change
            new_ref[slot, part] = object_ref[part, :, at] + change * scale
    places = []
    for scan, strip, far in ((above, tile - 1, False), (third, tile - 2 + 2 * odd, True)):
        row, start = within(table_ref, scan, strip, height)
        index = int(far)
        roll_into(turned_ref.at[index], plain_ref[...], row, start % LANES, tall_ref.at[index])
        turned = turned_ref[index]
        begin = jnp.where(odd == 1, row, 0) if far else 0
        end = jnp.where(odd == 1, height, row) if far else height
        places.append((start, begin, end, turned[:height] if far else turned[height:]))
    chosen = []
    for slot, out_ref in ((0, first_ref), (1, second_ref)):
        direct = core == slot
        near, far = places
        out_ref[...] = jnp.where(direct, near[3], far[3])
        chosen += [jnp.where(direct, near[index], far[index]) for index in range(3)]
    keep_scalars(others_ref, chosen)
    fill.wait()
    copies = []
    for slot in range(3):
        block = jnp.minimum(col // LANES + slot, breadth // LANES - 1)
        at = pl.ds(pl.multiple_of(block * LANES, LANES), LANES)
        copies.append(write(slot, col, block, at, total_ref.at[:, :, at], new_ref, gradient_ref, updated_ref, sems))
    finish(copies)


def write(slot, col, block, at, source, new_ref, gradient_ref, updated_ref, sems):
    fresh = col // LANES + slot == block
    one = pltpu.make_async_copy(source, gradient_ref.at[:, :, at], sems.at[2 * slot])
    two = pltpu.make_async_copy(new_ref.at[slot], updated_ref.at[:, :, at], sems.at[2 * slot + 1])

    @pl.when(fresh)
    def _():
        one.start()
        two.start()

    return fresh, one, two


def finish(copies):
    for fresh, one, two in copies:

        @pl.when(fresh)
        def _(one=one, two=two):
            one.wait()
            two.wait()


def add_windows(windows, main, object_ref, total_ref, weight_ref, updated_ref, gradient_ref, new_ref, sum_ref, sems):
    height, breadth = object_ref.shape[1:]
    lane = lax.broadcasted_iota(jnp.int32, (height, LANES), 1)
    level = lax.broadcasted_iota(jnp.int32, (height, LANES), 0)
    col = windows[main][0]
    copies = []
    for slot in range(3):
        block = jnp.minimum(col // LANES + slot, breadth // LANES - 1)
        at = pl.ds(pl.multiple_of(block * LANES, LANES), LANES)
        weight = weight_ref[:, at]
        sums = [total_ref[0, :, at], total_ref[1, :, at]]
        for start, begin, end, light_ref, change_ref in windows:
            inside = (level >= begin) & (level < end)
            live = change_ref[2 * height : 2 * height + 1, :1]
            light = covers(start, block, light_ref[:, :LANES], light_ref[:, LANES:], lane)
            weight = weight + jnp.where(inside, light, 0.0) * live
            for part in range(2):
                rows = slice(part * height, (part + 1) * height)
                change = covers(start, block, change_ref[rows, :LANES], change_ref[rows, LANES:], lane)
                sums[part] = sums[part] + jnp.where(inside, change, 0.0)
        scale = 1.0 / (weight + ALPHA)
        for part in range(2):
            sum_ref[slot, part] = sums[part]
            new_ref[slot, part] = object_ref[part, :, at] + sums[part] * scale
        copies.append(write(slot, col, block, at, sum_ref.at[slot], new_ref, gradient_ref, updated_ref, sems))
    finish(copies)


def first_kernel(
    others_ref, object_ref, total_ref, weight_ref, first_ref, received_ref, old_updated_ref, old_gradient_ref,
    updated_ref, gradient_ref, new_ref, sum_ref, sems,
):
    del old_updated_ref, old_gradient_ref
    windows = [(*(scalar_of(others_ref, index) for index in range(3)), first_ref, received_ref)]
    add_windows(windows, 0, object_ref, total_ref, weight_ref, updated_ref, gradient_ref, new_ref, sum_ref, sems)


def second_kernel(
    others_ref, object_ref, total_ref, weight_ref, first_ref, second_ref, received_ref, swapped_ref,
    old_updated_ref, old_gradient_ref, updated_ref, gradient_ref, new_ref, sum_ref, sems,
):
    del old_updated_ref, old_gradient_ref
    windows = [
        (*(scalar_of(others_ref, index) for index in range(3)), first_ref, received_ref),
        (*(scalar_of(others_ref, index) for index in range(3, 6)), second_ref, swapped_ref),
    ]
    add_windows(windows, 1, object_ref, total_ref, weight_ref, updated_ref, gradient_ref, new_ref, sum_ref, sems)


def call(kernel, out_shape, in_specs, out_specs, scratch=(), mebibytes=16, aliases=None):
    return pl.pallas_call(
        kernel,
        out_shape=out_shape,
        in_specs=in_specs,
        out_specs=out_specs,
        scratch_shapes=list(scratch),
        input_output_aliases=aliases or {},
        compiler_params=pltpu.CompilerParams(vmem_limit_bytes=mebibytes << 20),
        cost_estimate=pl.CostEstimate(flops=5000000, bytes_accessed=5000000, transcendentals=0),
    )


def space(where):
    return pl.BlockSpec(memory_space=where)


def shape(*dims, dtype=jnp.float32):
    return jax.ShapeDtypeStruct(dims, dtype)


def solution(mesh):
    tiles, cores = mesh.shape["tile"], mesh.shape["mode"]
    up = [(2 * t, 2 * (t + 1)) for t in range(tiles - 1)] + [(2 * t + 1, 2 * (t + 2) + 1) for t in range(tiles - 2)]
    gather = [(2 * t, 2 * (t ^ 1)) for t in range(tiles)]
    gather += [(2 * t + 1, 2 * (t - 2) + 1) for t in range(2, tiles, 2)]
    gather += [(2 * t + 1, 2 * (t + 2) + 1) for t in range(1, tiles - 2, 2)]
    spread = [(target, source) for source, target in gather]
    onward = [(2 * t, 2 * (t + 2)) for t in range(1, tiles - 2, 2)]
    swap = [(2 * t + core, 2 * t + 1 - core) for t in range(tiles) for core in range(2)]
    assert cores == 2 and tiles % 2 == 0

    def move(value, pairs):
        return lax.ppermute(value, AXES, pairs)

    def step(object_tiles, probe_modes, amplitudes, scan_offsets, slot_scan, slot_count):
        height, breadth = object_tiles.shape[1:]
        modes, _, frame, _ = probe_modes.shape
        assert slot_scan.shape[0] == 1 and frame == 2 * height and height == LANES
        table = scan_offsets.T
        matrix = jnp.asarray(matrices(frame))
        received_scan = move(slot_scan, up)
        staged = move(object_tiles, swap)
        table = move(table, swap)
        other_probe = move(probe_modes, swap)
        received_amplitude = move(amplitudes, onward)
        scalar = pltpu.SMEM((1,), jnp.int32)
        window = call(
            select_kernel, shape(2, height, frame), [space(SMEM)] * 2 + [space(VMEM)] * 2, space(VMEM)
        )(slot_scan, received_scan, table, staged)
        received = move(window, gather)
        swapped_scan = move(received_scan, swap)
        swapped_amplitude = move(received_amplitude, swap)
        scalar = pltpu.SMEM((1,), jnp.int32)
        strip = shape(2 * modes, 2, height, frame)
        whole = shape(2, height, breadth)
        gradient, plain = call(
            fill_kernel,
            (whole, shape(frame, frame)),
            [space(VMEM)] * 2,
            [space(pl.ANY), space(VMEM)],
            [pltpu.VMEM((height // 8, breadth), jnp.float32), pltpu.SemaphoreType.DMA((16,))],
        )(probe_modes, other_probe)
        probe, own_window, light, place = call(
            prepare_kernel,
            (
                shape(2 * modes, 2, frame, frame),
                shape(2, height, frame),
                shape(frame, frame),
                shape(8, LANES),
            ),
            [space(pl.ANY)] * 3 + [space(VMEM)] * 5,
            [space(VMEM)] * 4,
            [
                pltpu.VMEM((4 * modes + 1, frame // LANES, frame + height, LANES), jnp.float32),
                scalar,
                scalar,
                scalar,
                pltpu.SemaphoreType.DMA((3,)),
            ],
        )(slot_scan, received_scan, swapped_scan, table, staged, probe_modes, other_probe, plain)
        swapped = move(received, swap)
        amplitude = call(
            reorder_kernel,
            shape(frame, frame),
            [space(VMEM)] * 3,
            space(VMEM),
            [pltpu.VMEM((frame // LANES, frame, LANES), jnp.float32)],
        )(amplitudes, received_amplitude, swapped_amplitude)
        own_strip, first_strip = call(strip_kernel, (strip, strip), [space(VMEM)] * 4, [space(VMEM)] * 2)(
            own_window, received, probe, matrix
        )
        send, keep = call(
            wave_kernel,
            (shape(2 * height + 8, frame), shape(2, height, frame)),
            [space(VMEM)] * 10,
            [space(VMEM)] * 2,
            [
                pltpu.VMEM((2, frame, frame), jnp.float32),
                pltpu.VMEM((2 * modes, 2, frame, frame), jnp.float32),
                pltpu.VMEM((2 * modes, 2, height, frame), jnp.float32),
            ],
            mebibytes=24,
        )(place, own_window, received, swapped, own_strip, first_strip, probe, amplitude, light, matrix)
        received_change = move(send, spread)
        blocks = pltpu.VMEM((3, 2, height, LANES), jnp.float32)
        semaphores = pltpu.SemaphoreType.DMA((6,))
        updated, gradient, total, weight, first, second, others = call(
            base_kernel,
            (
                whole,
                whole,
                whole,
                shape(height, breadth),
                shape(height, frame),
                shape(height, frame),
                shape(8, LANES),
            ),
            [space(VMEM)] + [space(pl.ANY)] * 3 + [space(VMEM)] * 5 + [space(pl.ANY)],
            [space(pl.ANY)] * 2 + [space(VMEM)] * 5,
            [
                blocks,
                pltpu.VMEM((2, frame // LANES, frame + height, LANES), jnp.float32),
                pltpu.VMEM((2, frame, frame), jnp.float32),
                scalar,
                scalar,
                scalar,
                semaphores,
                pltpu.SemaphoreType.DMA((4,)),
            ],
            aliases={9: 1},
        )(place, slot_scan, received_scan, swapped_scan, table, staged, keep, light, plain, gradient)
        swapped_change = move(received_change, swap)
        updated, gradient = call(
            first_kernel,
            (whole, whole),
            [space(VMEM)] * 6 + [space(pl.ANY)] * 2,
            [space(pl.ANY)] * 2,
            [blocks, blocks, semaphores],
            aliases={6: 0, 7: 1},
        )(others, staged, total, weight, first, received_change, updated, gradient)
        return call(
            second_kernel,
            (whole, whole),
            [space(VMEM)] * 8 + [space(pl.ANY)] * 2,
            [space(pl.ANY)] * 2,
            [blocks, blocks, semaphores],
            aliases={8: 0, 9: 1},
        )(others, staged, total, weight, first, second, received_change, swapped_change, updated, gradient)

    return jax.shard_map(
        step,
        mesh=mesh,
        in_specs=(
            P(None, "tile", None),
            P("mode", None, None, None),
            P("tile", None, None),
            P(),
            P("tile"),
            P("tile"),
        ),
        out_specs=(P(None, "tile", None), P(None, "tile", None)),
        check_vma=False,
    )
```

```python
import math

import jax
import jax.numpy as jnp
import numpy as np
from jax import lax
from jax.experimental import pallas as pl
from jax.experimental.pallas import tpu as pltpu
from jax.sharding import PartitionSpec as P


FLOOR = 0.25
ALPHA = 0.5
LANES = 128
AXES = ("tile", "mode")
VMEM = pltpu.VMEM
SMEM = pltpu.SMEM


def split(value):
    high = value.astype(jnp.bfloat16)
    low = (value - high.astype(jnp.float32)).astype(jnp.bfloat16)
    return high, low


def matrices(frame):
    half = frame // 2
    pixel = np.arange(half)[:, None]
    wave = np.arange(half)[None, :]
    blocks = []
    for parity in (0, 1):
        phase = 2.0 * math.pi * (pixel * (2 * wave + parity) % frame) / frame
        cos, sin = np.cos(phase) / math.sqrt(frame), np.sin(phase) / math.sqrt(frame)
        forward = np.block([[cos, -sin], [sin, cos]])
        for table in (forward, forward.T):
            high = table.astype(jnp.bfloat16)
            blocks.append(high)
            blocks.append((table - high.astype(np.float64)).astype(jnp.bfloat16))
    return np.stack(blocks)


def lookup(table_ref, scan):
    base = pl.multiple_of((scan // LANES) * LANES, LANES)
    chunk = table_ref[:, pl.ds(base, LANES)].astype(jnp.float32)
    lane = lax.broadcasted_iota(jnp.int32, chunk.shape, 1)
    picked = jnp.where(lane == scan - base, chunk, 0.0)
    row = jnp.sum(picked[0:1]).astype(jnp.int32)
    col = jnp.sum(picked[1:2]).astype(jnp.int32)
    return row, col


def strip_window(object_ref, col):
    blocks = object_ref.shape[2] // LANES
    block, shift = col // LANES, col % LANES
    first = object_ref[:, :, pl.ds(pl.multiple_of(block * LANES, LANES), LANES)]
    second = object_ref[:, :, pl.ds(pl.multiple_of((block + 1) * LANES, LANES), LANES)]
    last = jnp.minimum(block + 2, blocks - 1)
    third = object_ref[:, :, pl.ds(pl.multiple_of(last * LANES, LANES), LANES)]
    lane = lax.broadcasted_iota(jnp.int32, first.shape, 2)
    return jnp.where(lane < shift, third, first), second


def fetch(pairs, sems, first=0):
    copies = [pltpu.make_async_copy(a, b, sems.at[first + index]) for index, (a, b) in enumerate(pairs)]
    for copy in copies:
        copy.start()
    return copies


def select_kernel(own_scan_ref, scan_ref, table_ref, object_ref, out_ref, found_ref):
    odd = lax.axis_index("tile") % 2 == 1
    got, own = lookup(table_ref, scan_ref[0]), lookup(table_ref, own_scan_ref[0])
    low, high = strip_window(object_ref, jnp.where(odd & (lax.axis_index("mode") == 1), own[1], got[1]))
    out_ref[:, :, :LANES] = low
    out_ref[:, :, LANES:] = high
    keep_scalars(found_ref, (*got, *own))


def slots(found_ref, swapped_ref):
    first = lax.axis_index("mode") == 0
    odd = lax.axis_index("tile") % 2 == 1

    def choose(flag, one, two):
        return tuple(jnp.where(flag, a, b) for a, b in zip(one, two))

    got = scalar_of(found_ref, 0), scalar_of(found_ref, 1)
    own = scalar_of(found_ref, 2), scalar_of(found_ref, 3)
    other = scalar_of(swapped_ref, 0), scalar_of(swapped_ref, 1)
    above, further = choose(first, got, other), choose(first, other, got)
    return choose(odd, further, own), above, choose(odd, own, further)


def keep_scalars(out_ref, values):
    for index, value in enumerate(values):
        row = jnp.full((1, out_ref.shape[1]), value, jnp.int32)
        out_ref[index : index + 1] = row.astype(jnp.float32)


def scalar_of(ref, index):
    return jnp.max(ref[index : index + 1]).astype(jnp.int32)


def within(place, strip, height):
    return jnp.clip(place[0] - strip * height, 0, height - 1), place[1]


def roll_into(out_ref, value, row, col, tall_ref):
    frame = value.shape[0]
    half = frame // 2
    turned = pltpu.roll(value, col, 1)
    for index in range(frame // LANES):
        at = slice(index * LANES, (index + 1) * LANES)
        tall_ref[index, :half] = turned[half:, at]
        tall_ref[index, half:] = turned[:, at]
        out_ref[:, at] = tall_ref[index, pl.ds(half - row, frame), :]


def reorder_kernel(own_ref, received_ref, swapped_ref, factor_ref, rows_ref):
    frame = own_ref.shape[1]
    odd = lax.axis_index("tile") % 2 == 1
    moved = jnp.where(lax.axis_index("mode") == 0, received_ref[0], swapped_ref[0])
    value = jnp.where(odd, moved, own_ref[0])
    source = lax.broadcasted_iota(jnp.int32, (frame, frame), 0)
    target = lax.broadcasted_iota(jnp.int32, (frame, frame), 1)
    half = frame // 2
    order = jnp.where(target < half, 2 * target, 2 * target - frame + 1)
    pick = jnp.where(source == order, 1.0, 0.0).astype(jnp.bfloat16)
    high = value.astype(jnp.bfloat16)
    rest = value - high.astype(jnp.float32)
    middle = rest.astype(jnp.bfloat16)
    low = (rest - middle.astype(jnp.float32)).astype(jnp.bfloat16)
    columns = jnp.dot(high, pick, preferred_element_type=jnp.float32)
    columns = columns + jnp.dot(middle, pick, preferred_element_type=jnp.float32)
    columns = columns + jnp.dot(low, pick, preferred_element_type=jnp.float32)
    for index in range(frame // LANES):
        at = slice(index * LANES, (index + 1) * LANES)
        rows_ref[index] = columns[:, at]
        factor_ref[:half, at] = rows_ref[index, pl.ds(0, half, stride=2), :]
        factor_ref[half:, at] = rows_ref[index, pl.ds(1, half, stride=2), :]


def probe_parts(own_probe_ref, other_probe_ref):
    modes = own_probe_ref.shape[0]
    return [ref.at[mode, part] for ref in (own_probe_ref, other_probe_ref) for mode in range(modes) for part in range(2)]


def fill_kernel(own_probe_ref, other_probe_ref, gradient_ref, total_ref, zero_ref, sems):
    zero_ref[...] = jnp.zeros_like(zero_ref)
    step = zero_ref.shape[0]
    copies = []
    for part in range(2):
        for at in range(0, gradient_ref.shape[1], step):
            copies += fetch([(zero_ref, gradient_ref.at[part, at : at + step])], sems, len(copies))
    total = jnp.zeros(total_ref.shape, jnp.float32)
    for source in probe_parts(own_probe_ref, other_probe_ref):
        total = total + source[...] * source[...]
    total_ref[...] = total
    for copy in copies:
        copy.wait()


def prepare_kernel(
    found_ref, swapped_ref, object_ref, own_probe_ref, other_probe_ref, total_ref,
    probe_ref, window_ref, light_ref, place_ref, tall_ref,
):
    sources = probe_parts(own_probe_ref, other_probe_ref)
    height = object_ref.shape[1]
    tile = lax.axis_index("tile")
    odd = tile % 2
    main, _, _ = slots(found_ref, swapped_ref)
    row, col = within(main, tile - 2 * odd, height)
    shift = col % LANES
    for index, source in enumerate(sources):
        roll_into(probe_ref.at[index // 2, index % 2], source[...], row, shift, tall_ref.at[index])
    roll_into(light_ref, total_ref[...], row, shift, tall_ref.at[len(sources)])
    low, high = strip_window(object_ref, col)
    window_ref[:, :, :LANES] = low
    window_ref[:, :, LANES:] = high
    live = jnp.where(odd == 1, (tile >= 2).astype(jnp.int32), 1)
    keep_scalars(place_ref, (jnp.where(odd == 1, 0, row), jnp.where(odd == 1, row, height), live))


def right(value, high, low):
    first, second = split(value)
    return jnp.dot(
        jnp.concatenate([first, second, first], axis=1),
        jnp.concatenate([high, high, low], axis=0),
        preferred_element_type=jnp.float32,
    )


def left(high, low, value):
    first, second = split(value)
    return jnp.dot(
        jnp.concatenate([high, high, low], axis=1),
        jnp.concatenate([first, second, first], axis=0),
        preferred_element_type=jnp.float32,
    )


def transform_rows(probe_ref, start, window_ref, matrix_ref, out_ref):
    modes = probe_ref.shape[0]
    height, frame = window_ref.shape[1:]
    half = frame // 2
    sums, differences = [], []
    for mode in range(modes):
        probe_re = probe_ref[mode, 0, pl.ds(start, height), :]
        probe_im = probe_ref[mode, 1, pl.ds(start, height), :]
        wave_re = probe_re * window_ref[0] - probe_im * window_ref[1]
        wave_im = probe_re * window_ref[1] + probe_im * window_ref[0]
        for pieces, sign in ((sums, 1.0), (differences, -1.0)):
            pieces.append(
                jnp.concatenate(
                    [wave_re[:, :half] + sign * wave_re[:, half:], wave_im[:, :half] + sign * wave_im[:, half:]],
                    axis=1,
                )
            )
    even = right(jnp.concatenate(sums, axis=0), matrix_ref[0], matrix_ref[1])
    odd = right(jnp.concatenate(differences, axis=0), matrix_ref[4], matrix_ref[5])
    for mode in range(modes):
        at = slice(mode * height, (mode + 1) * height)
        out_ref[mode, 0] = jnp.concatenate([even[at, :half], odd[at, :half]], axis=1)
        out_ref[mode, 1] = jnp.concatenate([even[at, half:], odd[at, half:]], axis=1)


def strip_kernel(own_ref, received_ref, probe_ref, matrix_ref, own_out_ref, out_ref):
    height = received_ref.shape[1]
    start = pl.multiple_of((1 - lax.axis_index("mode")) * height, height)
    transform_rows(probe_ref, 0, own_ref, matrix_ref, own_out_ref)
    transform_rows(probe_ref, start, received_ref, matrix_ref, out_ref)


def forward_kernel(
    place_ref, window_ref, received_ref, swapped_ref, own_ref, first_ref, probe_ref, light_ref, matrix_ref,
    known_ref, far_ref, intensity_ref, second_ref,
):
    modes, _, frame, _ = probe_ref.shape
    height = window_ref.shape[1]
    half = frame // 2
    core = lax.axis_index("mode")
    low, high = place_ref[0:1, :1].astype(jnp.int32), place_ref[1:2, :1].astype(jnp.int32)
    transform_rows(probe_ref, pl.multiple_of(core * height, height), swapped_ref, matrix_ref, second_ref)
    level = lax.broadcasted_iota(jnp.int32, (height, frame), 0)

    def assemble(own, got, given):
        nearer = jnp.where(core == 0, got, given)
        farther = jnp.where(core == 0, given, got)
        return jnp.where((level >= low) & (level < high), own, farther), nearer

    for part in range(2):
        top, bottom = assemble(window_ref[part], received_ref[part], swapped_ref[part])
        known_ref[part, :height] = top * light_ref[:height]
        known_ref[part, height:] = bottom * light_ref[height:]
    intensity = jnp.zeros((frame, frame), jnp.float32)
    for mode in range(modes):
        top_re, bottom_re = assemble(own_ref[mode, 0], first_ref[mode, 0], second_ref[mode, 0])
        top_im, bottom_im = assemble(own_ref[mode, 1], first_ref[mode, 1], second_ref[mode, 1])
        added = jnp.concatenate([top_re + bottom_re, top_im + bottom_im], axis=0)
        taken = jnp.concatenate([top_re - bottom_re, top_im - bottom_im], axis=0)
        even = left(matrix_ref[2], matrix_ref[3], added)
        odd = left(matrix_ref[6], matrix_ref[7], taken)
        far_ref[mode, 0] = even
        far_ref[mode, 1] = odd
        squares = jnp.concatenate(
            [even[:half] * even[:half] + even[half:] * even[half:], odd[:half] * odd[:half] + odd[half:] * odd[half:]],
            axis=0,
        )
        intensity = intensity + squares
    intensity_ref[...] = intensity


def inverse_kernel(
    place_ref, probe_ref, amplitude_ref, matrix_ref, known_ref, far_ref, intensity_ref, send_ref, keep_ref
):
    modes, _, frame, _ = probe_ref.shape
    height = keep_ref.shape[1]
    half = frame // 2
    core = lax.axis_index("mode")
    factor = amplitude_ref[...] * lax.rsqrt(jnp.maximum(intensity_ref[...], FLOOR))
    grad_re = jnp.zeros((frame, frame), jnp.float32)
    grad_im = jnp.zeros((frame, frame), jnp.float32)
    even_factor = jnp.concatenate([factor[:half], factor[:half]], axis=0)
    odd_factor = jnp.concatenate([factor[half:], factor[half:]], axis=0)
    evens, odds = [], []
    for mode in range(modes):
        even = left(matrix_ref[0], matrix_ref[1], far_ref[mode, 0] * even_factor)
        odd = left(matrix_ref[4], matrix_ref[5], far_ref[mode, 1] * odd_factor)
        top, bottom = even + odd, even - odd
        mid_re = jnp.concatenate([top[:half], bottom[:half]], axis=0)
        mid_im = jnp.concatenate([top[half:], bottom[half:]], axis=0)
        evens.append(jnp.concatenate([mid_re[:, :half], mid_im[:, :half]], axis=1))
        odds.append(jnp.concatenate([mid_re[:, half:], mid_im[:, half:]], axis=1))
    even = right(jnp.concatenate(evens, axis=0), matrix_ref[2], matrix_ref[3])
    odd = right(jnp.concatenate(odds, axis=0), matrix_ref[6], matrix_ref[7])
    fores, afts = even + odd, even - odd
    for mode in range(modes):
        fore = fores[mode * frame : (mode + 1) * frame]
        aft = afts[mode * frame : (mode + 1) * frame]
        back_re = jnp.concatenate([fore[:, :half], aft[:, :half]], axis=1)
        back_im = jnp.concatenate([fore[:, half:], aft[:, half:]], axis=1)
        probe_re, probe_im = probe_ref[mode, 0], probe_ref[mode, 1]
        grad_re = grad_re + (probe_re * back_re + probe_im * back_im)
        grad_im = grad_im + (probe_re * back_im - probe_im * back_re)
    live = place_ref[2:3, :1]
    grad_re = (grad_re - known_ref[0]) * live
    grad_im = (grad_im - known_ref[1]) * live
    send_ref[:height] = jnp.where(core == 0, grad_re[height:], grad_re[:height])
    send_ref[height : 2 * height] = jnp.where(core == 0, grad_im[height:], grad_im[:height])
    send_ref[2 * height :] = jnp.broadcast_to(live, (8, frame))
    keep_ref[0] = grad_re[:height]
    keep_ref[1] = grad_im[:height]


def covers(col, block, low, high, lane):
    start, shift = col // LANES, col % LANES
    distance = block - start
    value = jnp.where(distance == 1, high, low)
    first = jnp.where(distance == 0, shift, jnp.where(distance == 1, 0, LANES))
    last = jnp.where(distance == 2, shift, 0)
    keep = (lane >= first) | (lane < last)
    return jnp.where(keep, value, 0.0)


def base_kernel(
    place_ref, found_ref, swapped_ref, object_ref, keep_ref, light_ref, plain_ref,
    old_gradient_ref,
    updated_ref, gradient_ref, total_ref, weight_ref, first_ref, second_ref, others_ref, new_ref, tall_ref, turned_ref, sems, fills,
):
    del old_gradient_ref
    height, breadth = object_ref.shape[1:]
    tile = lax.axis_index("tile")
    core = lax.axis_index("mode")
    fill = pltpu.make_async_copy(object_ref, updated_ref, fills.at[0])
    fill.start()
    total_ref[...] = jnp.zeros_like(total_ref)
    weight_ref[...] = jnp.zeros_like(weight_ref)
    odd = tile % 2
    (_, col), above, third = slots(found_ref, swapped_ref)
    live = place_ref[2:3, :1]
    start, stop = place_ref[0:1, :1].astype(jnp.int32), place_ref[1:2, :1].astype(jnp.int32)
    lane = lax.broadcasted_iota(jnp.int32, (height, LANES), 1)
    level = lax.broadcasted_iota(jnp.int32, (height, LANES), 0)
    kept = (level >= start) & (level < stop)
    for slot in range(3):
        block = jnp.minimum(col // LANES + slot, breadth // LANES - 1)
        at = pl.ds(pl.multiple_of(block * LANES, LANES), LANES)
        light = covers(col, block, light_ref[:height, :LANES], light_ref[:height, LANES:], lane)
        weight = jnp.where(kept, light * live, 0.0)
        weight_ref[:, at] = weight
        scale = 1.0 / (weight + ALPHA)
        for part in range(2):
            change = covers(col, block, keep_ref[part, :, :LANES], keep_ref[part, :, LANES:], lane)
            change = jnp.where(kept, change, 0.0)
            total_ref[part, :, at] = change
            new_ref[slot, part] = object_ref[part, :, at] + change * scale
    places = []
    for place, strip, far in ((above, tile - 1, False), (third, tile - 2 + 2 * odd, True)):
        row, start = within(place, strip, height)
        index = int(far)
        roll_into(turned_ref.at[index], plain_ref[...], row, start % LANES, tall_ref.at[index])
        turned = turned_ref[index]
        begin = jnp.where(odd == 1, row, 0) if far else 0
        end = jnp.where(odd == 1, height, row) if far else height
        places.append((start, begin, end, turned[:height] if far else turned[height:]))
    chosen = []
    for slot, out_ref in ((0, first_ref), (1, second_ref)):
        direct = core == slot
        near, far = places
        out_ref[...] = jnp.where(direct, near[3], far[3])
        chosen += [jnp.where(direct, near[index], far[index]) for index in range(3)]
    keep_scalars(others_ref, chosen)
    fill.wait()
    copies = []
    for slot in range(3):
        block = jnp.minimum(col // LANES + slot, breadth // LANES - 1)
        at = pl.ds(pl.multiple_of(block * LANES, LANES), LANES)
        copies.append(write(slot, col, block, at, total_ref.at[:, :, at], new_ref, gradient_ref, updated_ref, sems))
    finish(copies)


def write(slot, col, block, at, source, new_ref, gradient_ref, updated_ref, sems):
    fresh = col // LANES + slot == block
    one = pltpu.make_async_copy(source, gradient_ref.at[:, :, at], sems.at[2 * slot])
    two = pltpu.make_async_copy(new_ref.at[slot], updated_ref.at[:, :, at], sems.at[2 * slot + 1])

    @pl.when(fresh)
    def _():
        one.start()
        two.start()

    return fresh, one, two


def finish(copies):
    for fresh, one, two in copies:

        @pl.when(fresh)
        def _(one=one, two=two):
            one.wait()
            two.wait()


def add_windows(windows, main, object_ref, total_ref, weight_ref, updated_ref, gradient_ref, new_ref, sum_ref, sems):
    height, breadth = object_ref.shape[1:]
    lane = lax.broadcasted_iota(jnp.int32, (height, LANES), 1)
    level = lax.broadcasted_iota(jnp.int32, (height, LANES), 0)
    col = windows[main][0]
    copies = []
    for slot in range(3):
        block = jnp.minimum(col // LANES + slot, breadth // LANES - 1)
        at = pl.ds(pl.multiple_of(block * LANES, LANES), LANES)
        weight = weight_ref[:, at]
        sums = [total_ref[0, :, at], total_ref[1, :, at]]
        for start, begin, end, light_ref, change_ref in windows:
            inside = (level >= begin) & (level < end)
            live = change_ref[2 * height : 2 * height + 1, :1]
            light = covers(start, block, light_ref[:, :LANES], light_ref[:, LANES:], lane)
            weight = weight + jnp.where(inside, light, 0.0) * live
            for part in range(2):
                rows = slice(part * height, (part + 1) * height)
                change = covers(start, block, change_ref[rows, :LANES], change_ref[rows, LANES:], lane)
                sums[part] = sums[part] + jnp.where(inside, change, 0.0)
        scale = 1.0 / (weight + ALPHA)
        for part in range(2):
            sum_ref[slot, part] = sums[part]
            new_ref[slot, part] = object_ref[part, :, at] + sums[part] * scale
        copies.append(write(slot, col, block, at, sum_ref.at[slot], new_ref, gradient_ref, updated_ref, sems))
    finish(copies)


def first_kernel(
    others_ref, object_ref, total_ref, weight_ref, first_ref, received_ref, old_updated_ref, old_gradient_ref,
    updated_ref, gradient_ref, new_ref, sum_ref, sems,
):
    del old_updated_ref, old_gradient_ref
    windows = [(*(scalar_of(others_ref, index) for index in range(3)), first_ref, received_ref)]
    add_windows(windows, 0, object_ref, total_ref, weight_ref, updated_ref, gradient_ref, new_ref, sum_ref, sems)


def second_kernel(
    others_ref, object_ref, total_ref, weight_ref, first_ref, second_ref, received_ref, swapped_ref,
    old_updated_ref, old_gradient_ref, updated_ref, gradient_ref, new_ref, sum_ref, sems,
):
    del old_updated_ref, old_gradient_ref
    windows = [
        (*(scalar_of(others_ref, index) for index in range(3)), first_ref, received_ref),
        (*(scalar_of(others_ref, index) for index in range(3, 6)), second_ref, swapped_ref),
    ]
    add_windows(windows, 1, object_ref, total_ref, weight_ref, updated_ref, gradient_ref, new_ref, sum_ref, sems)


def call(kernel, out_shape, in_specs, out_specs, scratch=(), mebibytes=16, aliases=None):
    return pl.pallas_call(
        kernel,
        out_shape=out_shape,
        in_specs=in_specs,
        out_specs=out_specs,
        scratch_shapes=list(scratch),
        input_output_aliases=aliases or {},
        compiler_params=pltpu.CompilerParams(vmem_limit_bytes=mebibytes << 20),
        cost_estimate=pl.CostEstimate(flops=5000000, bytes_accessed=5000000, transcendentals=0),
    )


def space(where):
    return pl.BlockSpec(memory_space=where)


def shape(*dims, dtype=jnp.float32):
    return jax.ShapeDtypeStruct(dims, dtype)


def solution(mesh):
    tiles, cores = mesh.shape["tile"], mesh.shape["mode"]
    up = [(2 * t, 2 * (t + 1)) for t in range(tiles - 1)] + [(2 * t + 1, 2 * (t + 2) + 1) for t in range(tiles - 2)]
    gather = [(2 * t, 2 * (t ^ 1)) for t in range(tiles)]
    gather += [(2 * t + 1, 2 * (t - 2) + 1) for t in range(2, tiles, 2)]
    gather += [(2 * t + 1, 2 * (t + 2) + 1) for t in range(1, tiles - 2, 2)]
    spread = [(target, source) for source, target in gather]
    onward = [(2 * t, 2 * (t + 2)) for t in range(1, tiles - 2, 2)]
    swap = [(2 * t + core, 2 * t + 1 - core) for t in range(tiles) for core in range(2)]
    assert cores == 2 and tiles % 2 == 0

    def move(value, pairs):
        return lax.ppermute(value, AXES, pairs)

    def step(object_tiles, probe_modes, amplitudes, scan_offsets, slot_scan, slot_count):
        height, breadth = object_tiles.shape[1:]
        modes, _, frame, _ = probe_modes.shape
        assert slot_scan.shape[0] == 1 and frame == 2 * height and height == LANES
        table = scan_offsets.T
        matrix = jnp.asarray(matrices(frame))
        received_scan = move(slot_scan, up)
        staged = move(object_tiles, swap)
        table = move(table, swap)
        other_probe = move(probe_modes, swap)
        received_amplitude = move(amplitudes, onward)
        window, found = call(
            select_kernel,
            (shape(2, height, frame), shape(8, LANES)),
            [space(SMEM)] * 2 + [space(VMEM)] * 2,
            [space(VMEM)] * 2,
        )(slot_scan, received_scan, table, staged)
        received = move(window, gather)
        swapped_found = move(found, swap)
        swapped_amplitude = move(received_amplitude, swap)
        strip = shape(2 * modes, 2, height, frame)
        whole = shape(2, height, breadth)
        gradient, plain = call(
            fill_kernel,
            (whole, shape(frame, frame)),
            [space(VMEM)] * 2,
            [space(pl.ANY), space(VMEM)],
            [pltpu.VMEM((height // 8, breadth), jnp.float32), pltpu.SemaphoreType.DMA((16,))],
        )(probe_modes, other_probe)
        probe, own_window, light, place = call(
            prepare_kernel,
            (
                shape(2 * modes, 2, frame, frame),
                shape(2, height, frame),
                shape(frame, frame),
                shape(8, LANES),
            ),
            [space(VMEM)] * 6,
            [space(VMEM)] * 4,
            [pltpu.VMEM((4 * modes + 1, frame // LANES, frame + height, LANES), jnp.float32)],
        )(found, swapped_found, staged, probe_modes, other_probe, plain)
        swapped = move(received, swap)
        amplitude = call(
            reorder_kernel,
            shape(frame, frame),
            [space(VMEM)] * 3,
            space(VMEM),
            [pltpu.VMEM((frame // LANES, frame, LANES), jnp.float32)],
        )(amplitudes, received_amplitude, swapped_amplitude)
        own_strip, first_strip = call(strip_kernel, (strip, strip), [space(VMEM)] * 4, [space(VMEM)] * 2)(
            own_window, received, probe, matrix
        )
        known, far, intensity = call(
            forward_kernel,
            (shape(2, frame, frame), shape(2 * modes, 2, frame, frame), shape(frame, frame)),
            [space(VMEM)] * 9,
            [space(VMEM)] * 3,
            [pltpu.VMEM((2 * modes, 2, height, frame), jnp.float32)],
        )(place, own_window, received, swapped, own_strip, first_strip, probe, light, matrix)
        send, keep = call(
            inverse_kernel,
            (shape(2 * height + 8, frame), shape(2, height, frame)),
            [space(VMEM)] * 7,
            [space(VMEM)] * 2,
        )(place, probe, amplitude, matrix, known, far, intensity)
        received_change = move(send, spread)
        blocks = pltpu.VMEM((3, 2, height, LANES), jnp.float32)
        semaphores = pltpu.SemaphoreType.DMA((6,))
        updated, gradient, total, weight, first, second, others = call(
            base_kernel,
            (
                whole,
                whole,
                whole,
                shape(height, breadth),
                shape(height, frame),
                shape(height, frame),
                shape(8, LANES),
            ),
            [space(VMEM)] * 7 + [space(pl.ANY)],
            [space(pl.ANY)] * 2 + [space(VMEM)] * 5,
            [
                blocks,
                pltpu.VMEM((2, frame // LANES, frame + height, LANES), jnp.float32),
                pltpu.VMEM((2, frame, frame), jnp.float32),
                semaphores,
                pltpu.SemaphoreType.DMA((1,)),
            ],
            aliases={7: 1},
        )(place, found, swapped_found, staged, keep, light, plain, gradient)
        swapped_change = move(received_change, swap)
        updated, gradient = call(
            first_kernel,
            (whole, whole),
            [space(VMEM)] * 6 + [space(pl.ANY)] * 2,
            [space(pl.ANY)] * 2,
            [blocks, blocks, semaphores],
            aliases={6: 0, 7: 1},
        )(others, staged, total, weight, first, received_change, updated, gradient)
        return call(
            second_kernel,
            (whole, whole),
            [space(VMEM)] * 8 + [space(pl.ANY)] * 2,
            [space(pl.ANY)] * 2,
            [blocks, blocks, semaphores],
            aliases={8: 0, 9: 1},
        )(others, staged, total, weight, first, second, received_change, swapped_change, updated, gradient)

    return jax.shard_map(
        step,
        mesh=mesh,
        in_specs=(
            P(None, "tile", None),
            P("mode", None, None, None),
            P("tile", None, None),
            P(),
            P("tile"),
            P("tile"),
        ),
        out_specs=(P(None, "tile", None), P(None, "tile", None)),
        check_vma=False,
    )
```

```python
import math

import jax
import jax.numpy as jnp
import numpy as np
from jax import lax
from jax.experimental import pallas as pl
from jax.experimental.pallas import tpu as pltpu
from jax.sharding import PartitionSpec as P


FLOOR = 0.25
ALPHA = 0.5
LANES = 128
AXES = ("tile", "mode")
VMEM = pltpu.VMEM
SMEM = pltpu.SMEM


def split(value):
    high = value.astype(jnp.bfloat16)
    low = (value - high.astype(jnp.float32)).astype(jnp.bfloat16)
    return high, low


def matrices(frame):
    half = frame // 2
    pixel = np.arange(half)[:, None]
    wave = np.arange(half)[None, :]
    blocks = []
    for parity in (0, 1):
        phase = 2.0 * math.pi * (pixel * (2 * wave + parity) % frame) / frame
        cos, sin = np.cos(phase) / math.sqrt(frame), np.sin(phase) / math.sqrt(frame)
        forward = np.block([[cos, -sin], [sin, cos]])
        for table in (forward, forward.T):
            high = table.astype(jnp.bfloat16)
            blocks.append(high)
            blocks.append((table - high.astype(np.float64)).astype(jnp.bfloat16))
    return np.stack(blocks)


def lookup(table_ref, scan):
    base = pl.multiple_of((scan // LANES) * LANES, LANES)
    chunk = table_ref[:, pl.ds(base, LANES)].astype(jnp.float32)
    lane = lax.broadcasted_iota(jnp.int32, chunk.shape, 1)
    picked = jnp.where(lane == scan - base, chunk, 0.0)
    row = jnp.sum(picked[0:1]).astype(jnp.int32)
    col = jnp.sum(picked[1:2]).astype(jnp.int32)
    return row, col


def strip_window(object_ref, col):
    blocks = object_ref.shape[2] // LANES
    block, shift = col // LANES, col % LANES
    first = object_ref[:, :, pl.ds(pl.multiple_of(block * LANES, LANES), LANES)]
    second = object_ref[:, :, pl.ds(pl.multiple_of((block + 1) * LANES, LANES), LANES)]
    last = jnp.minimum(block + 2, blocks - 1)
    third = object_ref[:, :, pl.ds(pl.multiple_of(last * LANES, LANES), LANES)]
    lane = lax.broadcasted_iota(jnp.int32, first.shape, 2)
    return jnp.where(lane < shift, third, first), second


def fetch(pairs, sems, first=0):
    copies = [pltpu.make_async_copy(a, b, sems.at[first + index]) for index, (a, b) in enumerate(pairs)]
    for copy in copies:
        copy.start()
    return copies


def select_kernel(own_scan_ref, scan_ref, table_ref, object_ref, out_ref, found_ref):
    odd = lax.axis_index("tile") % 2 == 1
    got, own = lookup(table_ref, scan_ref[0]), lookup(table_ref, own_scan_ref[0])
    low, high = strip_window(object_ref, jnp.where(odd & (lax.axis_index("mode") == 1), own[1], got[1]))
    out_ref[:, :, :LANES] = low
    out_ref[:, :, LANES:] = high
    keep_scalars(found_ref, (*got, *own))


def slots(found_ref, swapped_ref):
    first = lax.axis_index("mode") == 0
    odd = lax.axis_index("tile") % 2 == 1

    def choose(flag, one, two):
        return tuple(jnp.where(flag, a, b) for a, b in zip(one, two))

    got = scalar_of(found_ref, 0), scalar_of(found_ref, 1)
    own = scalar_of(found_ref, 2), scalar_of(found_ref, 3)
    other = scalar_of(swapped_ref, 0), scalar_of(swapped_ref, 1)
    above, further = choose(first, got, other), choose(first, other, got)
    return choose(odd, further, own), above, choose(odd, own, further)


def keep_scalars(out_ref, values):
    for index, value in enumerate(values):
        row = jnp.full((1, out_ref.shape[1]), value, jnp.int32)
        out_ref[index : index + 1] = row.astype(jnp.float32)


def scalar_of(ref, index):
    return jnp.max(ref[index : index + 1]).astype(jnp.int32)


def within(place, strip, height):
    return jnp.clip(place[0] - strip * height, 0, height - 1), place[1]


def roll_into(out_ref, value, row, col, tall_ref):
    frame = value.shape[0]
    half = frame // 2
    turned = pltpu.roll(value, col, 1)
    for index in range(frame // LANES):
        at = slice(index * LANES, (index + 1) * LANES)
        tall_ref[index, :half] = turned[half:, at]
        tall_ref[index, half:] = turned[:, at]
        out_ref[:, at] = tall_ref[index, pl.ds(half - row, frame), :]


def reorder_kernel(own_ref, received_ref, swapped_ref, factor_ref, rows_ref):
    frame = own_ref.shape[1]
    odd = lax.axis_index("tile") % 2 == 1
    moved = jnp.where(lax.axis_index("mode") == 0, received_ref[0], swapped_ref[0])
    value = jnp.where(odd, moved, own_ref[0])
    source = lax.broadcasted_iota(jnp.int32, (frame, frame), 0)
    target = lax.broadcasted_iota(jnp.int32, (frame, frame), 1)
    half = frame // 2
    order = jnp.where(target < half, 2 * target, 2 * target - frame + 1)
    pick = jnp.where(source == order, 1.0, 0.0).astype(jnp.bfloat16)
    high = value.astype(jnp.bfloat16)
    rest = value - high.astype(jnp.float32)
    middle = rest.astype(jnp.bfloat16)
    low = (rest - middle.astype(jnp.float32)).astype(jnp.bfloat16)
    columns = jnp.dot(high, pick, preferred_element_type=jnp.float32)
    columns = columns + jnp.dot(middle, pick, preferred_element_type=jnp.float32)
    columns = columns + jnp.dot(low, pick, preferred_element_type=jnp.float32)
    for index in range(frame // LANES):
        at = slice(index * LANES, (index + 1) * LANES)
        rows_ref[index] = columns[:, at]
        factor_ref[:half, at] = rows_ref[index, pl.ds(0, half, stride=2), :]
        factor_ref[half:, at] = rows_ref[index, pl.ds(1, half, stride=2), :]


def probe_parts(own_probe_ref, other_probe_ref):
    modes = own_probe_ref.shape[0]
    return [ref.at[mode, part] for ref in (own_probe_ref, other_probe_ref) for mode in range(modes) for part in range(2)]


def fill_kernel(own_probe_ref, other_probe_ref, gradient_ref, total_ref, zero_ref, sems):
    zero_ref[...] = jnp.zeros_like(zero_ref)
    step = zero_ref.shape[0]
    copies = []
    for part in range(2):
        for at in range(0, gradient_ref.shape[1], step):
            copies += fetch([(zero_ref, gradient_ref.at[part, at : at + step])], sems, len(copies))
    total = jnp.zeros(total_ref.shape, jnp.float32)
    for source in probe_parts(own_probe_ref, other_probe_ref):
        total = total + source[...] * source[...]
    total_ref[...] = total
    for copy in copies:
        copy.wait()


def prepare_kernel(
    found_ref, swapped_ref, object_ref, own_probe_ref, other_probe_ref, total_ref,
    probe_ref, window_ref, light_ref, place_ref, tall_ref,
):
    sources = probe_parts(own_probe_ref, other_probe_ref)
    height = object_ref.shape[1]
    tile = lax.axis_index("tile")
    odd = tile % 2
    main, _, _ = slots(found_ref, swapped_ref)
    row, col = within(main, tile - 2 * odd, height)
    shift = col % LANES
    for index, source in enumerate(sources):
        roll_into(probe_ref.at[index // 2, index % 2], source[...], row, shift, tall_ref.at[index])
    roll_into(light_ref, total_ref[...], row, shift, tall_ref.at[len(sources)])
    low, high = strip_window(object_ref, col)
    window_ref[:, :, :LANES] = low
    window_ref[:, :, LANES:] = high
    live = jnp.where(odd == 1, (tile >= 2).astype(jnp.int32), 1)
    keep_scalars(place_ref, (jnp.where(odd == 1, 0, row), jnp.where(odd == 1, row, height), live))


def right(value, high, low):
    first, second = split(value)
    return jnp.dot(
        jnp.concatenate([first, second, first], axis=1),
        jnp.concatenate([high, high, low], axis=0),
        preferred_element_type=jnp.float32,
    )


def left(high, low, value):
    first, second = split(value)
    return jnp.dot(
        jnp.concatenate([high, high, low], axis=1),
        jnp.concatenate([first, second, first], axis=0),
        preferred_element_type=jnp.float32,
    )


def transform_rows(probe_ref, start, window_ref, matrix_ref, out_ref):
    modes = probe_ref.shape[0]
    height, frame = window_ref.shape[1:]
    half = frame // 2
    sums, differences = [], []
    for mode in range(modes):
        probe_re = probe_ref[mode, 0, pl.ds(start, height), :]
        probe_im = probe_ref[mode, 1, pl.ds(start, height), :]
        wave_re = probe_re * window_ref[0] - probe_im * window_ref[1]
        wave_im = probe_re * window_ref[1] + probe_im * window_ref[0]
        for pieces, sign in ((sums, 1.0), (differences, -1.0)):
            pieces.append(
                jnp.concatenate(
                    [wave_re[:, :half] + sign * wave_re[:, half:], wave_im[:, :half] + sign * wave_im[:, half:]],
                    axis=1,
                )
            )
    even = right(jnp.concatenate(sums, axis=0), matrix_ref[0], matrix_ref[1])
    odd = right(jnp.concatenate(differences, axis=0), matrix_ref[4], matrix_ref[5])
    for mode in range(modes):
        at = slice(mode * height, (mode + 1) * height)
        out_ref[mode, 0] = jnp.concatenate([even[at, :half], odd[at, :half]], axis=1)
        out_ref[mode, 1] = jnp.concatenate([even[at, half:], odd[at, half:]], axis=1)


def strip_kernel(own_ref, received_ref, probe_ref, matrix_ref, own_out_ref, out_ref):
    height = received_ref.shape[1]
    start = pl.multiple_of((1 - lax.axis_index("mode")) * height, height)
    transform_rows(probe_ref, 0, own_ref, matrix_ref, own_out_ref)
    transform_rows(probe_ref, start, received_ref, matrix_ref, out_ref)


def wave_kernel(
    place_ref, window_ref, received_ref, swapped_ref, own_ref, first_ref, probe_ref, amplitude_ref, light_ref,
    matrix_ref, send_ref, keep_ref, patch_ref, far_ref, second_ref,
):
    modes, _, frame, _ = probe_ref.shape
    height = window_ref.shape[1]
    half = frame // 2
    core = lax.axis_index("mode")
    low, high = place_ref[0:1, :1].astype(jnp.int32), place_ref[1:2, :1].astype(jnp.int32)
    transform_rows(probe_ref, pl.multiple_of(core * height, height), swapped_ref, matrix_ref, second_ref)
    level = lax.broadcasted_iota(jnp.int32, (height, frame), 0)

    def assemble(own, got, given):
        nearer = jnp.where(core == 0, got, given)
        farther = jnp.where(core == 0, given, got)
        return jnp.where((level >= low) & (level < high), own, farther), nearer

    for part in range(2):
        top, bottom = assemble(window_ref[part], received_ref[part], swapped_ref[part])
        patch_ref[part, :height] = top
        patch_ref[part, height:] = bottom
    intensity = jnp.zeros((frame, frame), jnp.float32)
    for mode in range(modes):
        top_re, bottom_re = assemble(own_ref[mode, 0], first_ref[mode, 0], second_ref[mode, 0])
        top_im, bottom_im = assemble(own_ref[mode, 1], first_ref[mode, 1], second_ref[mode, 1])
        added = jnp.concatenate([top_re + bottom_re, top_im + bottom_im], axis=0)
        taken = jnp.concatenate([top_re - bottom_re, top_im - bottom_im], axis=0)
        even = left(matrix_ref[2], matrix_ref[3], added)
        odd = left(matrix_ref[6], matrix_ref[7], taken)
        far_ref[mode, 0] = even
        far_ref[mode, 1] = odd
        squares = jnp.concatenate(
            [even[:half] * even[:half] + even[half:] * even[half:], odd[:half] * odd[:half] + odd[half:] * odd[half:]],
            axis=0,
        )
        intensity = intensity + squares
    factor = amplitude_ref[...] * lax.rsqrt(jnp.maximum(intensity, FLOOR))
    grad_re = jnp.zeros((frame, frame), jnp.float32)
    grad_im = jnp.zeros((frame, frame), jnp.float32)
    even_factor = jnp.concatenate([factor[:half], factor[:half]], axis=0)
    odd_factor = jnp.concatenate([factor[half:], factor[half:]], axis=0)
    evens, odds = [], []
    for mode in range(modes):
        even = left(matrix_ref[0], matrix_ref[1], far_ref[mode, 0] * even_factor)
        odd = left(matrix_ref[4], matrix_ref[5], far_ref[mode, 1] * odd_factor)
        top, bottom = even + odd, even - odd
        mid_re = jnp.concatenate([top[:half], bottom[:half]], axis=0)
        mid_im = jnp.concatenate([top[half:], bottom[half:]], axis=0)
        evens.append(jnp.concatenate([mid_re[:, :half], mid_im[:, :half]], axis=1))
        odds.append(jnp.concatenate([mid_re[:, half:], mid_im[:, half:]], axis=1))
    even = right(jnp.concatenate(evens, axis=0), matrix_ref[2], matrix_ref[3])
    odd = right(jnp.concatenate(odds, axis=0), matrix_ref[6], matrix_ref[7])
    fores, afts = even + odd, even - odd
    for mode in range(modes):
        fore = fores[mode * frame : (mode + 1) * frame]
        aft = afts[mode * frame : (mode + 1) * frame]
        back_re = jnp.concatenate([fore[:, :half], aft[:, :half]], axis=1)
        back_im = jnp.concatenate([fore[:, half:], aft[:, half:]], axis=1)
        probe_re, probe_im = probe_ref[mode, 0], probe_ref[mode, 1]
        grad_re = grad_re + (probe_re * back_re + probe_im * back_im)
        grad_im = grad_im + (probe_re * back_im - probe_im * back_re)
    live = place_ref[2:3, :1]
    grad_re = (grad_re - light_ref[...] * patch_ref[0]) * live
    grad_im = (grad_im - light_ref[...] * patch_ref[1]) * live
    send_ref[:height] = jnp.where(core == 0, grad_re[height:], grad_re[:height])
    send_ref[height : 2 * height] = jnp.where(core == 0, grad_im[height:], grad_im[:height])
    send_ref[2 * height :] = jnp.broadcast_to(live, (8, frame))
    keep_ref[0] = grad_re[:height]
    keep_ref[1] = grad_im[:height]


def covers(col, block, low, high, lane):
    start, shift = col // LANES, col % LANES
    distance = block - start
    value = jnp.where(distance == 1, high, low)
    first = jnp.where(distance == 0, shift, jnp.where(distance == 1, 0, LANES))
    last = jnp.where(distance == 2, shift, 0)
    keep = (lane >= first) | (lane < last)
    return jnp.where(keep, value, 0.0)


def base_kernel(
    place_ref, found_ref, swapped_ref, object_ref, keep_ref, light_ref, plain_ref,
    old_gradient_ref,
    updated_ref, gradient_ref, total_ref, weight_ref, first_ref, second_ref, others_ref, new_ref, tall_ref, turned_ref, sems, fills,
):
    del old_gradient_ref
    height, breadth = object_ref.shape[1:]
    tile = lax.axis_index("tile")
    core = lax.axis_index("mode")
    fill = pltpu.make_async_copy(object_ref, updated_ref, fills.at[0])
    fill.start()
    total_ref[...] = jnp.zeros_like(total_ref)
    weight_ref[...] = jnp.zeros_like(weight_ref)
    odd = tile % 2
    (_, col), above, third = slots(found_ref, swapped_ref)
    live = place_ref[2:3, :1]
    start, stop = place_ref[0:1, :1].astype(jnp.int32), place_ref[1:2, :1].astype(jnp.int32)
    lane = lax.broadcasted_iota(jnp.int32, (height, LANES), 1)
    level = lax.broadcasted_iota(jnp.int32, (height, LANES), 0)
    kept = (level >= start) & (level < stop)
    for slot in range(3):
        block = jnp.minimum(col // LANES + slot, breadth // LANES - 1)
        at = pl.ds(pl.multiple_of(block * LANES, LANES), LANES)
        light = covers(col, block, light_ref[:height, :LANES], light_ref[:height, LANES:], lane)
        weight = jnp.where(kept, light * live, 0.0)
        weight_ref[:, at] = weight
        scale = 1.0 / (weight + ALPHA)
        for part in range(2):
            change = covers(col, block, keep_ref[part, :, :LANES], keep_ref[part, :, LANES:], lane)
            change = jnp.where(kept, change, 0.0)
            total_ref[part, :, at] = change
            new_ref[slot, part] = object_ref[part, :, at] + change * scale
    places = []
    for place, strip, far in ((above, tile - 1, False), (third, tile - 2 + 2 * odd, True)):
        row, start = within(place, strip, height)
        index = int(far)
        roll_into(turned_ref.at[index], plain_ref[...], row, start % LANES, tall_ref.at[index])
        turned = turned_ref[index]
        begin = jnp.where(odd == 1, row, 0) if far else 0
        end = jnp.where(odd == 1, height, row) if far else height
        places.append((start, begin, end, turned[:height] if far else turned[height:]))
    chosen = []
    for slot, out_ref in ((0, first_ref), (1, second_ref)):
        direct = core == slot
        near, far = places
        out_ref[...] = jnp.where(direct, near[3], far[3])
        chosen += [jnp.where(direct, near[index], far[index]) for index in range(3)]
    keep_scalars(others_ref, chosen)
    fill.wait()
    copies = []
    for slot in range(3):
        block = jnp.minimum(col // LANES + slot, breadth // LANES - 1)
        at = pl.ds(pl.multiple_of(block * LANES, LANES), LANES)
        copies.append(write(slot, col, block, at, total_ref.at[:, :, at], new_ref, gradient_ref, updated_ref, sems))
    finish(copies)


def write(slot, col, block, at, source, new_ref, gradient_ref, updated_ref, sems):
    fresh = col // LANES + slot == block
    one = pltpu.make_async_copy(source, gradient_ref.at[:, :, at], sems.at[2 * slot])
    two = pltpu.make_async_copy(new_ref.at[slot], updated_ref.at[:, :, at], sems.at[2 * slot + 1])

    @pl.when(fresh)
    def _():
        one.start()
        two.start()

    return fresh, one, two


def finish(copies):
    for fresh, one, two in copies:

        @pl.when(fresh)
        def _(one=one, two=two):
            one.wait()
            two.wait()


def add_windows(windows, main, object_ref, total_ref, weight_ref, updated_ref, gradient_ref, new_ref, sum_ref, sems):
    height, breadth = object_ref.shape[1:]
    lane = lax.broadcasted_iota(jnp.int32, (height, LANES), 1)
    level = lax.broadcasted_iota(jnp.int32, (height, LANES), 0)
    col = windows[main][0]
    copies = []
    for slot in range(3):
        block = jnp.minimum(col // LANES + slot, breadth // LANES - 1)
        at = pl.ds(pl.multiple_of(block * LANES, LANES), LANES)
        weight = weight_ref[:, at]
        sums = [total_ref[0, :, at], total_ref[1, :, at]]
        for start, begin, end, light_ref, change_ref in windows:
            inside = (level >= begin) & (level < end)
            live = change_ref[2 * height : 2 * height + 1, :1]
            light = covers(start, block, light_ref[:, :LANES], light_ref[:, LANES:], lane)
            weight = weight + jnp.where(inside, light, 0.0) * live
            for part in range(2):
                rows = slice(part * height, (part + 1) * height)
                change = covers(start, block, change_ref[rows, :LANES], change_ref[rows, LANES:], lane)
                sums[part] = sums[part] + jnp.where(inside, change, 0.0)
        scale = 1.0 / (weight + ALPHA)
        for part in range(2):
            sum_ref[slot, part] = sums[part]
            new_ref[slot, part] = object_ref[part, :, at] + sums[part] * scale
        copies.append(write(slot, col, block, at, sum_ref.at[slot], new_ref, gradient_ref, updated_ref, sems))
    finish(copies)


def first_kernel(
    others_ref, object_ref, total_ref, weight_ref, first_ref, received_ref, old_updated_ref, old_gradient_ref,
    updated_ref, gradient_ref, new_ref, sum_ref, sems,
):
    del old_updated_ref, old_gradient_ref
    windows = [(*(scalar_of(others_ref, index) for index in range(3)), first_ref, received_ref)]
    add_windows(windows, 0, object_ref, total_ref, weight_ref, updated_ref, gradient_ref, new_ref, sum_ref, sems)


def second_kernel(
    others_ref, object_ref, total_ref, weight_ref, first_ref, second_ref, received_ref, swapped_ref,
    old_updated_ref, old_gradient_ref, updated_ref, gradient_ref, new_ref, sum_ref, sems,
):
    del old_updated_ref, old_gradient_ref
    windows = [
        (*(scalar_of(others_ref, index) for index in range(3)), first_ref, received_ref),
        (*(scalar_of(others_ref, index) for index in range(3, 6)), second_ref, swapped_ref),
    ]
    add_windows(windows, 1, object_ref, total_ref, weight_ref, updated_ref, gradient_ref, new_ref, sum_ref, sems)


def call(kernel, out_shape, in_specs, out_specs, scratch=(), mebibytes=16, aliases=None):
    return pl.pallas_call(
        kernel,
        out_shape=out_shape,
        in_specs=in_specs,
        out_specs=out_specs,
        scratch_shapes=list(scratch),
        input_output_aliases=aliases or {},
        compiler_params=pltpu.CompilerParams(vmem_limit_bytes=mebibytes << 20),
        cost_estimate=pl.CostEstimate(flops=5000000, bytes_accessed=5000000, transcendentals=0),
    )


def space(where):
    return pl.BlockSpec(memory_space=where)


def shape(*dims, dtype=jnp.float32):
    return jax.ShapeDtypeStruct(dims, dtype)


def solution(mesh):
    tiles, cores = mesh.shape["tile"], mesh.shape["mode"]
    up = [(2 * t, 2 * (t + 1)) for t in range(tiles - 1)] + [(2 * t + 1, 2 * (t + 2) + 1) for t in range(tiles - 2)]
    gather = [(2 * t, 2 * (t ^ 1)) for t in range(tiles)]
    gather += [(2 * t + 1, 2 * (t - 2) + 1) for t in range(2, tiles, 2)]
    gather += [(2 * t + 1, 2 * (t + 2) + 1) for t in range(1, tiles - 2, 2)]
    spread = [(target, source) for source, target in gather]
    onward = [(2 * t, 2 * (t + 2)) for t in range(1, tiles - 2, 2)]
    swap = [(2 * t + core, 2 * t + 1 - core) for t in range(tiles) for core in range(2)]
    assert cores == 2 and tiles % 2 == 0

    def move(value, pairs):
        return lax.ppermute(value, AXES, pairs)

    def step(object_tiles, probe_modes, amplitudes, scan_offsets, slot_scan, slot_count):
        height, breadth = object_tiles.shape[1:]
        modes, _, frame, _ = probe_modes.shape
        assert slot_scan.shape[0] == 1 and frame == 2 * height and height == LANES
        table = scan_offsets.T
        matrix = jnp.asarray(matrices(frame))
        received_scan = move(slot_scan, up)
        staged = move(object_tiles, swap)
        table = move(table, swap)
        own_scan = move(slot_scan, swap)
        other_probe = move(probe_modes, swap)
        received_amplitude = move(amplitudes, onward)
        window, found = call(
            select_kernel,
            (shape(2, height, frame), shape(8, LANES)),
            [space(SMEM)] * 2 + [space(VMEM)] * 2,
            [space(VMEM)] * 2,
        )(own_scan, received_scan, table, staged)
        received = move(window, gather)
        swapped_found = move(found, swap)
        swapped_amplitude = move(received_amplitude, swap)
        strip = shape(2 * modes, 2, height, frame)
        whole = shape(2, height, breadth)
        gradient, plain = call(
            fill_kernel,
            (whole, shape(frame, frame)),
            [space(VMEM)] * 2,
            [space(pl.ANY), space(VMEM)],
            [pltpu.VMEM((height // 8, breadth), jnp.float32), pltpu.SemaphoreType.DMA((16,))],
        )(probe_modes, other_probe)
        probe, own_window, light, place = call(
            prepare_kernel,
            (
                shape(2 * modes, 2, frame, frame),
                shape(2, height, frame),
                shape(frame, frame),
                shape(8, LANES),
            ),
            [space(VMEM)] * 6,
            [space(VMEM)] * 4,
            [pltpu.VMEM((4 * modes + 1, frame // LANES, frame + height, LANES), jnp.float32)],
        )(found, swapped_found, staged, probe_modes, other_probe, plain)
        swapped = move(received, swap)
        amplitude = call(
            reorder_kernel,
            shape(frame, frame),
            [space(VMEM)] * 3,
            space(VMEM),
            [pltpu.VMEM((frame // LANES, frame, LANES), jnp.float32)],
        )(amplitudes, received_amplitude, swapped_amplitude)
        own_strip, first_strip = call(strip_kernel, (strip, strip), [space(VMEM)] * 4, [space(VMEM)] * 2)(
            own_window, received, probe, matrix
        )
        send, keep = call(
            wave_kernel,
            (shape(2 * height + 8, frame), shape(2, height, frame)),
            [space(VMEM)] * 10,
            [space(VMEM)] * 2,
            [
                pltpu.VMEM((2, frame, frame), jnp.float32),
                pltpu.VMEM((2 * modes, 2, frame, frame), jnp.float32),
                pltpu.VMEM((2 * modes, 2, height, frame), jnp.float32),
            ],
            mebibytes=24,
        )(place, own_window, received, swapped, own_strip, first_strip, probe, amplitude, light, matrix)
        received_change = move(send, spread)
        blocks = pltpu.VMEM((3, 2, height, LANES), jnp.float32)
        semaphores = pltpu.SemaphoreType.DMA((6,))
        updated, gradient, total, weight, first, second, others = call(
            base_kernel,
            (
                whole,
                whole,
                whole,
                shape(height, breadth),
                shape(height, frame),
                shape(height, frame),
                shape(8, LANES),
            ),
            [space(VMEM)] * 7 + [space(pl.ANY)],
            [space(pl.ANY)] * 2 + [space(VMEM)] * 5,
            [
                blocks,
                pltpu.VMEM((2, frame // LANES, frame + height, LANES), jnp.float32),
                pltpu.VMEM((2, frame, frame), jnp.float32),
                semaphores,
                pltpu.SemaphoreType.DMA((1,)),
            ],
            aliases={7: 1},
        )(place, found, swapped_found, staged, keep, light, plain, gradient)
        swapped_change = move(received_change, swap)
        updated, gradient = call(
            first_kernel,
            (whole, whole),
            [space(VMEM)] * 6 + [space(pl.ANY)] * 2,
            [space(pl.ANY)] * 2,
            [blocks, blocks, semaphores],
            aliases={6: 0, 7: 1},
        )(others, staged, total, weight, first, received_change, updated, gradient)
        return call(
            second_kernel,
            (whole, whole),
            [space(VMEM)] * 8 + [space(pl.ANY)] * 2,
            [space(pl.ANY)] * 2,
            [blocks, blocks, semaphores],
            aliases={8: 0, 9: 1},
        )(others, staged, total, weight, first, second, received_change, swapped_change, updated, gradient)

    return jax.shard_map(
        step,
        mesh=mesh,
        in_specs=(
            P(None, "tile", None),
            P("mode", None, None, None),
            P("tile", None, None),
            P(),
            P("tile"),
            P("tile"),
        ),
        out_specs=(P(None, "tile", None), P(None, "tile", None)),
        check_vma=False,
    )
```

```python
import math

import jax
import jax.numpy as jnp
import numpy as np
from jax import lax
from jax.experimental import pallas as pl
from jax.experimental.pallas import tpu as pltpu
from jax.sharding import PartitionSpec as P


FLOOR = 0.25
ALPHA = 0.5
LANES = 128
AXES = ("tile", "mode")
VMEM = pltpu.VMEM
SMEM = pltpu.SMEM


def split(value):
    high = value.astype(jnp.bfloat16)
    low = (value - high.astype(jnp.float32)).astype(jnp.bfloat16)
    return high, low


def matrices(frame):
    half = frame // 2
    pixel = np.arange(half)[:, None]
    wave = np.arange(half)[None, :]
    blocks = []
    for parity in (0, 1):
        phase = 2.0 * math.pi * (pixel * (2 * wave + parity) % frame) / frame
        cos, sin = np.cos(phase) / math.sqrt(frame), np.sin(phase) / math.sqrt(frame)
        forward = np.block([[cos, -sin], [sin, cos]])
        for table in (forward, forward.T):
            high = table.astype(jnp.bfloat16)
            blocks.append(high)
            blocks.append((table - high.astype(np.float64)).astype(jnp.bfloat16))
    return np.stack(blocks)


def lookup(table_ref, scan):
    base = pl.multiple_of((scan // LANES) * LANES, LANES)
    chunk = table_ref[:, pl.ds(base, LANES)].astype(jnp.float32)
    lane = lax.broadcasted_iota(jnp.int32, chunk.shape, 1)
    picked = jnp.where(lane == scan - base, chunk, 0.0)
    row = jnp.sum(picked[0:1]).astype(jnp.int32)
    col = jnp.sum(picked[1:2]).astype(jnp.int32)
    return row, col


def strip_window(object_ref, col):
    blocks = object_ref.shape[2] // LANES
    block, shift = col // LANES, col % LANES
    first = object_ref[:, :, pl.ds(pl.multiple_of(block * LANES, LANES), LANES)]
    second = object_ref[:, :, pl.ds(pl.multiple_of((block + 1) * LANES, LANES), LANES)]
    last = jnp.minimum(block + 2, blocks - 1)
    third = object_ref[:, :, pl.ds(pl.multiple_of(last * LANES, LANES), LANES)]
    lane = lax.broadcasted_iota(jnp.int32, first.shape, 2)
    return jnp.where(lane < shift, third, first), second


def fetch(pairs, sems, first=0):
    copies = [pltpu.make_async_copy(a, b, sems.at[first + index]) for index, (a, b) in enumerate(pairs)]
    for copy in copies:
        copy.start()
    return copies


def select_kernel(own_scan_ref, scan_ref, table_ref, object_ref, out_ref, found_ref):
    odd = lax.axis_index("tile") % 2 == 1
    got, own = lookup(table_ref, scan_ref[0]), lookup(table_ref, own_scan_ref[0])
    low, high = strip_window(object_ref, jnp.where(odd & (lax.axis_index("mode") == 1), own[1], got[1]))
    out_ref[:, :, :LANES] = low
    out_ref[:, :, LANES:] = high
    keep_scalars(found_ref, (*got, *own))


def slots(found_ref, swapped_ref):
    first = lax.axis_index("mode") == 0
    odd = lax.axis_index("tile") % 2 == 1

    def choose(flag, one, two):
        return tuple(jnp.where(flag, a, b) for a, b in zip(one, two))

    got = scalar_of(found_ref, 0), scalar_of(found_ref, 1)
    own = scalar_of(found_ref, 2), scalar_of(found_ref, 3)
    other = scalar_of(swapped_ref, 0), scalar_of(swapped_ref, 1)
    above, further = choose(first, got, other), choose(first, other, got)
    return choose(odd, further, own), above, choose(odd, own, further)


def keep_scalars(out_ref, values):
    for index, value in enumerate(values):
        row = jnp.full((1, out_ref.shape[1]), value, jnp.int32)
        out_ref[index : index + 1] = row.astype(jnp.float32)


def scalar_of(ref, index):
    return jnp.max(ref[index : index + 1]).astype(jnp.int32)


def within(place, strip, height):
    return jnp.clip(place[0] - strip * height, 0, height - 1), place[1]


def roll_into(out_ref, value, row, col, tall_ref):
    frame = value.shape[0]
    half = frame // 2
    turned = pltpu.roll(value, col, 1)
    for index in range(frame // LANES):
        at = slice(index * LANES, (index + 1) * LANES)
        tall_ref[index, :half] = turned[half:, at]
        tall_ref[index, half:] = turned[:, at]
        out_ref[:, at] = tall_ref[index, pl.ds(half - row, frame), :]


def reorder_kernel(own_ref, received_ref, swapped_ref, factor_ref, rows_ref):
    frame = own_ref.shape[1]
    odd = lax.axis_index("tile") % 2 == 1
    moved = jnp.where(lax.axis_index("mode") == 0, received_ref[0], swapped_ref[0])
    value = jnp.where(odd, moved, own_ref[0])
    source = lax.broadcasted_iota(jnp.int32, (frame, frame), 0)
    target = lax.broadcasted_iota(jnp.int32, (frame, frame), 1)
    half = frame // 2
    order = jnp.where(target < half, 2 * target, 2 * target - frame + 1)
    pick = jnp.where(source == order, 1.0, 0.0).astype(jnp.bfloat16)
    high = value.astype(jnp.bfloat16)
    rest = value - high.astype(jnp.float32)
    middle = rest.astype(jnp.bfloat16)
    low = (rest - middle.astype(jnp.float32)).astype(jnp.bfloat16)
    columns = jnp.dot(high, pick, preferred_element_type=jnp.float32)
    columns = columns + jnp.dot(middle, pick, preferred_element_type=jnp.float32)
    columns = columns + jnp.dot(low, pick, preferred_element_type=jnp.float32)
    for index in range(frame // LANES):
        at = slice(index * LANES, (index + 1) * LANES)
        rows_ref[index] = columns[:, at]
        factor_ref[:half, at] = rows_ref[index, pl.ds(0, half, stride=2), :]
        factor_ref[half:, at] = rows_ref[index, pl.ds(1, half, stride=2), :]


def probe_parts(own_probe_ref, other_probe_ref):
    modes = own_probe_ref.shape[0]
    return [ref.at[mode, part] for ref in (own_probe_ref, other_probe_ref) for mode in range(modes) for part in range(2)]


def fill_kernel(own_probe_ref, other_probe_ref, gradient_ref, total_ref, zero_ref, sems):
    zero_ref[...] = jnp.zeros_like(zero_ref)
    step = zero_ref.shape[0]
    copies = []
    for part in range(2):
        for at in range(0, gradient_ref.shape[1], step):
            copies += fetch([(zero_ref, gradient_ref.at[part, at : at + step])], sems, len(copies))
    total = jnp.zeros(total_ref.shape, jnp.float32)
    for source in probe_parts(own_probe_ref, other_probe_ref):
        total = total + source[...] * source[...]
    total_ref[...] = total
    for copy in copies:
        copy.wait()


def prepare_kernel(
    found_ref, swapped_ref, object_ref, own_probe_ref, other_probe_ref, total_ref, matrix_ref,
    probe_ref, window_ref, light_ref, place_ref, strip_ref, tall_ref,
):
    sources = probe_parts(own_probe_ref, other_probe_ref)
    height = object_ref.shape[1]
    tile = lax.axis_index("tile")
    odd = tile % 2
    main, _, _ = slots(found_ref, swapped_ref)
    row, col = within(main, tile - 2 * odd, height)
    shift = col % LANES
    for index, source in enumerate(sources):
        roll_into(probe_ref.at[index // 2, index % 2], source[...], row, shift, tall_ref.at[index])
    roll_into(light_ref, total_ref[...], row, shift, tall_ref.at[len(sources)])
    low, high = strip_window(object_ref, col)
    window_ref[:, :, :LANES] = low
    window_ref[:, :, LANES:] = high
    live = jnp.where(odd == 1, (tile >= 2).astype(jnp.int32), 1)
    keep_scalars(place_ref, (jnp.where(odd == 1, 0, row), jnp.where(odd == 1, row, height), live))
    transform_rows(probe_ref, 0, window_ref, matrix_ref, strip_ref)


def right(value, high, low):
    first, second = split(value)
    return jnp.dot(
        jnp.concatenate([first, second, first], axis=1),
        jnp.concatenate([high, high, low], axis=0),
        preferred_element_type=jnp.float32,
    )


def left(high, low, value):
    first, second = split(value)
    return jnp.dot(
        jnp.concatenate([high, high, low], axis=1),
        jnp.concatenate([first, second, first], axis=0),
        preferred_element_type=jnp.float32,
    )


def transform_rows(probe_ref, start, window_ref, matrix_ref, out_ref):
    modes = probe_ref.shape[0]
    height, frame = window_ref.shape[1:]
    half = frame // 2
    sums, differences = [], []
    for mode in range(modes):
        probe_re = probe_ref[mode, 0, pl.ds(start, height), :]
        probe_im = probe_ref[mode, 1, pl.ds(start, height), :]
        wave_re = probe_re * window_ref[0] - probe_im * window_ref[1]
        wave_im = probe_re * window_ref[1] + probe_im * window_ref[0]
        for pieces, sign in ((sums, 1.0), (differences, -1.0)):
            pieces.append(
                jnp.concatenate(
                    [wave_re[:, :half] + sign * wave_re[:, half:], wave_im[:, :half] + sign * wave_im[:, half:]],
                    axis=1,
                )
            )
    even = right(jnp.concatenate(sums, axis=0), matrix_ref[0], matrix_ref[1])
    odd = right(jnp.concatenate(differences, axis=0), matrix_ref[4], matrix_ref[5])
    for mode in range(modes):
        at = slice(mode * height, (mode + 1) * height)
        out_ref[mode, 0] = jnp.concatenate([even[at, :half], odd[at, :half]], axis=1)
        out_ref[mode, 1] = jnp.concatenate([even[at, half:], odd[at, half:]], axis=1)


def strip_kernel(received_ref, probe_ref, matrix_ref, out_ref):
    height = received_ref.shape[1]
    start = pl.multiple_of((1 - lax.axis_index("mode")) * height, height)
    transform_rows(probe_ref, start, received_ref, matrix_ref, out_ref)


def wave_kernel(
    place_ref, window_ref, received_ref, swapped_ref, own_ref, first_ref, probe_ref, amplitude_ref, light_ref,
    matrix_ref, send_ref, keep_ref, patch_ref, far_ref, second_ref,
):
    modes, _, frame, _ = probe_ref.shape
    height = window_ref.shape[1]
    half = frame // 2
    core = lax.axis_index("mode")
    low, high = place_ref[0:1, :1].astype(jnp.int32), place_ref[1:2, :1].astype(jnp.int32)
    transform_rows(probe_ref, pl.multiple_of(core * height, height), swapped_ref, matrix_ref, second_ref)
    level = lax.broadcasted_iota(jnp.int32, (height, frame), 0)

    def assemble(own, got, given):
        nearer = jnp.where(core == 0, got, given)
        farther = jnp.where(core == 0, given, got)
        return jnp.where((level >= low) & (level < high), own, farther), nearer

    for part in range(2):
        top, bottom = assemble(window_ref[part], received_ref[part], swapped_ref[part])
        patch_ref[part, :height] = top
        patch_ref[part, height:] = bottom
    intensity = jnp.zeros((frame, frame), jnp.float32)
    for mode in range(modes):
        top_re, bottom_re = assemble(own_ref[mode, 0], first_ref[mode, 0], second_ref[mode, 0])
        top_im, bottom_im = assemble(own_ref[mode, 1], first_ref[mode, 1], second_ref[mode, 1])
        added = jnp.concatenate([top_re + bottom_re, top_im + bottom_im], axis=0)
        taken = jnp.concatenate([top_re - bottom_re, top_im - bottom_im], axis=0)
        even = left(matrix_ref[2], matrix_ref[3], added)
        odd = left(matrix_ref[6], matrix_ref[7], taken)
        far_ref[mode, 0] = even
        far_ref[mode, 1] = odd
        squares = jnp.concatenate(
            [even[:half] * even[:half] + even[half:] * even[half:], odd[:half] * odd[:half] + odd[half:] * odd[half:]],
            axis=0,
        )
        intensity = intensity + squares
    factor = amplitude_ref[...] * lax.rsqrt(jnp.maximum(intensity, FLOOR))
    grad_re = jnp.zeros((frame, frame), jnp.float32)
    grad_im = jnp.zeros((frame, frame), jnp.float32)
    even_factor = jnp.concatenate([factor[:half], factor[:half]], axis=0)
    odd_factor = jnp.concatenate([factor[half:], factor[half:]], axis=0)
    evens, odds = [], []
    for mode in range(modes):
        even = left(matrix_ref[0], matrix_ref[1], far_ref[mode, 0] * even_factor)
        odd = left(matrix_ref[4], matrix_ref[5], far_ref[mode, 1] * odd_factor)
        top, bottom = even + odd, even - odd
        mid_re = jnp.concatenate([top[:half], bottom[:half]], axis=0)
        mid_im = jnp.concatenate([top[half:], bottom[half:]], axis=0)
        evens.append(jnp.concatenate([mid_re[:, :half], mid_im[:, :half]], axis=1))
        odds.append(jnp.concatenate([mid_re[:, half:], mid_im[:, half:]], axis=1))
    even = right(jnp.concatenate(evens, axis=0), matrix_ref[2], matrix_ref[3])
    odd = right(jnp.concatenate(odds, axis=0), matrix_ref[6], matrix_ref[7])
    fores, afts = even + odd, even - odd
    for mode in range(modes):
        fore = fores[mode * frame : (mode + 1) * frame]
        aft = afts[mode * frame : (mode + 1) * frame]
        back_re = jnp.concatenate([fore[:, :half], aft[:, :half]], axis=1)
        back_im = jnp.concatenate([fore[:, half:], aft[:, half:]], axis=1)
        probe_re, probe_im = probe_ref[mode, 0], probe_ref[mode, 1]
        grad_re = grad_re + (probe_re * back_re + probe_im * back_im)
        grad_im = grad_im + (probe_re * back_im - probe_im * back_re)
    live = place_ref[2:3, :1]
    grad_re = (grad_re - light_ref[...] * patch_ref[0]) * live
    grad_im = (grad_im - light_ref[...] * patch_ref[1]) * live
    send_ref[:height] = jnp.where(core == 0, grad_re[height:], grad_re[:height])
    send_ref[height : 2 * height] = jnp.where(core == 0, grad_im[height:], grad_im[:height])
    send_ref[2 * height :] = jnp.broadcast_to(live, (8, frame))
    keep_ref[0] = grad_re[:height]
    keep_ref[1] = grad_im[:height]


def covers(col, block, low, high, lane):
    start, shift = col // LANES, col % LANES
    distance = block - start
    value = jnp.where(distance == 1, high, low)
    first = jnp.where(distance == 0, shift, jnp.where(distance == 1, 0, LANES))
    last = jnp.where(distance == 2, shift, 0)
    keep = (lane >= first) | (lane < last)
    return jnp.where(keep, value, 0.0)


def base_kernel(
    place_ref, found_ref, swapped_ref, object_ref, keep_ref, light_ref, plain_ref,
    old_gradient_ref,
    updated_ref, gradient_ref, total_ref, weight_ref, first_ref, second_ref, others_ref, new_ref, tall_ref, turned_ref, sems, fills,
):
    del old_gradient_ref
    height, breadth = object_ref.shape[1:]
    tile = lax.axis_index("tile")
    core = lax.axis_index("mode")
    fill = pltpu.make_async_copy(object_ref, updated_ref, fills.at[0])
    fill.start()
    total_ref[...] = jnp.zeros_like(total_ref)
    weight_ref[...] = jnp.zeros_like(weight_ref)
    odd = tile % 2
    (_, col), above, third = slots(found_ref, swapped_ref)
    live = place_ref[2:3, :1]
    start, stop = place_ref[0:1, :1].astype(jnp.int32), place_ref[1:2, :1].astype(jnp.int32)
    lane = lax.broadcasted_iota(jnp.int32, (height, LANES), 1)
    level = lax.broadcasted_iota(jnp.int32, (height, LANES), 0)
    kept = (level >= start) & (level < stop)
    for slot in range(3):
        block = jnp.minimum(col // LANES + slot, breadth // LANES - 1)
        at = pl.ds(pl.multiple_of(block * LANES, LANES), LANES)
        light = covers(col, block, light_ref[:height, :LANES], light_ref[:height, LANES:], lane)
        weight = jnp.where(kept, light * live, 0.0)
        weight_ref[:, at] = weight
        scale = 1.0 / (weight + ALPHA)
        for part in range(2):
            change = covers(col, block, keep_ref[part, :, :LANES], keep_ref[part, :, LANES:], lane)
            change = jnp.where(kept, change, 0.0)
            total_ref[part, :, at] = change
            new_ref[slot, part] = object_ref[part, :, at] + change * scale
    places = []
    for place, strip, far in ((above, tile - 1, False), (third, tile - 2 + 2 * odd, True)):
        row, start = within(place, strip, height)
        index = int(far)
        roll_into(turned_ref.at[index], plain_ref[...], row, start % LANES, tall_ref.at[index])
        turned = turned_ref[index]
        begin = jnp.where(odd == 1, row, 0) if far else 0
        end = jnp.where(odd == 1, height, row) if far else height
        places.append((start, begin, end, turned[:height] if far else turned[height:]))
    chosen = []
    for slot, out_ref in ((0, first_ref), (1, second_ref)):
        direct = core == slot
        near, far = places
        out_ref[...] = jnp.where(direct, near[3], far[3])
        chosen += [jnp.where(direct, near[index], far[index]) for index in range(3)]
    keep_scalars(others_ref, chosen)
    fill.wait()
    copies = []
    for slot in range(3):
        block = jnp.minimum(col // LANES + slot, breadth // LANES - 1)
        at = pl.ds(pl.multiple_of(block * LANES, LANES), LANES)
        copies.append(write(slot, col, block, at, total_ref.at[:, :, at], new_ref, gradient_ref, updated_ref, sems))
    finish(copies)


def write(slot, col, block, at, source, new_ref, gradient_ref, updated_ref, sems):
    fresh = col // LANES + slot == block
    one = pltpu.make_async_copy(source, gradient_ref.at[:, :, at], sems.at[2 * slot])
    two = pltpu.make_async_copy(new_ref.at[slot], updated_ref.at[:, :, at], sems.at[2 * slot + 1])

    @pl.when(fresh)
    def _():
        one.start()
        two.start()

    return fresh, one, two


def finish(copies):
    for fresh, one, two in copies:

        @pl.when(fresh)
        def _(one=one, two=two):
            one.wait()
            two.wait()


def add_windows(windows, main, object_ref, total_ref, weight_ref, updated_ref, gradient_ref, new_ref, sum_ref, sems):
    height, breadth = object_ref.shape[1:]
    lane = lax.broadcasted_iota(jnp.int32, (height, LANES), 1)
    level = lax.broadcasted_iota(jnp.int32, (height, LANES), 0)
    col = windows[main][0]
    copies = []
    for slot in range(3):
        block = jnp.minimum(col // LANES + slot, breadth // LANES - 1)
        at = pl.ds(pl.multiple_of(block * LANES, LANES), LANES)
        weight = weight_ref[:, at]
        sums = [total_ref[0, :, at], total_ref[1, :, at]]
        for start, begin, end, light_ref, change_ref in windows:
            inside = (level >= begin) & (level < end)
            live = change_ref[2 * height : 2 * height + 1, :1]
            light = covers(start, block, light_ref[:, :LANES], light_ref[:, LANES:], lane)
            weight = weight + jnp.where(inside, light, 0.0) * live
            for part in range(2):
                rows = slice(part * height, (part + 1) * height)
                change = covers(start, block, change_ref[rows, :LANES], change_ref[rows, LANES:], lane)
                sums[part] = sums[part] + jnp.where(inside, change, 0.0)
        scale = 1.0 / (weight + ALPHA)
        for part in range(2):
            sum_ref[slot, part] = sums[part]
            new_ref[slot, part] = object_ref[part, :, at] + sums[part] * scale
        copies.append(write(slot, col, block, at, sum_ref.at[slot], new_ref, gradient_ref, updated_ref, sems))
    finish(copies)


def first_kernel(
    others_ref, object_ref, total_ref, weight_ref, first_ref, received_ref, old_updated_ref, old_gradient_ref,
    updated_ref, gradient_ref, new_ref, sum_ref, sems,
):
    del old_updated_ref, old_gradient_ref
    windows = [(*(scalar_of(others_ref, index) for index in range(3)), first_ref, received_ref)]
    add_windows(windows, 0, object_ref, total_ref, weight_ref, updated_ref, gradient_ref, new_ref, sum_ref, sems)


def second_kernel(
    others_ref, object_ref, total_ref, weight_ref, first_ref, second_ref, received_ref, swapped_ref,
    old_updated_ref, old_gradient_ref, updated_ref, gradient_ref, new_ref, sum_ref, sems,
):
    del old_updated_ref, old_gradient_ref
    windows = [
        (*(scalar_of(others_ref, index) for index in range(3)), first_ref, received_ref),
        (*(scalar_of(others_ref, index) for index in range(3, 6)), second_ref, swapped_ref),
    ]
    add_windows(windows, 1, object_ref, total_ref, weight_ref, updated_ref, gradient_ref, new_ref, sum_ref, sems)


def call(kernel, out_shape, in_specs, out_specs, scratch=(), mebibytes=16, aliases=None):
    return pl.pallas_call(
        kernel,
        out_shape=out_shape,
        in_specs=in_specs,
        out_specs=out_specs,
        scratch_shapes=list(scratch),
        input_output_aliases=aliases or {},
        compiler_params=pltpu.CompilerParams(vmem_limit_bytes=mebibytes << 20),
        cost_estimate=pl.CostEstimate(flops=5000000, bytes_accessed=5000000, transcendentals=0),
    )


def space(where):
    return pl.BlockSpec(memory_space=where)


def shape(*dims, dtype=jnp.float32):
    return jax.ShapeDtypeStruct(dims, dtype)


def solution(mesh):
    tiles, cores = mesh.shape["tile"], mesh.shape["mode"]
    up = [(2 * t, 2 * (t + 1)) for t in range(tiles - 1)] + [(2 * t + 1, 2 * (t + 2) + 1) for t in range(tiles - 2)]
    gather = [(2 * t, 2 * (t ^ 1)) for t in range(tiles)]
    gather += [(2 * t + 1, 2 * (t - 2) + 1) for t in range(2, tiles, 2)]
    gather += [(2 * t + 1, 2 * (t + 2) + 1) for t in range(1, tiles - 2, 2)]
    spread = [(target, source) for source, target in gather]
    onward = [(2 * t, 2 * (t + 2)) for t in range(1, tiles - 2, 2)]
    swap = [(2 * t + core, 2 * t + 1 - core) for t in range(tiles) for core in range(2)]
    assert cores == 2 and tiles % 2 == 0

    def move(value, pairs):
        return lax.ppermute(value, AXES, pairs)

    def step(object_tiles, probe_modes, amplitudes, scan_offsets, slot_scan, slot_count):
        height, breadth = object_tiles.shape[1:]
        modes, _, frame, _ = probe_modes.shape
        assert slot_scan.shape[0] == 1 and frame == 2 * height and height == LANES
        table = scan_offsets.T
        matrix = jnp.asarray(matrices(frame))
        received_scan = move(slot_scan, up)
        staged = move(object_tiles, swap)
        table = move(table, swap)
        other_probe = move(probe_modes, swap)
        received_amplitude = move(amplitudes, onward)
        window, found = call(
            select_kernel,
            (shape(2, height, frame), shape(8, LANES)),
            [space(SMEM)] * 2 + [space(VMEM)] * 2,
            [space(VMEM)] * 2,
        )(slot_scan, received_scan, table, staged)
        received = move(window, gather)
        swapped_found = move(found, swap)
        swapped_amplitude = move(received_amplitude, swap)
        strip = shape(2 * modes, 2, height, frame)
        whole = shape(2, height, breadth)
        gradient, plain = call(
            fill_kernel,
            (whole, shape(frame, frame)),
            [space(VMEM)] * 2,
            [space(pl.ANY), space(VMEM)],
            [pltpu.VMEM((height // 8, breadth), jnp.float32), pltpu.SemaphoreType.DMA((16,))],
        )(probe_modes, other_probe)
        probe, own_window, light, place, own_strip = call(
            prepare_kernel,
            (
                shape(2 * modes, 2, frame, frame),
                shape(2, height, frame),
                shape(frame, frame),
                shape(8, LANES),
                strip,
            ),
            [space(VMEM)] * 7,
            [space(VMEM)] * 5,
            [pltpu.VMEM((4 * modes + 1, frame // LANES, frame + height, LANES), jnp.float32)],
        )(found, swapped_found, staged, probe_modes, other_probe, plain, matrix)
        swapped = move(received, swap)
        amplitude = call(
            reorder_kernel,
            shape(frame, frame),
            [space(VMEM)] * 3,
            space(VMEM),
            [pltpu.VMEM((frame // LANES, frame, LANES), jnp.float32)],
        )(amplitudes, received_amplitude, swapped_amplitude)
        first_strip = call(strip_kernel, strip, [space(VMEM)] * 3, space(VMEM))(received, probe, matrix)
        send, keep = call(
            wave_kernel,
            (shape(2 * height + 8, frame), shape(2, height, frame)),
            [space(VMEM)] * 10,
            [space(VMEM)] * 2,
            [
                pltpu.VMEM((2, frame, frame), jnp.float32),
                pltpu.VMEM((2 * modes, 2, frame, frame), jnp.float32),
                pltpu.VMEM((2 * modes, 2, height, frame), jnp.float32),
            ],
            mebibytes=24,
        )(place, own_window, received, swapped, own_strip, first_strip, probe, amplitude, light, matrix)
        received_change = move(send, spread)
        blocks = pltpu.VMEM((3, 2, height, LANES), jnp.float32)
        semaphores = pltpu.SemaphoreType.DMA((6,))
        updated, gradient, total, weight, first, second, others = call(
            base_kernel,
            (
                whole,
                whole,
                whole,
                shape(height, breadth),
                shape(height, frame),
                shape(height, frame),
                shape(8, LANES),
            ),
            [space(VMEM)] * 7 + [space(pl.ANY)],
            [space(pl.ANY)] * 2 + [space(VMEM)] * 5,
            [
                blocks,
                pltpu.VMEM((2, frame // LANES, frame + height, LANES), jnp.float32),
                pltpu.VMEM((2, frame, frame), jnp.float32),
                semaphores,
                pltpu.SemaphoreType.DMA((1,)),
            ],
            aliases={7: 1},
        )(place, found, swapped_found, staged, keep, light, plain, gradient)
        swapped_change = move(received_change, swap)
        updated, gradient = call(
            first_kernel,
            (whole, whole),
            [space(VMEM)] * 6 + [space(pl.ANY)] * 2,
            [space(pl.ANY)] * 2,
            [blocks, blocks, semaphores],
            aliases={6: 0, 7: 1},
        )(others, staged, total, weight, first, received_change, updated, gradient)
        return call(
            second_kernel,
            (whole, whole),
            [space(VMEM)] * 8 + [space(pl.ANY)] * 2,
            [space(pl.ANY)] * 2,
            [blocks, blocks, semaphores],
            aliases={8: 0, 9: 1},
        )(others, staged, total, weight, first, second, received_change, swapped_change, updated, gradient)

    return jax.shard_map(
        step,
        mesh=mesh,
        in_specs=(
            P(None, "tile", None),
            P("mode", None, None, None),
            P("tile", None, None),
            P(),
            P("tile"),
            P("tile"),
        ),
        out_specs=(P(None, "tile", None), P(None, "tile", None)),
        check_vma=False,
    )
```

```python
import math

import jax
import jax.numpy as jnp
import numpy as np
from jax import lax
from jax.experimental import pallas as pl
from jax.experimental.pallas import tpu as pltpu
from jax.sharding import PartitionSpec as P


FLOOR = 0.25
ALPHA = 0.5
LANES = 128
AXES = ("tile", "mode")
VMEM = pltpu.VMEM
SMEM = pltpu.SMEM


def split(value):
    high = value.astype(jnp.bfloat16)
    low = (value - high.astype(jnp.float32)).astype(jnp.bfloat16)
    return high, low


def matrices(frame):
    half = frame // 2
    pixel = np.arange(half)[:, None]
    wave = np.arange(half)[None, :]
    blocks = []
    for parity in (0, 1):
        phase = 2.0 * math.pi * (pixel * (2 * wave + parity) % frame) / frame
        cos, sin = np.cos(phase) / math.sqrt(frame), np.sin(phase) / math.sqrt(frame)
        forward = np.block([[cos, -sin], [sin, cos]])
        for table in (forward, forward.T):
            high = table.astype(jnp.bfloat16)
            blocks.append(high)
            blocks.append((table - high.astype(np.float64)).astype(jnp.bfloat16))
    return np.stack(blocks)


def lookup(table_ref, scan):
    base = pl.multiple_of((scan // LANES) * LANES, LANES)
    chunk = table_ref[:, pl.ds(base, LANES)].astype(jnp.float32)
    lane = lax.broadcasted_iota(jnp.int32, chunk.shape, 1)
    picked = jnp.where(lane == scan - base, chunk, 0.0)
    row = jnp.sum(picked[0:1]).astype(jnp.int32)
    col = jnp.sum(picked[1:2]).astype(jnp.int32)
    return row, col


def strip_window(object_ref, col):
    blocks = object_ref.shape[2] // LANES
    block, shift = col // LANES, col % LANES
    first = object_ref[:, :, pl.ds(pl.multiple_of(block * LANES, LANES), LANES)]
    second = object_ref[:, :, pl.ds(pl.multiple_of((block + 1) * LANES, LANES), LANES)]
    last = jnp.minimum(block + 2, blocks - 1)
    third = object_ref[:, :, pl.ds(pl.multiple_of(last * LANES, LANES), LANES)]
    lane = lax.broadcasted_iota(jnp.int32, first.shape, 2)
    return jnp.where(lane < shift, third, first), second


def fetch(pairs, sems, first=0):
    copies = [pltpu.make_async_copy(a, b, sems.at[first + index]) for index, (a, b) in enumerate(pairs)]
    for copy in copies:
        copy.start()
    return copies


def select_kernel(own_scan_ref, scan_ref, table_ref, object_ref, out_ref, found_ref):
    odd = lax.axis_index("tile") % 2 == 1
    got, own = lookup(table_ref, scan_ref[0]), lookup(table_ref, own_scan_ref[0])
    low, high = strip_window(object_ref, jnp.where(odd & (lax.axis_index("mode") == 1), own[1], got[1]))
    out_ref[:, :, :LANES] = low
    out_ref[:, :, LANES:] = high
    keep_scalars(found_ref, (*got, *own))


def slots(found_ref, swapped_ref):
    first = lax.axis_index("mode") == 0
    odd = lax.axis_index("tile") % 2 == 1

    def choose(flag, one, two):
        return tuple(jnp.where(flag, a, b) for a, b in zip(one, two))

    got = scalar_of(found_ref, 0), scalar_of(found_ref, 1)
    own = scalar_of(found_ref, 2), scalar_of(found_ref, 3)
    other = scalar_of(swapped_ref, 0), scalar_of(swapped_ref, 1)
    above, further = choose(first, got, other), choose(first, other, got)
    return choose(odd, further, own), above, choose(odd, own, further)


def keep_scalars(out_ref, values):
    for index, value in enumerate(values):
        row = jnp.full((1, out_ref.shape[1]), value, jnp.int32)
        out_ref[index : index + 1] = row.astype(jnp.float32)


def scalar_of(ref, index):
    return jnp.max(ref[index : index + 1]).astype(jnp.int32)


def within(place, strip, height):
    return jnp.clip(place[0] - strip * height, 0, height - 1), place[1]


def roll_into(out_ref, value, row, col, tall_ref):
    frame = value.shape[0]
    half = frame // 2
    turned = pltpu.roll(value, col, 1)
    for index in range(frame // LANES):
        at = slice(index * LANES, (index + 1) * LANES)
        tall_ref[index, :half] = turned[half:, at]
        tall_ref[index, half:] = turned[:, at]
        out_ref[:, at] = tall_ref[index, pl.ds(half - row, frame), :]


def reorder_kernel(own_ref, received_ref, swapped_ref, factor_ref, rows_ref):
    frame = own_ref.shape[1]
    odd = lax.axis_index("tile") % 2 == 1
    moved = jnp.where(lax.axis_index("mode") == 0, received_ref[0], swapped_ref[0])
    value = jnp.where(odd, moved, own_ref[0])
    source = lax.broadcasted_iota(jnp.int32, (frame, frame), 0)
    target = lax.broadcasted_iota(jnp.int32, (frame, frame), 1)
    half = frame // 2
    order = jnp.where(target < half, 2 * target, 2 * target - frame + 1)
    pick = jnp.where(source == order, 1.0, 0.0).astype(jnp.bfloat16)
    high = value.astype(jnp.bfloat16)
    rest = value - high.astype(jnp.float32)
    middle = rest.astype(jnp.bfloat16)
    low = (rest - middle.astype(jnp.float32)).astype(jnp.bfloat16)
    columns = jnp.dot(high, pick, preferred_element_type=jnp.float32)
    columns = columns + jnp.dot(middle, pick, preferred_element_type=jnp.float32)
    columns = columns + jnp.dot(low, pick, preferred_element_type=jnp.float32)
    for index in range(frame // LANES):
        at = slice(index * LANES, (index + 1) * LANES)
        rows_ref[index] = columns[:, at]
        factor_ref[:half, at] = rows_ref[index, pl.ds(0, half, stride=2), :]
        factor_ref[half:, at] = rows_ref[index, pl.ds(1, half, stride=2), :]


def probe_parts(own_probe_ref, other_probe_ref):
    modes = own_probe_ref.shape[0]
    return [ref.at[mode, part] for ref in (own_probe_ref, other_probe_ref) for mode in range(modes) for part in range(2)]


def fill_kernel(own_probe_ref, other_probe_ref, gradient_ref, total_ref, zero_ref, sems):
    zero_ref[...] = jnp.zeros_like(zero_ref)
    step = zero_ref.shape[0]
    copies = []
    for part in range(2):
        for at in range(0, gradient_ref.shape[1], step):
            copies += fetch([(zero_ref, gradient_ref.at[part, at : at + step])], sems, len(copies))
    total = jnp.zeros(total_ref.shape, jnp.float32)
    for source in probe_parts(own_probe_ref, other_probe_ref):
        total = total + source[...] * source[...]
    total_ref[...] = total
    for copy in copies:
        copy.wait()


def prepare_kernel(
    found_ref, swapped_ref, object_ref, own_probe_ref, other_probe_ref, total_ref,
    probe_ref, window_ref, light_ref, place_ref, tall_ref,
):
    sources = probe_parts(own_probe_ref, other_probe_ref)
    height = object_ref.shape[1]
    tile = lax.axis_index("tile")
    odd = tile % 2
    main, _, _ = slots(found_ref, swapped_ref)
    row, col = within(main, tile - 2 * odd, height)
    shift = col % LANES
    for index, source in enumerate(sources):
        roll_into(probe_ref.at[index // 2, index % 2], source[...], row, shift, tall_ref.at[index])
    roll_into(light_ref, total_ref[...], row, shift, tall_ref.at[len(sources)])
    low, high = strip_window(object_ref, col)
    window_ref[:, :, :LANES] = low
    window_ref[:, :, LANES:] = high
    live = jnp.where(odd == 1, (tile >= 2).astype(jnp.int32), 1)
    keep_scalars(place_ref, (jnp.where(odd == 1, 0, row), jnp.where(odd == 1, row, height), live))


def right(value, high, low):
    first, second = split(value)
    return jnp.dot(
        jnp.concatenate([first, second, first], axis=1),
        jnp.concatenate([high, high, low], axis=0),
        preferred_element_type=jnp.float32,
    )


def left(high, low, value):
    first, second = split(value)
    return jnp.dot(
        jnp.concatenate([high, high, low], axis=1),
        jnp.concatenate([first, second, first], axis=0),
        preferred_element_type=jnp.float32,
    )


def transform_rows(probe_ref, start, window_ref, matrix_ref, out_ref):
    modes = probe_ref.shape[0]
    height, frame = window_ref.shape[1:]
    half = frame // 2
    sums, differences = [], []
    for mode in range(modes):
        probe_re = probe_ref[mode, 0, pl.ds(start, height), :]
        probe_im = probe_ref[mode, 1, pl.ds(start, height), :]
        wave_re = probe_re * window_ref[0] - probe_im * window_ref[1]
        wave_im = probe_re * window_ref[1] + probe_im * window_ref[0]
        for pieces, sign in ((sums, 1.0), (differences, -1.0)):
            pieces.append(
                jnp.concatenate(
                    [wave_re[:, :half] + sign * wave_re[:, half:], wave_im[:, :half] + sign * wave_im[:, half:]],
                    axis=1,
                )
            )
    even = right(jnp.concatenate(sums, axis=0), matrix_ref[0], matrix_ref[1])
    odd = right(jnp.concatenate(differences, axis=0), matrix_ref[4], matrix_ref[5])
    for mode in range(modes):
        at = slice(mode * height, (mode + 1) * height)
        out_ref[mode, 0] = jnp.concatenate([even[at, :half], odd[at, :half]], axis=1)
        out_ref[mode, 1] = jnp.concatenate([even[at, half:], odd[at, half:]], axis=1)


def strip_kernel(own_ref, received_ref, probe_ref, matrix_ref, own_out_ref, out_ref):
    height = received_ref.shape[1]
    start = pl.multiple_of((1 - lax.axis_index("mode")) * height, height)
    transform_rows(probe_ref, 0, own_ref, matrix_ref, own_out_ref)
    transform_rows(probe_ref, start, received_ref, matrix_ref, out_ref)


def wave_kernel(
    place_ref, window_ref, received_ref, swapped_ref, own_ref, first_ref, probe_ref, amplitude_ref, light_ref,
    matrix_ref, send_ref, keep_ref, patch_ref, far_ref, second_ref,
):
    modes, _, frame, _ = probe_ref.shape
    height = window_ref.shape[1]
    half = frame // 2
    core = lax.axis_index("mode")
    low, high = place_ref[0:1, :1].astype(jnp.int32), place_ref[1:2, :1].astype(jnp.int32)
    transform_rows(probe_ref, pl.multiple_of(core * height, height), swapped_ref, matrix_ref, second_ref)
    level = lax.broadcasted_iota(jnp.int32, (height, frame), 0)

    def assemble(own, got, given):
        nearer = jnp.where(core == 0, got, given)
        farther = jnp.where(core == 0, given, got)
        return jnp.where((level >= low) & (level < high), own, farther), nearer

    for part in range(2):
        top, bottom = assemble(window_ref[part], received_ref[part], swapped_ref[part])
        patch_ref[part, :height] = top
        patch_ref[part, height:] = bottom
    intensity = jnp.zeros((frame, frame), jnp.float32)
    for mode in range(modes):
        top_re, bottom_re = assemble(own_ref[mode, 0], first_ref[mode, 0], second_ref[mode, 0])
        top_im, bottom_im = assemble(own_ref[mode, 1], first_ref[mode, 1], second_ref[mode, 1])
        added = jnp.concatenate([top_re + bottom_re, top_im + bottom_im], axis=0)
        taken = jnp.concatenate([top_re - bottom_re, top_im - bottom_im], axis=0)
        even = left(matrix_ref[2], matrix_ref[3], added)
        odd = left(matrix_ref[6], matrix_ref[7], taken)
        far_ref[mode, 0] = even
        far_ref[mode, 1] = odd
        squares = jnp.concatenate(
            [even[:half] * even[:half] + even[half:] * even[half:], odd[:half] * odd[:half] + odd[half:] * odd[half:]],
            axis=0,
        )
        intensity = intensity + squares
    factor = amplitude_ref[...] * lax.rsqrt(jnp.maximum(intensity, FLOOR))
    grad_re = jnp.zeros((frame, frame), jnp.float32)
    grad_im = jnp.zeros((frame, frame), jnp.float32)
    even_factor = jnp.concatenate([factor[:half], factor[:half]], axis=0)
    odd_factor = jnp.concatenate([factor[half:], factor[half:]], axis=0)
    evens, odds = [], []
    for mode in range(modes):
        even = left(matrix_ref[0], matrix_ref[1], far_ref[mode, 0] * even_factor)
        odd = left(matrix_ref[4], matrix_ref[5], far_ref[mode, 1] * odd_factor)
        top, bottom = even + odd, even - odd
        mid_re = jnp.concatenate([top[:half], bottom[:half]], axis=0)
        mid_im = jnp.concatenate([top[half:], bottom[half:]], axis=0)
        evens.append(jnp.concatenate([mid_re[:, :half], mid_im[:, :half]], axis=1))
        odds.append(jnp.concatenate([mid_re[:, half:], mid_im[:, half:]], axis=1))
    even = right(jnp.concatenate(evens, axis=0), matrix_ref[2], matrix_ref[3])
    odd = right(jnp.concatenate(odds, axis=0), matrix_ref[6], matrix_ref[7])
    fores, afts = even + odd, even - odd
    for mode in range(modes):
        fore = fores[mode * frame : (mode + 1) * frame]
        aft = afts[mode * frame : (mode + 1) * frame]
        back_re = jnp.concatenate([fore[:, :half], aft[:, :half]], axis=1)
        back_im = jnp.concatenate([fore[:, half:], aft[:, half:]], axis=1)
        probe_re, probe_im = probe_ref[mode, 0], probe_ref[mode, 1]
        grad_re = grad_re + (probe_re * back_re + probe_im * back_im)
        grad_im = grad_im + (probe_re * back_im - probe_im * back_re)
    live = place_ref[2:3, :1]
    grad_re = (grad_re - light_ref[...] * patch_ref[0]) * live
    grad_im = (grad_im - light_ref[...] * patch_ref[1]) * live
    send_ref[:height] = jnp.where(core == 0, grad_re[height:], grad_re[:height])
    send_ref[height : 2 * height] = jnp.where(core == 0, grad_im[height:], grad_im[:height])
    keep_ref[0] = grad_re[:height]
    keep_ref[1] = grad_im[:height]


def covers(col, block, low, high, lane):
    start, shift = col // LANES, col % LANES
    distance = block - start
    value = jnp.where(distance == 1, high, low)
    first = jnp.where(distance == 0, shift, jnp.where(distance == 1, 0, LANES))
    last = jnp.where(distance == 2, shift, 0)
    keep = (lane >= first) | (lane < last)
    return jnp.where(keep, value, 0.0)


def base_kernel(
    place_ref, found_ref, swapped_ref, object_ref, keep_ref, light_ref, plain_ref,
    old_gradient_ref,
    updated_ref, gradient_ref, total_ref, weight_ref, first_ref, second_ref, others_ref, new_ref, tall_ref, turned_ref, sems, fills,
):
    del old_gradient_ref
    height, breadth = object_ref.shape[1:]
    tile = lax.axis_index("tile")
    core = lax.axis_index("mode")
    fill = pltpu.make_async_copy(object_ref, updated_ref, fills.at[0])
    fill.start()
    total_ref[...] = jnp.zeros_like(total_ref)
    weight_ref[...] = jnp.zeros_like(weight_ref)
    odd = tile % 2
    (_, col), above, third = slots(found_ref, swapped_ref)
    live = place_ref[2:3, :1]
    start, stop = place_ref[0:1, :1].astype(jnp.int32), place_ref[1:2, :1].astype(jnp.int32)
    lane = lax.broadcasted_iota(jnp.int32, (height, LANES), 1)
    level = lax.broadcasted_iota(jnp.int32, (height, LANES), 0)
    kept = (level >= start) & (level < stop)
    for slot in range(3):
        block = jnp.minimum(col // LANES + slot, breadth // LANES - 1)
        at = pl.ds(pl.multiple_of(block * LANES, LANES), LANES)
        light = covers(col, block, light_ref[:height, :LANES], light_ref[:height, LANES:], lane)
        weight = jnp.where(kept, light * live, 0.0)
        weight_ref[:, at] = weight
        scale = 1.0 / (weight + ALPHA)
        for part in range(2):
            change = covers(col, block, keep_ref[part, :, :LANES], keep_ref[part, :, LANES:], lane)
            change = jnp.where(kept, change, 0.0)
            total_ref[part, :, at] = change
            new_ref[slot, part] = object_ref[part, :, at] + change * scale
    places = []
    for place, strip, far in ((above, tile - 1, False), (third, tile - 2 + 2 * odd, True)):
        row, start = within(place, strip, height)
        index = int(far)
        roll_into(turned_ref.at[index], plain_ref[...], row, start % LANES, tall_ref.at[index])
        turned = turned_ref[index]
        begin = jnp.where(odd == 1, row, 0) if far else 0
        end = jnp.where(odd == 1, height, row) if far else height
        slot = strip
        there = ((slot >= 0) & (slot < lax.axis_size("tile") - 1)).astype(jnp.float32)
        places.append((start, begin, end, (turned[:height] if far else turned[height:]) * there))
    chosen = []
    for slot, out_ref in ((0, first_ref), (1, second_ref)):
        direct = core == slot
        near, far = places
        out_ref[...] = jnp.where(direct, near[3], far[3])
        chosen += [jnp.where(direct, near[index], far[index]) for index in range(3)]
    keep_scalars(others_ref, chosen)
    fill.wait()
    copies = []
    for slot in range(3):
        block = jnp.minimum(col // LANES + slot, breadth // LANES - 1)
        at = pl.ds(pl.multiple_of(block * LANES, LANES), LANES)
        copies.append(write(slot, col, block, at, total_ref.at[:, :, at], new_ref, gradient_ref, updated_ref, sems))
    finish(copies)


def write(slot, col, block, at, source, new_ref, gradient_ref, updated_ref, sems):
    fresh = col // LANES + slot == block
    one = pltpu.make_async_copy(source, gradient_ref.at[:, :, at], sems.at[2 * slot])
    two = pltpu.make_async_copy(new_ref.at[slot], updated_ref.at[:, :, at], sems.at[2 * slot + 1])

    @pl.when(fresh)
    def _():
        one.start()
        two.start()

    return fresh, one, two


def finish(copies):
    for fresh, one, two in copies:

        @pl.when(fresh)
        def _(one=one, two=two):
            one.wait()
            two.wait()


def add_windows(windows, main, object_ref, total_ref, weight_ref, updated_ref, gradient_ref, new_ref, sum_ref, sems):
    height, breadth = object_ref.shape[1:]
    lane = lax.broadcasted_iota(jnp.int32, (height, LANES), 1)
    level = lax.broadcasted_iota(jnp.int32, (height, LANES), 0)
    col = windows[main][0]
    copies = []
    for slot in range(3):
        block = jnp.minimum(col // LANES + slot, breadth // LANES - 1)
        at = pl.ds(pl.multiple_of(block * LANES, LANES), LANES)
        weight = weight_ref[:, at]
        sums = [total_ref[0, :, at], total_ref[1, :, at]]
        for start, begin, end, light_ref, change_ref in windows:
            inside = (level >= begin) & (level < end)
            light = covers(start, block, light_ref[:, :LANES], light_ref[:, LANES:], lane)
            weight = weight + jnp.where(inside, light, 0.0)
            for part in range(2):
                rows = slice(part * height, (part + 1) * height)
                change = covers(start, block, change_ref[rows, :LANES], change_ref[rows, LANES:], lane)
                sums[part] = sums[part] + jnp.where(inside, change, 0.0)
        scale = 1.0 / (weight + ALPHA)
        for part in range(2):
            sum_ref[slot, part] = sums[part]
            new_ref[slot, part] = object_ref[part, :, at] + sums[part] * scale
        copies.append(write(slot, col, block, at, sum_ref.at[slot], new_ref, gradient_ref, updated_ref, sems))
    finish(copies)


def first_kernel(
    others_ref, object_ref, total_ref, weight_ref, first_ref, received_ref, old_updated_ref, old_gradient_ref,
    updated_ref, gradient_ref, new_ref, sum_ref, sems,
):
    del old_updated_ref, old_gradient_ref
    windows = [(*(scalar_of(others_ref, index) for index in range(3)), first_ref, received_ref)]
    add_windows(windows, 0, object_ref, total_ref, weight_ref, updated_ref, gradient_ref, new_ref, sum_ref, sems)


def second_kernel(
    others_ref, object_ref, total_ref, weight_ref, first_ref, second_ref, received_ref, swapped_ref,
    old_updated_ref, old_gradient_ref, updated_ref, gradient_ref, new_ref, sum_ref, sems,
):
    del old_updated_ref, old_gradient_ref
    windows = [
        (*(scalar_of(others_ref, index) for index in range(3)), first_ref, received_ref),
        (*(scalar_of(others_ref, index) for index in range(3, 6)), second_ref, swapped_ref),
    ]
    add_windows(windows, 1, object_ref, total_ref, weight_ref, updated_ref, gradient_ref, new_ref, sum_ref, sems)


def call(kernel, out_shape, in_specs, out_specs, scratch=(), mebibytes=16, aliases=None):
    return pl.pallas_call(
        kernel,
        out_shape=out_shape,
        in_specs=in_specs,
        out_specs=out_specs,
        scratch_shapes=list(scratch),
        input_output_aliases=aliases or {},
        compiler_params=pltpu.CompilerParams(vmem_limit_bytes=mebibytes << 20),
        cost_estimate=pl.CostEstimate(flops=5000000, bytes_accessed=5000000, transcendentals=0),
    )


def space(where):
    return pl.BlockSpec(memory_space=where)


def shape(*dims, dtype=jnp.float32):
    return jax.ShapeDtypeStruct(dims, dtype)


def solution(mesh):
    tiles, cores = mesh.shape["tile"], mesh.shape["mode"]
    up = [(2 * t, 2 * (t + 1)) for t in range(tiles - 1)] + [(2 * t + 1, 2 * (t + 2) + 1) for t in range(tiles - 2)]
    gather = [(2 * t, 2 * (t ^ 1)) for t in range(tiles)]
    gather += [(2 * t + 1, 2 * (t - 2) + 1) for t in range(2, tiles, 2)]
    gather += [(2 * t + 1, 2 * (t + 2) + 1) for t in range(1, tiles - 2, 2)]
    spread = [(target, source) for source, target in gather]
    onward = [(2 * t, 2 * (t + 2)) for t in range(1, tiles - 2, 2)]
    swap = [(2 * t + core, 2 * t + 1 - core) for t in range(tiles) for core in range(2)]
    assert cores == 2 and tiles % 2 == 0

    def move(value, pairs):
        return lax.ppermute(value, AXES, pairs)

    def step(object_tiles, probe_modes, amplitudes, scan_offsets, slot_scan, slot_count):
        height, breadth = object_tiles.shape[1:]
        modes, _, frame, _ = probe_modes.shape
        assert slot_scan.shape[0] == 1 and frame == 2 * height and height == LANES
        table = scan_offsets.T
        matrix = jnp.asarray(matrices(frame))
        received_scan = move(slot_scan, up)
        staged = move(object_tiles, swap)
        table = move(table, swap)
        other_probe = move(probe_modes, swap)
        received_amplitude = move(amplitudes, onward)
        window, found = call(
            select_kernel,
            (shape(2, height, frame), shape(8, LANES)),
            [space(SMEM)] * 2 + [space(VMEM)] * 2,
            [space(VMEM)] * 2,
        )(slot_scan, received_scan, table, staged)
        received = move(window, gather)
        swapped_found = move(found, swap)
        swapped_amplitude = move(received_amplitude, swap)
        strip = shape(2 * modes, 2, height, frame)
        whole = shape(2, height, breadth)
        gradient, plain = call(
            fill_kernel,
            (whole, shape(frame, frame)),
            [space(VMEM)] * 2,
            [space(pl.ANY), space(VMEM)],
            [pltpu.VMEM((height // 8, breadth), jnp.float32), pltpu.SemaphoreType.DMA((16,))],
        )(probe_modes, other_probe)
        probe, own_window, light, place = call(
            prepare_kernel,
            (
                shape(2 * modes, 2, frame, frame),
                shape(2, height, frame),
                shape(frame, frame),
                shape(8, LANES),
            ),
            [space(VMEM)] * 6,
            [space(VMEM)] * 4,
            [pltpu.VMEM((4 * modes + 1, frame // LANES, frame + height, LANES), jnp.float32)],
        )(found, swapped_found, staged, probe_modes, other_probe, plain)
        swapped = move(received, swap)
        amplitude = call(
            reorder_kernel,
            shape(frame, frame),
            [space(VMEM)] * 3,
            space(VMEM),
            [pltpu.VMEM((frame // LANES, frame, LANES), jnp.float32)],
        )(amplitudes, received_amplitude, swapped_amplitude)
        own_strip, first_strip = call(strip_kernel, (strip, strip), [space(VMEM)] * 4, [space(VMEM)] * 2)(
            own_window, received, probe, matrix
        )
        send, keep = call(
            wave_kernel,
            (shape(2 * height, frame), shape(2, height, frame)),
            [space(VMEM)] * 10,
            [space(VMEM)] * 2,
            [
                pltpu.VMEM((2, frame, frame), jnp.float32),
                pltpu.VMEM((2 * modes, 2, frame, frame), jnp.float32),
                pltpu.VMEM((2 * modes, 2, height, frame), jnp.float32),
            ],
            mebibytes=24,
        )(place, own_window, received, swapped, own_strip, first_strip, probe, amplitude, light, matrix)
        received_change = move(send, spread)
        blocks = pltpu.VMEM((3, 2, height, LANES), jnp.float32)
        semaphores = pltpu.SemaphoreType.DMA((6,))
        updated, gradient, total, weight, first, second, others = call(
            base_kernel,
            (
                whole,
                whole,
                whole,
                shape(height, breadth),
                shape(height, frame),
                shape(height, frame),
                shape(8, LANES),
            ),
            [space(VMEM)] * 7 + [space(pl.ANY)],
            [space(pl.ANY)] * 2 + [space(VMEM)] * 5,
            [
                blocks,
                pltpu.VMEM((2, frame // LANES, frame + height, LANES), jnp.float32),
                pltpu.VMEM((2, frame, frame), jnp.float32),
                semaphores,
                pltpu.SemaphoreType.DMA((1,)),
            ],
            aliases={7: 1},
        )(place, found, swapped_found, staged, keep, light, plain, gradient)
        swapped_change = move(received_change, swap)
        updated, gradient = call(
            first_kernel,
            (whole, whole),
            [space(VMEM)] * 6 + [space(pl.ANY)] * 2,
            [space(pl.ANY)] * 2,
            [blocks, blocks, semaphores],
            aliases={6: 0, 7: 1},
        )(others, staged, total, weight, first, received_change, updated, gradient)
        return call(
            second_kernel,
            (whole, whole),
            [space(VMEM)] * 8 + [space(pl.ANY)] * 2,
            [space(pl.ANY)] * 2,
            [blocks, blocks, semaphores],
            aliases={8: 0, 9: 1},
        )(others, staged, total, weight, first, second, received_change, swapped_change, updated, gradient)

    return jax.shard_map(
        step,
        mesh=mesh,
        in_specs=(
            P(None, "tile", None),
            P("mode", None, None, None),
            P("tile", None, None),
            P(),
            P("tile"),
            P("tile"),
        ),
        out_specs=(P(None, "tile", None), P(None, "tile", None)),
        check_vma=False,
    )
```
